32 devices in a mesh: grp: 2 (over x), gx: 8 (over z, y), gy: 2 (over core).
Axes of the slice: x: 2, y: 2, z: 4, core: 2. Of those that a mesh axis runs over, the one named last changes fastest.
Arguments:
- spectrum: float32 [16, 96, 1152], P('gx', 'gy', 'grp'), may hold values from 0 to 2
- wet_mask: int32 [16, 96], P('gx', 'gy'), may hold values 0 or 1
- ocean_source: int32 [16, 96], P('gx', 'gy'), may hold values from 0 to 95
- ocean_u: float32 [16, 96, 40], P('gx', 'gy', 'grp'), may hold values from -2 to 2
- ocean_v: float32 [16, 96, 40], P('gx', 'gy', 'grp'), may hold values from -2 to 2
- current_weights: float32 [40, 32], replicated, may hold values from 0.005 to 0.04
- drift_weights: float32 [40, 32], replicated, may hold values from 0.005 to 0.05
- inter_left: bfloat16 [1152, 512], P('grp'), may hold values from -0.25 to 0.25
- inter_right: bfloat16 [1152, 512], P('grp'), may hold values from -0.25 to 0.25
- inter_out: bfloat16 [512, 1152], P(None, 'grp'), may hold values from -0.25 to 0.25
- mixing: float32 [40, 40], P(None, 'grp'), may hold values from -0.47434166 to 0.47434166
Outputs:
- spectrum_out: float32 [16, 96, 1152], P('gx', 'gy', 'grp')
- ocean_u_out: float32 [16, 96, 40], P('gx', 'gy', 'grp')
- ocean_v_out: float32 [16, 96, 40], P('gx', 'gy', 'grp')
- drift_u: float32 [16, 96, 40], P('gx', 'gy', 'grp')
- drift_v: float32 [16, 96, 40], P('gx', 'gy', 'grp')
The draws below stay inside these ranges and needn't reach their ends.
Inputs may be any that keep to these rules, and one draw needn't show every extreme that they name: `wet_mask`: 1 marks a sea column, 0 a land column. `ocean_source`: each entry numbers a column of the same tile of 2 x 48 columns as (x mod 2) * 48 + (y mod 48).
All inputs are finite; a program needn't handle non-finite values. No bound on the sum of `wet_mask` on one device may be relied on, other than what follows from the above.
Results may differ from the reference program's by a relative error of at most 0.00077.
Values sent between devices are 32-bit elements; how exact they have to be, the bound alone decides.
A program may use at most 64 MiB of HBM per device.

```python
import math
import jax
import jax.numpy as jnp
from jax import lax

NF = 32
ND = 36
NLEV = 40
RANK = 512
WAVE_SECTIONS = 3
OCEAN_SECTIONS = 2
CX = 2
CY = 48
NX = 16
NY = 96
NBIN = 1152
NFL = 16


def touch_ends(result, stream_key, smallest, high):
    index_at = [jax.random.randint(jax.random.fold_in(stream_key, axis), (), 0, length) for axis, length in enumerate(result.shape)]
    main_axis = result.shape.index(max(result.shape))
    beside = index_at[:main_axis] + [(index_at[main_axis] + 1) % result.shape[main_axis]] + index_at[main_axis + 1:]
    return result.at[tuple(index_at)].set(smallest).at[tuple(beside)].set(high)


def block_scale(own_key, shape, pieces, low, largest):
    level, own = 1.0, jax.random.fold_in(own_key, 6)
    for dim, shards_of in pieces:
        steps = jnp.exp(jax.random.uniform(jax.random.fold_in(own, dim), (shards_of,), jnp.float32, low / len(pieces), largest / len(pieces)))
        level = level * jnp.repeat(steps, shape[dim] // shards_of).reshape([-1 if axis == dim else 1 for axis in range(len(shape))])
    return level


def noise(own_key, dims, spread, most, pieces=(), dtype=jnp.bfloat16):
    gain = block_scale(own_key, dims, pieces, -0.22, 0.18) if pieces else 1.0
    array = jax.random.normal(own_key, dims, jnp.float32) * spread * gain
    return jnp.minimum(jnp.maximum(array, -most), most).astype(dtype)


def setup_inputs(seed: int = 0) -> dict:
    splits = jax.random.split(jax.random.key(seed), 12)
    return {
        "spectrum": jnp.clip(2.0 * jax.random.uniform(splits[0], (NX, NY, NBIN), jnp.float32) ** block_scale(splits[0], (NX, NY, NBIN), ((0, 8), (1, 2), (2, 2)), -0.2, 0.2), 0.0, 2.0),
        "wet_mask": touch_ends((jax.random.randint(splits[1], (NX, NY), 0, 5) < 4).astype(jnp.int32), jax.random.fold_in(splits[1], 1), 0, 1),
        "ocean_source": touch_ends(jax.random.randint(splits[2], (NX, NY), 0, CX * CY), jax.random.fold_in(splits[2], 1), 0, (CX * CY) - 1).astype(jnp.int32),
        "ocean_u": noise(splits[3], (NX, NY, NLEV), 0.5, 2.0, ((0, 8), (1, 2), (2, 2)), jnp.float32),
        "ocean_v": noise(splits[4], (NX, NY, NLEV), 0.5, 2.0, ((0, 8), (1, 2), (2, 2)), jnp.float32),
        "current_weights": jnp.clip(jnp.exp(jax.random.uniform(splits[5], (NLEV, NF), jnp.float32, math.log(0.005), math.log(0.04))), 0.005, 0.04),
        "drift_weights": jnp.clip(jnp.exp(jax.random.uniform(splits[6], (NLEV, NF), jnp.float32, math.log(0.005), math.log(0.05))), 0.005, 0.05),
        "inter_left": noise(splits[7], (NBIN, RANK), (NBIN // 2) ** -0.5, 0.25, ((0, 2),)),
        "inter_right": noise(splits[8], (NBIN, RANK), (NBIN // 2) ** -0.5, 0.25, ((0, 2),)),
        "inter_out": noise(splits[9], (RANK, NBIN), RANK ** -0.5, 0.25, ((1, 2),)),
        "mixing": noise(splits[10], (NLEV, NLEV), (0.5 / NLEV ** 0.5), 0.47434166, ((1, 2),), jnp.float32),
    }


highest = lax.Precision.HIGHEST
inter_step = 0.1
ocean_step = 0.4
coriolis = 0.5
viscosity = 0.1


def bin_tables(band_index, bin_count):
    position = jnp.arange(bin_count)
    direction = (position // NFL).astype(jnp.float32)
    frequency = (band_index * NFL + position % NFL).astype(jnp.float32)
    angle_value = 2.0 * jnp.pi * direction / ND
    group_speed = 0.2 + 0.4 * (NF - 1 - frequency) / (NF - 1)
    turning = 0.5 * (frequency + 1.0) / NF
    return jnp.cos(angle_value), jnp.sin(angle_value), group_speed, turning


def beam_sweep(padded, velocity, which_axis):
    extent = velocity.shape[which_axis]

    def take_part(offset):
        return lax.slice_in_dim(padded, offset, offset + extent, axis=which_axis)

    centre = take_part(2)
    upwind_one = jnp.where(velocity >= 0.0, take_part(1), take_part(3))
    beyond = jnp.where(velocity >= 0.0, take_part(0), take_part(4))
    magnitude = jnp.abs(velocity)
    return centre - 0.5 * magnitude * (3.0 * centre - 4.0 * upwind_one + beyond) + 0.5 * magnitude * magnitude * (centre - 2.0 * upwind_one + beyond)


def wave_section(spectrum_now, speed_x, speed_y, turn_rate, left_band, right_band, out_band, wet_factor):
    padded = jnp.pad(spectrum_now, ((2, 2), (0, 0), (0, 0)))
    shifted = beam_sweep(padded, speed_x, 0)
    padded = jnp.pad(shifted, ((0, 0), (2, 2), (0, 0)))
    shifted = beam_sweep(padded, speed_y, 1)
    behind = jnp.roll(shifted, NFL, axis=2)
    ahead_dir = jnp.roll(shifted, -NFL, axis=2)
    upwind = jnp.where(turn_rate >= 0.0, behind, ahead_dir)
    turned = shifted - jnp.abs(turn_rate) * (shifted - upwind)
    flat_bins = spectrum_now.reshape(-1, spectrum_now.shape[2]).astype(jnp.bfloat16)
    product = jnp.dot(flat_bins, left_band, preferred_element_type=jnp.float32) * jnp.dot(flat_bins, right_band, preferred_element_type=jnp.float32)
    source = inter_step * jnp.dot(product.astype(jnp.bfloat16), out_band, preferred_element_type=jnp.float32)
    return wet_factor * (turned + source.reshape(spectrum_now.shape))


def laplace(values):
    padded = jnp.pad(values, ((1, 1), (1, 1), (0, 0)))
    return padded[2:, 1:-1] + padded[:-2, 1:-1] + padded[1:-1, 2:] + padded[1:-1, :-2] - 4.0 * values


def reference(spectrum, wet_mask, ocean_source, ocean_u, ocean_v, current_weights, drift_weights, inter_left, inter_right, inter_out, mixing):
    wet_factor = wet_mask.astype(jnp.float32)[:, :, None]
    columns_x = jnp.arange(NX)[:, None]
    columns_y = jnp.arange(NY)[None, :]
    source_x = (columns_x // CX) * CX + ocean_source // CY
    source_y = (columns_y // CY) * CY + ocean_source % CY
    source_u = ocean_u[source_x, source_y]
    source_v = ocean_v[source_x, source_y]
    bin_count = NBIN // 2
    kept_bands = []
    drift_x = jnp.zeros((NX, NY, NLEV), jnp.float32)
    drift_y = jnp.zeros((NX, NY, NLEV), jnp.float32)
    for band_index in range(2):
        cosine, sine_value, group_speed, turning = bin_tables(band_index, bin_count)
        weights_band = current_weights[:, band_index * NFL:(band_index + 1) * NFL]
        flow_x = jnp.tile(jnp.einsum("abk,kf->abf", source_u, weights_band, precision=highest), (1, 1, ND))
        flow_y = jnp.tile(jnp.einsum("abk,kf->abf", source_v, weights_band, precision=highest), (1, 1, ND))
        speed_x = group_speed * cosine + flow_x
        speed_y = group_speed * sine_value + flow_y
        turn_rate = turning * (sine_value * flow_x - cosine * flow_y)
        lower = band_index * bin_count
        upper = lower + bin_count
        spectrum_now = wet_factor * spectrum[:, :, lower:upper]
        for repeat in range(WAVE_SECTIONS):
            spectrum_now = wave_section(spectrum_now, speed_x, speed_y, turn_rate, inter_left[lower:upper], inter_right[lower:upper], inter_out[:, lower:upper], wet_factor)
        kept_bands.append(spectrum_now)
        profile = jnp.tile(drift_weights[:, band_index * NFL:(band_index + 1) * NFL], (1, ND))
        drift_x = drift_x + jnp.einsum("abn,kn->abk", spectrum_now, profile * cosine, precision=highest)
        drift_y = drift_y + jnp.einsum("abn,kn->abk", spectrum_now, profile * sine_value, precision=highest)
    spectrum_out = jnp.concatenate(kept_bands, axis=2)
    velocity_u = ocean_u
    velocity_v = ocean_v
    for repeat in range(OCEAN_SECTIONS):
        first_u = velocity_u + ocean_step * (coriolis * (velocity_v + drift_y) + viscosity * laplace(velocity_u))
        first_v = velocity_v + ocean_step * (-coriolis * (velocity_u + drift_x) + viscosity * laplace(velocity_v))
        velocity_u = wet_factor * (first_u + jnp.einsum("abk,kl->abl", first_u, mixing, precision=highest))
        velocity_v = wet_factor * (first_v + jnp.einsum("abk,kl->abl", first_v, mixing, precision=highest))
    return spectrum_out, velocity_u, velocity_v, drift_x, drift_y
```

```python
import functools

import jax
import jax.numpy as jnp
import numpy as np
from jax import lax
from jax.experimental import pallas as pl
from jax.experimental.pallas import tpu as pltpu
from jax.sharding import PartitionSpec as P

NF = 32
ND = 36
NLEV = 40
WAVE_SECTIONS = 3
NFL = 16
LANES = 128
MESH = pl.DeviceIdType.MESH

highest = lax.Precision.HIGHEST
inter_step = 0.1
ocean_step = 0.4
coriolis = 0.5
viscosity = 0.1


def exact_dot(a, b):
    return jnp.dot(a, b, precision=highest, preferred_element_type=jnp.float32)


def dot_on(a, b, dim_a, dim_b, precision=highest):
    return lax.dot_general(
        a, b, (((dim_a,), (dim_b,)), ((), ())), precision=precision, preferred_element_type=jnp.float32
    )


def sweep(centre, back_one, back_two, next_one, next_two, velocity):
    up = velocity >= 0.0
    one = jnp.where(up, back_one, next_one)
    two = jnp.where(up, back_two, next_two)
    size = jnp.abs(velocity)
    half = 0.5 * size
    return centre - half * (3.0 * centre - 4.0 * one + two) + half * size * (centre - 2.0 * one + two)


def iota(shape, dim):
    return lax.broadcasted_iota(jnp.int32, shape, dim)


class Move:
    def __init__(self, src, dst, send, recv, device, sends, receives):
        self.copy = pltpu.make_async_remote_copy(
            src_ref=src, dst_ref=dst, send_sem=send, recv_sem=recv, device_id=device, device_id_type=MESH
        )
        self.sends, self.receives = sends, receives

    def when(self, cond, act):
        if cond is True:
            act()
        else:
            pl.when(cond)(act)

    def start(self):
        self.when(self.sends, self.copy.start)

    def wait_send(self):
        self.when(self.sends, self.copy.wait_send)

    def wait_recv(self):
        self.when(self.receives, self.copy.wait_recv)


def kernel(
    sizes,
    spectrum_hbm,
    wet_mask,
    ocean_source,
    ocean_u,
    ocean_v,
    angles,
    cw,
    dw,
    left_hbm,
    right_hbm,
    out_hbm,
    mixing,
    spec_out,
    u_out,
    v_out,
    du_out,
    dv_out,
    spectrum,
    left,
    right,
    out_map,
    load_sem,
    pack,
    currents,
    profile,
    masked,
    packs,
    own_flow,
    flow,
    flow_edge,
    flow_halo,
    field,
    edge,
    halo_x,
    halo_y,
    corner,
    halo_c,
    speed_x,
    speed_y,
    turn,
    speed_l,
    speed_r,
    wide,
    source,
    mix,
    ocean,
    ocean_next,
    row_halo,
    col_edge,
    col_halo,
    drift_q,
    drift_n,
    init_send,
    init_recv,
    wave_send,
    wave_recv,
    sea_send,
    sea_recv,
):
    nx, ny = sizes
    loads = [
        pltpu.make_async_copy(src, dst, load_sem.at[k])
        for k, (src, dst) in enumerate(
            ((spectrum_hbm, spectrum), (left_hbm, left), (right_hbm, right), (out_hbm, out_map))
        )
    ]
    for load in loads:
        load.start()
    tile_x, tile_y, bins = spectrum.shape
    half = tile_y // 2
    own = u_out.shape[0]
    rows = 2 * tile_x
    g, gx, gy = lax.axis_index("grp"), lax.axis_index("gx"), lax.axis_index("gy")
    z, y = gx // 2, gx % 2
    flip = (y + gy) % 2
    q = 2 * gy + flip
    late = gy % 2 == 1
    nz, nq = nx // 2, 2 * ny

    def at(dg=0, x=gx, c=gy):
        return {"grp": (g + dg) % 2, "gx": x, "gy": c}

    pair = 2 * z + 1 - y

    def q_at(dz, dq):
        qq = q + dq
        return at(0, 2 * (z + dz) + (qq + qq // 2) % 2, qq // 2)

    def inside(value, step, limit):
        return value + step >= 0 if step < 0 else value + step < limit

    def both(dz, dq):
        cond = inside(q, dq, nq)
        return cond if dz == 0 else cond & inside(z, dz, nz)

    friends = [(True, at(1)), (True, at(0, pair)), (True, at(1, pair))]
    friends += [(inside(z, d, nz), at(0, gx + 2 * d)) for d in (-1, 1)]
    friends += [(both(dz, dq), q_at(dz, dq)) for dq in (-1, 1) for dz in (-1, 0, 1)]
    friends += [(inside(gx, d, nx), at(0, gx + d)) for d in (-1, 1)]
    friends += [(inside(gy, d, ny), at(0, gx, gy + d)) for d in (-1, 1)]
    barrier = pltpu.get_barrier_semaphore()
    total = 0
    for cond, device in friends:

        def hello(device=device):
            pl.semaphore_signal(barrier, inc=1, device_id=device, device_id_type=MESH)

        if cond is True:
            hello()
            total = total + 1
        else:
            pl.when(cond)(hello)
            total = total + jnp.where(cond, 1, 0)

    columns = tile_x * tile_y

    def as_columns(table):
        ones = jnp.ones((1, LANES), jnp.float32)
        values = table[...].astype(jnp.float32)
        return jnp.concatenate([dot_on(values[r : r + 1], ones, 0, 0) for r in range(tile_x)], axis=0)

    place_i, place_j = iota((own, LANES), 0), iota((own, LANES), 1)
    place_u = jnp.where(place_j == place_i + own * g, 1.0, 0.0)
    place_v = jnp.where(place_j == place_i + own * g + NLEV, 1.0, 0.0)
    for r in range(tile_x):
        pack[r * tile_y : (r + 1) * tile_y] = dot_on(ocean_u[:, r, :], place_u, 0, 0) + dot_on(
            ocean_v[:, r, :], place_v, 0, 0
        )
    pack[columns:] = dot_on(mixing[...], place_u, 0, 0)
    wet_wide = as_columns(wet_mask)
    wet_n = wet_wide[:, 0:1]

    @pl.when(z == 0)
    def _():
        halo_x[:, 0] = jnp.zeros_like(halo_x[:, 0])

    @pl.when(z == nz - 1)
    def _():
        halo_x[:, 1] = jnp.zeros_like(halo_x[:, 1])

    for side, dq in ((0, -1), (1, 1)):

        @pl.when(jnp.logical_not(inside(q, dq, nq)))
        def _():
            halo_y[:, side] = jnp.zeros_like(halo_y[:, side])
            halo_c[:, side] = jnp.zeros_like(halo_c[:, side])
            flow_halo[side] = jnp.zeros_like(flow_halo[side])

        for slot, dz in ((0, -1), (1, 1)):

            @pl.when(inside(q, dq, nq) & jnp.logical_not(inside(z, dz, nz)))
            def _():
                halo_c[:, side, slot] = jnp.zeros_like(halo_c[:, side, slot])

    for side, d in ((0, -1), (1, 1)):

        @pl.when(jnp.logical_not(inside(gx, d, nx)))
        def _():
            row_halo[:, side] = jnp.zeros_like(row_halo[:, side])

        @pl.when(jnp.logical_not(inside(gy, d, ny)))
        def _():
            col_halo[:, side] = jnp.zeros_like(col_halo[:, side])

    loads[0].wait()
    masked[...] = (spectrum[...].reshape(columns, bins) * wet_n).reshape(tile_x, tile_y, bins)

    pl.semaphore_wait(barrier, total)

    to_grp = Move(pack, packs, init_send.at[0], init_recv.at[0], at(1), True, True)
    to_grp.start()
    away = pl.ds(pl.multiple_of(half * (1 - flip), 8), half)
    mine = pl.ds(pl.multiple_of(half * flip, 8), half)
    my_rows = pl.ds(tile_x * y, tile_x)
    to_pair = [
        Move(
            masked.at[row, away, :],
            field.at[tile_x * y + row],
            init_send.at[k],
            init_recv.at[k],
            at(0, pair),
            True,
            True,
        )
        for k, row in ((1, y), (9, 1 - y))
    ]
    for m in to_pair:
        m.start()
    field[my_rows] = masked[:, mine, :]

    def wave_moves(s):
        moves = []
        for near in (True, False):
            for side, dz in ((0, -1), (1, 1)):
                layer = 0 if near == (dz < 0) else 1
                moves.append(
                    Move(
                        field.at[layer if dz < 0 else rows - 2 + layer],
                        halo_x.at[s, 1 - side, layer],
                        wave_send.at[s, len(moves)],
                        wave_recv.at[s, len(moves)],
                        at(0, gx + 2 * dz),
                        inside(z, dz, nz),
                        inside(z, -dz, nz),
                    )
                )
        k = 4
        for side, dq in ((0, -1), (1, 1)):
            for dz in (-1, 0, 1):
                moves.append(
                    Move(
                        edge.at[s, side] if dz == 0 else corner.at[s, side, (1 + dz) // 2],
                        halo_y.at[s, 1 - side] if dz == 0 else halo_c.at[s, 1 - side, (1 - dz) // 2],
                        wave_send.at[s, k],
                        wave_recv.at[s, k],
                        q_at(dz, dq),
                        both(dz, dq),
                        both(-dz, -dq),
                    )
                )
                k += 1
        return moves

    first_moves = wave_moves(0)
    for k in (0, 2):
        pl.when(y == 0)(first_moves[k].start)
        pl.when(y == 1)(first_moves[k + 1].start)

    chosen_at = as_columns(ocean_source)[:, 0:1]
    chosen = jnp.where(iota((columns, columns), 1).astype(jnp.float32) == chosen_at, 1.0, 0.0)
    currents[...] = jnp.zeros_like(currents)
    currents[0:NF, 0:NLEV] = cw[...]
    currents[NF : 2 * NF] = pltpu.roll(currents[0:NF], NLEV, 1)
    to_grp.wait_recv()
    everything = pack[...] + packs[...]
    ocean[...] = everything[:columns].reshape(ocean.shape)
    mix[...] = jnp.zeros_like(mix)
    mix[0:NLEV] = everything[columns:]
    mix[NLEV : 2 * NLEV] = pltpu.roll(everything[columns:], NLEV, 1)
    felt = exact_dot(chosen, dot_on(everything[:columns], currents[...], 1, 1))
    felt = felt + jnp.where(iota((columns, LANES), 1) == 2 * NF, wet_n, 0.0)
    own_flow[...] = felt.reshape(own_flow.shape)
    flow_pair = Move(
        own_flow.at[:, away, :], flow.at[my_rows], init_send.at[2], init_recv.at[2], at(0, pair), True, True
    )
    flow_pair.start()
    flow[my_rows] = own_flow[:, mine, :]

    def sea_moves(k, array):
        moves = []
        for side, d in ((0, -1), (1, 1)):
            moves.append(
                Move(
                    array.at[0 if d < 0 else tile_x - 1],
                    row_halo.at[k, 1 - side],
                    sea_send.at[k, side],
                    sea_recv.at[k, side],
                    at(0, gx + d),
                    inside(gx, d, nx),
                    inside(gx, -d, nx),
                )
            )
            moves.append(
                Move(
                    col_edge.at[k, side],
                    col_halo.at[k, 1 - side],
                    sea_send.at[k, 2 + side],
                    sea_recv.at[k, 2 + side],
                    at(0, gx, gy + d),
                    inside(gy, d, ny),
                    inside(gy, -d, ny),
                )
            )
        return moves

    def set_col_edges(k, array):
        for side, column in ((0, 0), (1, tile_y - 1)):
            for r in range(tile_x):
                col_edge[k, side, r : r + 1, :] = array[r, column : column + 1, :]

    lane = iota((1, bins), 1)
    frequency = (g * NFL + (lane & (NFL - 1))).astype(jnp.float32)
    group_speed = 0.2 + 0.4 * (NF - 1 - frequency) / (NF - 1)
    turning = 0.5 * (frequency + 1.0) / NF
    cosine, sine = angles[0:1, :], angles[1:2, :]
    spread_i = iota((LANES, bins), 0)
    spread_f = g * NFL + (iota((LANES, bins), 1) & (NFL - 1))
    spread_x = jnp.where(spread_i == spread_f, 1.0, 0.0)
    spread_y = jnp.where(spread_i == spread_f + NF, 1.0, 0.0)

    def set_edges(s):
        for side, first in ((0, 0), (1, half - 2)):
            for r in range(rows):
                pair_of = field[r, first : first + 2, :]
                edge[s, side, 2 * r : 2 * r + 2, :] = pair_of
                corner[s, side, r // 2, 2 * (r % 2) : 2 * (r % 2) + 2, :] = pair_of

    def interaction():
        now = field[...].reshape(rows * half, bins).astype(jnp.bfloat16)
        product = jnp.dot(now, left[...], preferred_element_type=jnp.float32) * jnp.dot(
            now, right[...], preferred_element_type=jnp.float32
        )
        result = dot_on(product.astype(jnp.bfloat16), out_map[...], 1, 1, None)
        source[...] = (inter_step * result).reshape(source.shape)

    def finish(s, moves):
        for m in moves[4:]:
            m.wait_recv()
        for side, speed, start in ((0, speed_l, 6), (1, speed_r, half + 8)):
            here = halo_y[s, side]
            before, after = (jnp.concatenate([halo_c[s, side, i]] * 2, axis=0) for i in range(2))
            low = iota((8, bins), 0)

            def joined(a, b, n):
                return jnp.where(low < n, pltpu.roll(a, n, 0), pltpu.roll(b, n, 0))

            packed = sweep(
                here,
                joined(before, here, 2),
                joined(before, here, 4),
                joined(here, after, 6),
                joined(here, after, 4),
                speed[...],
            )
            for r in range(rows):
                wide[r, start : start + 2, :] = packed[2 * r : 2 * r + 2]

        def line(r):
            if r < 0:
                return halo_x[s, 0, r + 2]
            if r >= rows:
                return halo_x[s, 1, r - rows]
            return field[r]

        waits = {1: moves[0:2], 0: moves[2:4]}
        for r in [*range(1, rows - 1), 0, rows - 1]:
            for m in waits.get(r, ()):
                m.wait_recv()
            wide[r, 8 : 8 + half, :] = sweep(
                line(r), line(r - 1), line(r - 2), line(r + 1), line(r + 2), speed_x[r]
            )
            b = sweep(
                wide[r, 8 : 8 + half, :],
                wide[r, 7 : 7 + half, :],
                wide[r, 6 : 6 + half, :],
                wide[r, 9 : 9 + half, :],
                wide[r, 10 : 10 + half, :],
                speed_y[r],
            )
            t = turn[r]
            behind = jnp.concatenate([b[:, bins - NFL :], b[:, : bins - NFL]], axis=1)
            ahead = jnp.concatenate([b[:, NFL:], b[:, :NFL]], axis=1)
            c = b - jnp.abs(t) * (b - jnp.where(t >= 0.0, behind, ahead))
            source[r] = flow[r, :, 2 * NF : 2 * NF + 1] * (c + source[r])
        for m in moves:
            m.wait_send()
        field[...] = source[...]

    def flow_moves():
        return [
            Move(
                flow_edge.at[side],
                flow_halo.at[1 - side],
                init_send.at[3 + side],
                init_recv.at[3 + side],
                q_at(0, dq),
                inside(q, dq, nq),
                inside(q, -dq, nq),
            )
            for side, dq in ((0, -1), (1, 1))
        ]

    def received(k, row):
        Move(
            masked.at[row, away, :], field.at[tile_x * (1 - y) + row], init_send.at[k], init_recv.at[k], at(0, pair), True, True
        ).wait_recv()

    received(1, 1 - y)
    pl.when(y == 1)(first_moves[0].start)
    pl.when(y == 0)(first_moves[1].start)
    received(9, y)
    set_edges(0)
    for m in first_moves[4:]:
        m.start()
    pl.when(y == 1)(first_moves[2].start)
    pl.when(y == 0)(first_moves[3].start)
    set_col_edges(0, ocean)
    flow_pair.wait_recv()
    for side, first in ((0, 0), (1, half - 2)):
        for r in range(rows):
            flow_edge[side, 2 * r : 2 * r + 2, :] = flow[r, first : first + 2, :]
    edges_flow = flow_moves()
    for m in edges_flow:
        m.start()
    sea_first = sea_moves(0, ocean)
    for m in sea_first:
        m.start()
    fq = flow[...].reshape(rows * half, LANES)
    fx = exact_dot(fq, spread_x)
    fy = exact_dot(fq, spread_y)
    speed_x[...] = (group_speed * cosine + fx).reshape(speed_x.shape)
    speed_y[...] = (group_speed * sine + fy).reshape(speed_x.shape)
    turn[...] = (turning * (sine * fx - cosine * fy)).reshape(speed_x.shape)
    for load in loads[1:]:
        load.wait()
    interaction()
    depth = dot_on(dw[...], spread_x[0:NF], 0, 0)
    profile[0:NLEV] = depth * cosine
    profile[NLEV : 2 * NLEV] = depth * sine
    profile[2 * NLEV :] = jnp.zeros((LANES - 2 * NLEV, bins), jnp.float32)
    for m in edges_flow:
        m.wait_recv()
    speed_l[...] = group_speed * cosine + exact_dot(flow_halo[0], spread_x)
    speed_r[...] = group_speed * cosine + exact_dot(flow_halo[1], spread_x)
    finish(0, first_moves)

    def section(s, carry):
        set_edges(s)
        moves = wave_moves(s)
        for m in moves[4:]:
            m.start()

        @pl.when(jnp.logical_not(late))
        def _():
            for m in moves[:4]:
                m.start()

        interaction()

        @pl.when(late)
        def _():
            for m in moves[:4]:
                m.start()

        finish(s, moves)
        return carry

    lax.fori_loop(1, WAVE_SECTIONS, section, 0)

    their_rows = pl.ds(tile_x * (1 - y), tile_x)
    back = Move(
        field.at[their_rows], spec_out.at[:, mine, :], init_send.at[5], init_recv.at[5], at(0, pair), True, True
    )
    drift = lax.dot_general(
        field[...].reshape(rows * half, bins),
        profile[...],
        (((1,), (1,)), ((), ())),
        precision=highest,
        preferred_element_type=jnp.float32,
    )
    drift_q[...] = drift.reshape(drift_q.shape)
    drift_moves = [
        Move(
            drift_q.at[pl.ds(tile_x * yy, tile_x)],
            drift_n.at[g, :, mine, :],
            init_send.at[6 + k],
            init_recv.at[6 + k],
            device,
            True,
            True,
        )
        for k, (yy, device) in enumerate(((y, at(1)), (1 - y, at(1, pair)), (1 - y, at(0, pair))))
    ]
    for k in (1, 2, 0):
        drift_moves[k].start()
    back.start()
    spec_out[:, mine, :] = field[my_rows]
    drift_n[g, :, mine, :] = drift_q[my_rows]

    lane_n = iota((columns, LANES), 1)
    column_n = iota((tile_y, LANES), 0)

    def neighbours(k, array):
        result = []
        for r in range(tile_x):
            a = array[r]
            below = array[r - 1] if r > 0 else row_halo[k, 0]
            above = array[r + 1] if r < tile_x - 1 else row_halo[k, 1]
            lower = jnp.where(column_n == 0, col_halo[k, 0, r : r + 1, :], pltpu.roll(a, 1, 0))
            upper = jnp.where(column_n == tile_y - 1, col_halo[k, 1, r : r + 1, :], pltpu.roll(a, tile_y - 1, 0))
            result.append(above + below + upper + lower - 4.0 * a)
        return jnp.concatenate(result, axis=0)

    def swapped(a):
        from_v = pltpu.roll(a, LANES - NLEV, 1)
        from_u = pltpu.roll(a, NLEV, 1)
        return jnp.where(lane_n < NLEV, from_v, jnp.where(lane_n < 2 * NLEV, -from_u, 0.0))

    def ocean_section(array, laplace, drift_all):
        flat = array[...].reshape(columns, LANES)
        first = flat + ocean_step * (coriolis * swapped(flat + drift_all) + viscosity * laplace)
        return wet_n * (first + exact_dot(first, mix[...]))

    for m in sea_first:
        m.wait_recv()
    laplace_first = neighbours(0, ocean)
    for k, device in enumerate((at(1), at(1, pair), at(0, pair))):
        landing = drift_n.at[1 - g if k < 2 else g, :, mine if k == 0 else away, :]
        Move(drift_q.at[my_rows], landing, init_send.at[6 + k], init_recv.at[6 + k], device, True, True).wait_recv()
    drift_all = (drift_n[0] + drift_n[1]).reshape(columns, LANES)
    ocean_next[...] = ocean_section(ocean, laplace_first, drift_all).reshape(ocean.shape)
    set_col_edges(1, ocean_next)
    sea_second = sea_moves(1, ocean_next)
    for m in sea_second:
        m.start()

    def picking(offset):
        i, j = iota((LANES, own), 0), iota((LANES, own), 1)
        return jnp.where(i == j + own * g + offset, 1.0, 0.0)

    pick_u, pick_v = picking(0), picking(NLEV)

    def give(out, pick, values):
        for r in range(tile_x):
            out[:, r, :] = dot_on(pick, values[r * tile_y : (r + 1) * tile_y], 0, 1)

    give(du_out, pick_u, drift_all)
    give(dv_out, pick_v, drift_all)
    for m in sea_second:
        m.wait_recv()
    final = ocean_section(ocean_next, neighbours(1, ocean_next), drift_all)
    give(u_out, pick_u, final)
    give(v_out, pick_v, final)
    back.wait_recv()
    for m in [to_grp, flow_pair, back] + to_pair + edges_flow + drift_moves + sea_first + sea_second:
        m.wait_send()


def store_kernel(*refs):
    count = (len(refs) - 1) // 2
    copies = [pltpu.make_async_copy(refs[i], refs[count + i], refs[-1].at[i]) for i in range(count)]
    for copy in copies:
        copy.start()
    for copy in copies:
        copy.wait()


def solution(mesh):
    sizes = (mesh.shape["gx"], mesh.shape["gy"])
    theta = 2.0 * np.pi * np.arange(ND) / ND
    table = np.zeros((8, ND * NFL), np.float32)
    table[0] = np.repeat(np.cos(theta), NFL)
    table[1] = np.repeat(np.sin(theta), NFL)

    def body(spectrum, wet_mask, ocean_source, ocean_u, ocean_v, current_weights, drift_weights, inter_left, inter_right, inter_out, mixing):
        tile_x, tile_y, bins = spectrum.shape
        half, rows = tile_y // 2, 2 * tile_x
        own = ocean_u.shape[2]
        columns = tile_x * tile_y
        f32 = jnp.float32
        vmem = pl.BlockSpec(memory_space=pltpu.VMEM)
        sea = (tile_x, tile_y, LANES)
        sections = WAVE_SECTIONS
        wave = (rows, half, bins)

        def V(*shape):
            return pltpu.VMEM(shape, f32)

        def D(*shape):
            return pltpu.SemaphoreType.DMA(shape)

        outs = (jax.ShapeDtypeStruct(spectrum.shape, f32),) + (
            jax.ShapeDtypeStruct((own, tile_x, tile_y), f32),
        ) * 4
        anywhere = pl.BlockSpec(memory_space=pl.ANY)
        results = pl.pallas_call(
            functools.partial(kernel, sizes),
            out_shape=tuple(pltpu.VMEM(a.shape, a.dtype) for a in outs),
            in_specs=[anywhere] + [vmem] * 7 + [anywhere] * 3 + [vmem],
            out_specs=(vmem,) * 5,
            scratch_shapes=[
                V(tile_x, tile_y, bins),
                pltpu.VMEM(inter_left.shape, inter_left.dtype),
                pltpu.VMEM(inter_right.shape, inter_right.dtype),
                pltpu.VMEM(inter_out.shape[::-1], inter_out.dtype),
                D(4),
                V(columns + NLEV, LANES),
                V(LANES, LANES),
                V(LANES, bins),
                V(tile_x, tile_y, bins),
                V(columns + NLEV, LANES),
                V(*sea),
                V(rows, half, LANES),
                V(2, 8, LANES),
                V(2, 8, LANES),
                V(*wave),
                V(sections, 2, 8, bins),
                V(sections, 2, 2, half, bins),
                V(sections, 2, 8, bins),
                V(sections, 2, 2, 4, bins),
                V(sections, 2, 2, 4, bins),
                V(*wave),
                V(*wave),
                V(*wave),
                V(8, bins),
                V(8, bins),
                V(rows, half + 16, bins),
                V(*wave),
                V(LANES, LANES),
                V(*sea),
                V(*sea),
                V(2, 2, tile_y, LANES),
                V(2, 2, 8, LANES),
                V(2, 2, 8, LANES),
                V(rows, half, LANES),
                V(2, *sea),
                D(10),
                D(10),
                D(sections, 10),
                D(sections, 10),
                D(2, 4),
                D(2, 4),
            ],
            compiler_params=pltpu.CompilerParams(collective_id=0, has_side_effects=True),
        )(
            spectrum,
            wet_mask,
            ocean_source,
            jnp.transpose(ocean_u, (2, 0, 1)),
            jnp.transpose(ocean_v, (2, 0, 1)),
            jnp.asarray(table),
            current_weights.T,
            drift_weights.T,
            inter_left,
            inter_right,
            inter_out.T,
            mixing.T,
        )
        results = pl.pallas_call(
            store_kernel,
            out_shape=outs,
            in_specs=[anywhere] * 5,
            out_specs=(anywhere,) * 5,
            scratch_shapes=[D(5)],
        )(*(pltpu.with_memory_space_constraint(a, pltpu.VMEM) for a in results))
        return (results[0],) + tuple(jnp.transpose(a, (1, 2, 0)) for a in results[1:])

    tile = P("gx", "gy", "grp")
    in_specs = (
        tile,
        P("gx", "gy"),
        P("gx", "gy"),
        tile,
        tile,
        P(),
        P(),
        P("grp", None),
        P("grp", None),
        P(None, "grp"),
        P(None, "grp"),
    )
    return jax.shard_map(body, mesh=mesh, in_specs=in_specs, out_specs=(tile,) * 5, check_vma=False)
```

```python
import functools

import jax
import jax.numpy as jnp
import numpy as np
from jax import lax
from jax.experimental import pallas as pl
from jax.experimental.pallas import tpu as pltpu
from jax.sharding import PartitionSpec as P

NF = 32
ND = 36
NLEV = 40
WAVE_SECTIONS = 3
NFL = 16
LANES = 128
MESH = pl.DeviceIdType.MESH

highest = lax.Precision.HIGHEST
inter_step = 0.1
ocean_step = 0.4
coriolis = 0.5
viscosity = 0.1


def exact_dot(a, b):
    return jnp.dot(a, b, precision=highest, preferred_element_type=jnp.float32)


def dot_on(a, b, dim_a, dim_b, precision=highest):
    return lax.dot_general(
        a, b, (((dim_a,), (dim_b,)), ((), ())), precision=precision, preferred_element_type=jnp.float32
    )


def sweep(centre, back_one, back_two, next_one, next_two, velocity):
    up = velocity >= 0.0
    one = jnp.where(up, back_one, next_one)
    two = jnp.where(up, back_two, next_two)
    size = jnp.abs(velocity)
    half = 0.5 * size
    return centre - half * (3.0 * centre - 4.0 * one + two) + half * size * (centre - 2.0 * one + two)


def iota(shape, dim):
    return lax.broadcasted_iota(jnp.int32, shape, dim)


class Move:
    def __init__(self, src, dst, send, recv, device, sends, receives):
        self.copy = pltpu.make_async_remote_copy(
            src_ref=src, dst_ref=dst, send_sem=send, recv_sem=recv, device_id=device, device_id_type=MESH
        )
        self.sends, self.receives = sends, receives

    def when(self, cond, act):
        if cond is True:
            act()
        elif cond is not False:
            pl.when(cond)(act)

    def start(self):
        self.when(self.sends, self.copy.start)

    def wait_send(self):
        self.when(self.sends, self.copy.wait_send)

    def wait_recv(self):
        self.when(self.receives, self.copy.wait_recv)


def kernel(
    sizes,
    spectrum_hbm,
    wet_mask_hbm,
    ocean_source_hbm,
    ocean_u_hbm,
    ocean_v_hbm,
    angles_hbm,
    cw_hbm,
    dw_hbm,
    left_hbm,
    right_hbm,
    out_hbm,
    mixing_hbm,
    spec_out,
    u_out,
    v_out,
    du_out,
    dv_out,
    spectrum,
    wet_mask,
    ocean_source,
    ocean_u,
    ocean_v,
    angles,
    cw,
    dw,
    left,
    right,
    out_map,
    mixing,
    load_sem,
    pack,
    currents,
    profile,
    masked,
    packs,
    shares,
    share_in,
    seam_in,
    flow,
    edge_first,
    halo_first,
    field,
    edge,
    halo_x,
    halo_y,
    corner,
    halo_c,
    speed_x,
    speed_y,
    turn,
    speed_l,
    speed_r,
    wide,
    source,
    mix,
    ocean,
    ocean_next,
    row_halo,
    col_edge,
    col_halo,
    drift_q,
    drift_n,
    drift_c,
    init_send,
    init_recv,
    first_send,
    first_recv,
    wave_send,
    wave_recv,
    sea_send,
    sea_recv,
    drift_send,
    drift_recv,
):
    nx, ny = sizes
    loads = [
        pltpu.make_async_copy(src, dst, load_sem.at[k])
        for k, (src, dst) in enumerate(
            (
                (spectrum_hbm, spectrum),
                (wet_mask_hbm, wet_mask),
                (ocean_source_hbm, ocean_source),
                (ocean_u_hbm, ocean_u),
                (ocean_v_hbm, ocean_v),
                (cw_hbm, cw),
                (mixing_hbm, mixing),
                (angles_hbm, angles),
                (dw_hbm, dw),
                (left_hbm, left),
                (right_hbm, right),
                (out_hbm, out_map),
            )
        )
    ]
    for load in loads[:2]:
        load.start()
    tile_x, tile_y, bins = spectrum.shape
    half = tile_y // 2
    own = u_out.shape[0]
    rows = 2 * tile_x
    g, gx, gy = lax.axis_index("grp"), lax.axis_index("gx"), lax.axis_index("gy")
    z, y = gx // 2, gx % 2
    flip = (y + gy) % 2
    q = 2 * gy + flip
    late = gy % 2 == 1
    nz, nq = nx // 2, 2 * ny

    def at(dg=0, x=gx, c=gy):
        return {"grp": (g + dg) % 2, "gx": x, "gy": c}

    pair = 2 * z + 1 - y

    def q_at(dz, dq):
        qq = q + dq
        return at(0, 2 * (z + dz) + (qq + qq // 2) % 2, qq // 2)

    def inside(value, step, limit):
        return value + step >= 0 if step < 0 else value + step < limit

    def both(dz, dq):
        cond = inside(q, dq, nq)
        return cond if dz == 0 else cond & inside(z, dz, nz)

    def near(dg, dz, yy, dc):
        return {"grp": (g + dg) % 2, "gx": 2 * (z + dz) + yy, "gy": gy + dc}

    barrier = pltpu.get_barrier_semaphore()
    total = 0
    for dz in (-1, 0, 1):
        for dc in (-1, 0, 1):
            friends = [at(1), at(0, pair), at(1, pair)]
            if dz or dc:
                groups = (0,) if dz and dc else (0, 1)
                friends = [near(dg, dz, yy, dc) for dg in groups for yy in (0, 1)]
            cond = inside(z, dz, nz) & inside(gy, dc, ny)

            @pl.when(cond)
            def _():
                for device in friends:
                    pl.semaphore_signal(barrier, inc=1, device_id=device, device_id_type=MESH)

            total = total + jnp.where(cond, len(friends), 0)

    for load in loads[2:]:
        load.start()
    columns = tile_x * tile_y

    def as_columns(table):
        ones = jnp.ones((1, LANES), jnp.float32)
        values = table[...].astype(jnp.float32)
        return jnp.concatenate([dot_on(values[r : r + 1], ones, 0, 0) for r in range(tile_x)], axis=0)

    loads[1].wait()
    wet_wide = as_columns(wet_mask)
    wet_n = wet_wide[:, 0:1]

    away = pl.ds(pl.multiple_of(half * (1 - flip), 8), half)
    mine = pl.ds(pl.multiple_of(half * flip, 8), half)
    my_rows = pl.ds(tile_x * y, tile_x)

    reaches = jnp.where(y == 0, z > 0, z < nz - 1)

    @pl.when(jnp.logical_not(reaches))
    def _():
        drift_n[:, (tile_x + 1) * y] = jnp.zeros_like(drift_n[:, 0])

    @pl.when(z == 0)
    def _():
        halo_x[:, 0] = jnp.zeros_like(halo_x[:, 0])

    @pl.when(z == nz - 1)
    def _():
        halo_x[:, 1] = jnp.zeros_like(halo_x[:, 1])

    for side, dq in ((0, -1), (1, 1)):

        @pl.when(jnp.logical_not(inside(q, dq, nq)))
        def _():
            halo_y[:, side] = jnp.zeros_like(halo_y[:, side])
            halo_c[:, side] = jnp.zeros_like(halo_c[:, side])
            halo_first[side] = jnp.zeros_like(halo_first[side])
            seam_in[...] = jnp.zeros_like(seam_in)

        for slot, dz in ((0, -1), (1, 1)):

            @pl.when(inside(q, dq, nq) & jnp.logical_not(inside(z, dz, nz)))
            def _():
                halo_c[:, side, slot] = jnp.zeros_like(halo_c[:, side, slot])

    for side, d in ((0, -1), (1, 1)):

        @pl.when(jnp.logical_not(inside(gx, d, nx)))
        def _():
            row_halo[:, side] = jnp.zeros_like(row_halo[:, side])

        @pl.when(jnp.logical_not(inside(gy, d, ny)))
        def _():
            col_halo[:, side] = jnp.zeros_like(col_halo[:, side])
            drift_c[:, side] = jnp.zeros_like(drift_c[:, side])

    loads[0].wait()
    masked[...] = (spectrum[...].reshape(columns, bins) * wet_n).reshape(tile_x, tile_y, bins)

    for k, first in enumerate((0, half - 2, half, tile_y - 2)):
        for r in range(tile_x):
            edge_first[k, 2 * r : 2 * r + 2, :] = masked[r, first : first + 2, :]

    for load in loads[2:8]:
        load.wait()
    place_i, place_j = iota((own, LANES), 0), iota((own, LANES), 1)
    place_u = jnp.where(place_j == place_i + own * g, 1.0, 0.0)
    place_v = jnp.where(place_j == place_i + own * g + NLEV, 1.0, 0.0)
    for r in range(tile_x):
        pack[r * tile_y : (r + 1) * tile_y] = dot_on(ocean_u[:, r, :], place_u, 0, 0) + dot_on(
            ocean_v[:, r, :], place_v, 0, 0
        )
    pack[columns:] = dot_on(mixing[...], place_u, 0, 0)
    chosen_at = as_columns(ocean_source)[:, 0:1]
    chosen = jnp.where(iota((columns, columns), 1).astype(jnp.float32) == chosen_at, 1.0, 0.0)
    currents[...] = jnp.zeros_like(currents)
    for b in range(NF // NFL):
        at_u = 2 * NFL * b
        currents[at_u : at_u + NFL, 0:NLEV] = cw[b * NFL : (b + 1) * NFL]
        currents[at_u + NFL : at_u + 2 * NFL] = pltpu.roll(currents[at_u : at_u + NFL], NLEV, 1)
    felt = exact_dot(chosen, dot_on(pack[:columns], currents[...], 1, 1))
    lane_t = iota((tile_y, LANES), 1)
    row_lanes = 2 * NFL
    for b in range(NF // NFL):
        share = jnp.zeros((tile_y, LANES), jnp.float32)
        for r in range(tile_x):
            own_row = felt[r * tile_y : (r + 1) * tile_y]
            shift = (r - b) * row_lanes % LANES
            own_row = pltpu.roll(own_row, shift, 1) if shift else own_row
            share = jnp.where((lane_t >= r * row_lanes) & (lane_t < (r + 1) * row_lanes), own_row, share)
            wet_lane = lane_t == jnp.where(g == b, tile_x * row_lanes + r, LANES)
            share = jnp.where(wet_lane, wet_wide[r * tile_y : (r + 1) * tile_y], share)
        shares[b] = share
    field[0, my_rows] = masked[:, mine, :]
    with jax.named_scope("barrier"):
        pl.semaphore_wait(barrier, total)

    to_pair = [
        Move(
            masked.at[row, away, :],
            field.at[0, tile_x * y + row],
            init_send.at[k],
            init_recv.at[k],
            at(0, pair),
            True,
            True,
        )
        for k, row in ((1, y), (9, 1 - y))
    ]
    dz_first = 2 * y - 1
    reaches_back = jnp.where(y == 0, z < nz - 1, z > 0)

    def layer(k, source_ref, row, owner, device, cond):
        return Move(
            source_ref,
            halo_x.at[0, 1 - owner, row],
            first_send.at[k],
            first_recv.at[2 * (1 - owner) + row],
            device,
            cond,
            False,
        )

    straight = [
        layer(k, masked.at[row, mine, :], row, y, near(0, dz_first, y, 0), reaches) for k, row in ((0, y), (1, 1 - y))
    ]
    across = [
        layer(k, masked.at[row, away, :], row, y, near(0, dz_first, 1 - y, 0), reaches & jnp.logical_not(late))
        for k, row in ((2, y), (3, 1 - y))
    ]
    passed_on = [
        layer(k, field.at[0, tile_x * (1 - y) + row], row, 1 - y, near(0, -dz_first, y, 0), reaches_back & late)
        for k, row in ((2, 1 - y), (3, y))
    ]
    def strip_at(dz, strip):
        return near(0, dz, (strip + strip // 2) % 2, strip // 2 - gy)

    left_tile, right_tile = gy > 0, gy < ny - 1
    edges_first = [
        Move(
            edge_first.at[1 + flip],
            halo_first.at[flip, y],
            first_send.at[4],
            first_recv.at[6],
            at(0, pair),
            True,
            True,
        )
    ]
    after = 1 - y
    for k, (cond, strip, side) in enumerate(
        ((left_tile, 2 * gy - 1, 1), (True, 2 * gy + 1, 0), (True, 2 * gy, 1), (right_tile, 2 * gy + 2, 0))
    ):
        if cond is not True:
            edges_first.append(
                Move(
                    edge_first.at[k],
                    halo_first.at[side, y],
                    first_send.at[5 + side],
                    first_recv.at[4 + y],
                    strip_at(0, strip),
                    cond,
                    False,
                )
            )
        edges_first.append(
            Move(
                edge_first.at[k],
                halo_c.at[0, side, after],
                first_send.at[7 + k],
                first_recv.at[7 + after if cond is True else 9 + after],
                strip_at(dz_first, strip),
                reaches if cond is True else reaches & cond,
                False,
            )
        )
    halo_first[1 - flip, y] = edge_first[2 - flip]

    def wave_moves(s):
        moves = []
        for near in (True, False):
            for side, dz in ((0, -1), (1, 1)):
                layer = 0 if near == (dz < 0) else 1
                moves.append(
                    Move(
                        field.at[s % 2, layer if dz < 0 else rows - 2 + layer],
                        halo_x.at[s, 1 - side, layer],
                        wave_send.at[s, len(moves)],
                        wave_recv.at[s, len(moves)],
                        at(0, gx + 2 * dz),
                        inside(z, dz, nz),
                        inside(z, -dz, nz),
                    )
                )
        k = 4
        for side, dq in ((0, -1), (1, 1)):
            for dz in (-1, 0, 1):
                moves.append(
                    Move(
                        edge.at[s, side] if dz == 0 else corner.at[s, side, (1 + dz) // 2],
                        halo_y.at[s, 1 - side] if dz == 0 else halo_c.at[s, 1 - side, (1 - dz) // 2],
                        wave_send.at[s, k],
                        wave_recv.at[s, k],
                        q_at(dz, dq),
                        both(dz, dq),
                        both(-dz, -dq),
                    )
                )
                k += 1
        return moves

    wider = half + 8

    def wide_strip(f):
        return pl.ds(pl.multiple_of((tile_y - wider) * f, 8), wider)

    share_moves = [
        Move(
            shares.at[(g + dg) % 2, wide_strip(f), :],
            share_in.at[g, y],
            init_send.at[2 + k],
            init_recv.at[2 + k],
            device,
            True,
            True,
        )
        for k, (dg, f, device) in enumerate(
            ((1, 1 - flip, at(1, pair)), (1, flip, at(1)), (0, 1 - flip, at(0, pair)))
        )
    ]
    for dg in (1, 0):
        for side, (cond, strip, block) in enumerate(
            ((left_tile, 2 * gy - 1, pl.ds(0, 8)), (right_tile, 2 * gy + 2, pl.ds(tile_y - 8, 8)))
        ):
            share_moves.append(
                Move(
                    shares.at[(g + dg) % 2, block, :],
                    seam_in.at[g, y],
                    first_send.at[11 + 2 * dg + side],
                    first_recv.at[11 + 2 * dg + y],
                    {**strip_at(0, strip), "grp": (g + dg) % 2},
                    cond,
                    False,
                )
            )
    for m in share_moves + to_pair + straight + edges_first + across:
        m.start()
    share_in[g, y] = shares[g, wide_strip(flip), :]
    to_grp = Move(pack, packs, init_send.at[0], init_recv.at[0], at(1), True, True)
    to_grp.start()

    def arrived(ref, sem, cond=True):
        Move(ref, ref, sem, sem, at(0, pair), False, cond).wait_recv()

    outer = jnp.where(flip == 0, left_tile, right_tile)
    above, below = z > 0, z < nz - 1

    def edges_arrived():
        edges_first[0].wait_recv()
        for yy in range(2):
            arrived(halo_first.at[flip, yy], first_recv.at[4 + yy], outer)
        for i, cond in enumerate((above, below)):
            arrived(halo_c.at[0, 1 - flip, i], first_recv.at[7 + i], cond)
            arrived(halo_c.at[0, flip, i], first_recv.at[9 + i], cond & outer)

    def layers_arrived(first):
        for side, cond, layer in ((0, above, 1 if first else 0), (1, below, 0 if first else 1)):
            arrived(halo_x.at[0, side, layer], first_recv.at[2 * side + layer], cond)

    def sea_moves(k, array):
        moves = []
        for side, d in ((0, -1), (1, 1)):
            moves.append(
                Move(
                    array.at[0 if d < 0 else tile_x - 1],
                    row_halo.at[k, 1 - side],
                    sea_send.at[k, side],
                    sea_recv.at[k, side],
                    at(0, gx + d),
                    inside(gx, d, nx),
                    inside(gx, -d, nx),
                )
            )
            moves.append(
                Move(
                    col_edge.at[k, side],
                    col_halo.at[k, 1 - side],
                    sea_send.at[k, 2 + side],
                    sea_recv.at[k, 2 + side],
                    at(0, gx, gy + d),
                    inside(gy, d, ny),
                    inside(gy, -d, ny),
                )
            )
        return moves

    def set_col_edges(k, array):
        for side, column in ((0, 0), (1, tile_y - 1)):
            for r in range(tile_x):
                col_edge[k, side, r : r + 1, :] = array[r, column : column + 1, :]

    lane = iota((1, bins), 1)
    frequency = (g * NFL + (lane & (NFL - 1))).astype(jnp.float32)
    group_speed = 0.2 + 0.4 * (NF - 1 - frequency) / (NF - 1)
    turning = 0.5 * (frequency + 1.0) / NF
    cosine, sine = angles[0:1, :], angles[1:2, :]
    spread_f = g * NFL + (iota((NF, bins), 1) & (NFL - 1))
    spread = jnp.where(iota((NF, bins), 0) == spread_f, 1.0, 0.0)

    def repeated(values, start):
        place = iota(values.shape, 1)
        values = pltpu.roll(values, LANES - start, 1) if start else values
        width = NFL
        while width < LANES:
            values = jnp.where(place < width, values, pltpu.roll(values, width, 1))
            width *= 2
        return jnp.concatenate([values] * (-(-bins // LANES)), axis=1)[:, :bins]

    def set_edges(s, r, values):
        for side, first in ((0, 0), (1, half - 2)):
            pair_of = values[first : first + 2]
            edge[s, side, 2 * r : 2 * r + 2, :] = pair_of
            corner[s, side, r // 2, 2 * (r % 2) : 2 * (r % 2) + 2, :] = pair_of

    def interaction(s):
        now = field[s % 2].reshape(rows * half, bins).astype(jnp.bfloat16)
        product = jnp.dot(now, left[...], preferred_element_type=jnp.float32) * jnp.dot(
            now, right[...], preferred_element_type=jnp.float32
        )
        result = dot_on(product.astype(jnp.bfloat16), out_map[...], 1, 1, None)
        source[...] = (inter_step * result).reshape(source.shape)

    def finish(s, edges_in, layers_in, edge_of, written):
        with jax.named_scope("wait_edges"):
            edges_in()
        for side, speed, start in ((0, speed_l, 6), (1, speed_r, half + 8)):
            here = edge_of(side)
            before, after = (jnp.concatenate([halo_c[s, side, i]] * 2, axis=0) for i in range(2))
            low = iota((8, bins), 0)

            def joined(a, b, n):
                return jnp.where(low < n, pltpu.roll(a, n, 0), pltpu.roll(b, n, 0))

            packed = sweep(
                here,
                joined(before, here, 2),
                joined(before, here, 4),
                joined(here, after, 6),
                joined(here, after, 4),
                speed[...],
            )
            for r in range(rows):
                wide[r, start : start + 2, :] = packed[2 * r : 2 * r + 2]

        def line(r):
            if r < 0:
                return halo_x[s, 0, r + 2]
            if r >= rows:
                return halo_x[s, 1, r - rows]
            return field[s % 2, r]

        for r in [*range(1, rows - 1), 0, rows - 1]:
            if r < 2:
                with jax.named_scope("wait_layers"):
                    layers_in(r == 1)
            wide[r, 8 : 8 + half, :] = sweep(
                line(r), line(r - 1), line(r - 2), line(r + 1), line(r + 2), speed_x[r]
            )
            b = sweep(
                wide[r, 8 : 8 + half, :],
                wide[r, 7 : 7 + half, :],
                wide[r, 6 : 6 + half, :],
                wide[r, 9 : 9 + half, :],
                wide[r, 10 : 10 + half, :],
                speed_y[r],
            )
            t = turn[r]
            behind = jnp.concatenate([b[:, bins - NFL :], b[:, : bins - NFL]], axis=1)
            ahead = jnp.concatenate([b[:, NFL:], b[:, :NFL]], axis=1)
            c = b - jnp.abs(t) * (b - jnp.where(t >= 0.0, behind, ahead))
            wet_at = tile_x * row_lanes + r % tile_x
            values = flow[r, :, wet_at : wet_at + 1] * (c + source[r])
            field[(s + 1) % 2, r] = values
            if s + 1 < WAVE_SECTIONS:
                set_edges(s + 1, r, values)
            if r in (rows - 2, rows - 1):
                written(r == rows - 2)

    with jax.named_scope("pair"):
        for m, onward in zip(to_pair, passed_on):
            m.wait_recv()
            onward.start()
    with jax.named_scope("load_rest"):
        for load in loads[8:]:
            load.wait()
    with jax.named_scope("inter"):
        interaction(0)
    with jax.named_scope("flow_wait"):
        for m in share_moves[:3]:
            m.wait_recv()
        for dg in range(2):
            for yy in range(2):
                arrived(seam_in.at[(g + dg) % 2, yy], first_recv.at[11 + 2 * dg + yy], outer)
    side_f = [[], []]
    low = iota((8, LANES), 0)
    for yy in range(2):
        felt_here = share_in[0, yy, pl.ds(pl.multiple_of(8 * flip, 8), half), :] + share_in[
            1, yy, pl.ds(pl.multiple_of(8 * flip, 8), half), :
        ]
        inner = pl.ds(pl.multiple_of(half * (1 - flip), 8), 8)
        inner_f = share_in[0, yy, inner, :] + share_in[1, yy, inner, :]
        seam_f = seam_in[0, yy] + seam_in[1, yy]
        for r in range(tile_x):
            row = tile_x * yy + r
            flow[row] = felt_here
            fx, fy = (repeated(felt_here, r * row_lanes + k * NFL) for k in (0, 1))
            speed_x[row] = group_speed * cosine + fx
            speed_y[row] = group_speed * sine + fy
            turn[row] = turning * (sine * fx - cosine * fy)
        side_f[0].append(jnp.where(flip == 0, seam_f, inner_f))
        side_f[1].append(jnp.where(flip == 0, inner_f, seam_f))
    for side, speed in ((0, speed_l), (1, speed_r)):
        packed_f = jnp.zeros((8, LANES), jnp.float32)
        for yy in range(2):
            for r in range(tile_x):
                at_row = 2 * (tile_x * yy + r)
                piece = side_f[side][yy]
                shift = (at_row - (6 if side == 0 else 0)) % 8
                piece = pltpu.roll(piece, shift, 0) if shift else piece
                piece = pltpu.roll(piece, LANES - r * row_lanes, 1) if r else piece
                packed_f = jnp.where((low >= at_row) & (low < at_row + 2), piece, packed_f)
        speed[...] = group_speed * cosine + repeated(packed_f, 0)
    column_n = iota((tile_y, LANES), 0)

    def neighbours(k, array):
        result = []
        for r in range(tile_x):
            a = array[r]
            below = array[r - 1] if r > 0 else row_halo[k, 0]
            above = array[r + 1] if r < tile_x - 1 else row_halo[k, 1]
            lower = jnp.where(column_n == 0, col_halo[k, 0, r : r + 1, :], pltpu.roll(a, 1, 0))
            upper = jnp.where(column_n == tile_y - 1, col_halo[k, 1, r : r + 1, :], pltpu.roll(a, tile_y - 1, 0))
            result.append(above + below + upper + lower - 4.0 * a)
        return jnp.concatenate(result, axis=0)

    def swapped(a):
        lane_n = iota(a.shape, 1)
        from_v = pltpu.roll(a, LANES - NLEV, 1)
        from_u = pltpu.roll(a, NLEV, 1)
        return jnp.where(lane_n < NLEV, from_v, jnp.where(lane_n < 2 * NLEV, -from_u, 0.0))

    def mixed(first, wet):
        return wet * (first + exact_dot(first, mix[...]))

    def with_wet(a):
        return jnp.where(iota(a.shape, 1) == 2 * NLEV, wet_wide, a)

    sea_first = sea_moves(0, ocean)
    sea_second = sea_moves(1, ocean_next)

    def ocean_gather():
        to_grp.wait_recv()
        everything = pack[...] + packs[...]
        ocean[...] = with_wet(everything[:columns]).reshape(ocean.shape)
        mix[...] = jnp.zeros_like(mix)
        mix[0:NLEV] = everything[columns:]
        mix[NLEV : 2 * NLEV] = pltpu.roll(everything[columns:], NLEV, 1)
        set_col_edges(0, ocean)
        for m in sea_first:
            m.start()

    def ocean_prepare():
        for m in sea_first:
            m.wait_recv()
        flat = ocean[...].reshape(columns, LANES)
        plain = flat + ocean_step * (coriolis * swapped(flat) + viscosity * neighbours(0, ocean))
        ocean_next[...] = with_wet(plain).reshape(ocean.shape)
        set_col_edges(1, ocean_next)
        for m in sea_second:
            m.start()
        for m in sea_first:
            m.wait_send()

    def wave_profile():
        depth = dot_on(dw[...], spread, 0, 0)
        profile[0:NLEV] = depth * cosine
        profile[NLEV : 2 * NLEV] = depth * sine
        profile[2 * NLEV :] = jnp.zeros((LANES - 2 * NLEV, bins), jnp.float32)

    all_moves = [None] + [wave_moves(s) for s in range(1, WAVE_SECTIONS)]

    def next_written(s):
        def written(interior):
            moves = all_moves[s]
            if interior:

                @pl.when(late)
                def _():
                    for m in moves[2:4]:
                        m.start()

            else:
                for m in moves[4:]:
                    m.start()
                for m in moves[:2]:
                    m.start()

                @pl.when(jnp.logical_not(late))
                def _():
                    for m in moves[2:4]:
                        m.start()

        return written

    their = tile_x * (1 - y)
    back = [
        Move(
            field.at[WAVE_SECTIONS % 2, their + row],
            spec_out.at[row, mine, :],
            init_send.at[k],
            init_recv.at[k],
            at(0, pair),
            True,
            True,
        )
        for k, row in ((5, y), (10, 1 - y))
    ]

    def last_written(interior):
        if interior:
            back[0].start()

    finish(
        0,
        edges_arrived,
        layers_arrived,
        lambda side: jnp.concatenate([halo_first[side, 0], halo_first[side, 1]], axis=0),
        next_written(1),
    )

    def section(s, meanwhile):
        moves = all_moves[s]
        with jax.named_scope("inter"):
            interaction(s)


        for work in meanwhile:
            work()
        with jax.named_scope("wait_send"):
            for m in all_moves[s - 1] if s > 1 else passed_on:
                m.wait_send()

        def edges_in():
            for m in moves[4:]:
                m.wait_recv()

        def layers_in(first):
            for m in moves[0:2] if first else moves[2:4]:
                m.wait_recv()

        written = next_written(s + 1) if s + 1 < WAVE_SECTIONS else last_written
        finish(s, edges_in, layers_in, lambda side: halo_y[s, side], written)

    for s in range(1, WAVE_SECTIONS):
        section(s, {1: (ocean_gather, wave_profile), 2: (ocean_prepare,)}.get(s, ()))

    last = field.at[WAVE_SECTIONS % 2]
    drift = lax.dot_general(
        last[...].reshape(rows * half, bins),
        profile[...],
        (((1,), (1,)), ((), ())),
        precision=highest,
        preferred_element_type=jnp.float32,
    )
    drift_q[...] = drift.reshape(drift_q.shape)
    drift_moves = [
        Move(
            drift_q.at[pl.ds((tile_x - 1) * yy, tile_x + 1)],
            drift_n.at[g, pl.ds(1 - yy, tile_x + 1), mine, :],
            init_send.at[6 + k],
            init_recv.at[6 + k],
            device,
            True,
            True,
        )
        for k, (yy, device) in enumerate(((1 - y, at(1, pair)), (1 - y, at(0, pair)), (y, at(1))))
    ]
    to_side = 1 - 2 * flip
    for dg in (1, 0):
        for side, (row, at_row, device, cond) in enumerate(
            ((0, tile_x + 1, near(dg, -1, 1, 0), above), (rows - 1, 0, near(dg, 1, 0, 0), below))
        ):
            drift_moves.append(
                Move(
                    drift_q.at[row],
                    drift_n.at[g, at_row, mine, :],
                    drift_send.at[2 * dg + side],
                    drift_recv.at[2 * dg + y],
                    device,
                    cond,
                    False,
                )
            )
        for yy in range(2):
            drift_moves.append(
                Move(
                    drift_q.at[pl.ds(tile_x * yy, tile_x), pl.ds(pl.multiple_of((half - 8) * flip, 8), 8), :],
                    drift_c.at[g, 1 - flip],
                    drift_send.at[4 + 2 * dg + yy],
                    drift_recv.at[4 + 2 * dg + 1 - flip],
                    near(dg, 0, yy, -to_side),
                    outer,
                    False,
                )
            )
    for m in drift_moves:
        m.start()
    back[1].start()
    spec_out[:, mine, :] = last[my_rows]
    drift_n[g, pl.ds(1 - y, tile_x + 1), mine, :] = drift_q[pl.ds((tile_x - 1) * y, tile_x + 1)]
    with jax.named_scope("sea_second"):
        for m in sea_second:
            m.wait_recv()
    with jax.named_scope("drift_wait"):
        for m in drift_moves[:3]:
            m.wait_recv()
        for dg in range(2):
            for yy in range(2):
                strip_cols = pl.ds(pl.multiple_of(half * ((yy + gy) % 2), 8), half)
                arrived(
                    drift_n.at[(g + dg) % 2, (tile_x + 1) * y, strip_cols, :], drift_recv.at[2 * dg + yy], reaches
                )
            for side, cond in enumerate((left_tile, right_tile)):
                arrived(drift_c.at[(g + dg) % 2, side], drift_recv.at[4 + 2 * dg + side], cond)
    drift_rows = (drift_n[0] + drift_n[1]).reshape((tile_x + 2) * tile_y, LANES)
    low_n = iota((8, LANES), 0)
    parts, drifts = [], [drift_rows]
    for side in range(2):
        beside = drift_c[0, side] + drift_c[1, side]
        packed = jnp.zeros((8, LANES), jnp.float32)
        for r in range(tile_x):
            shift = (r + 1) % 8 if side == 0 else r
            piece = pltpu.roll(beside[r], shift, 0) if shift else beside[r]
            packed = jnp.where(low_n == r, piece, packed)
        drifts.append(packed)
    plain = jnp.concatenate(
        [row_halo[1, 0]] + [ocean_next[r] for r in range(tile_x)] + [row_halo[1, 1], col_halo[1, 0], col_halo[1, 1]], axis=0
    )
    first = plain + ocean_step * coriolis * swapped(jnp.concatenate(drifts, axis=0))
    after_one = mixed(first, plain[:, 2 * NLEV : 2 * NLEV + 1])
    sea = (tile_x + 2) * tile_y
    row_halo[0, 0] = after_one[:tile_y]
    flat = after_one[tile_y : sea - tile_y]
    ocean[...] = flat.reshape(ocean.shape)
    row_halo[0, 1] = after_one[sea - tile_y : sea]
    col_halo[0, 0] = after_one[sea : sea + 8]
    col_halo[0, 1] = after_one[sea + 8 :]
    drift_all = drift_rows[tile_y : sea - tile_y]

    def picking(offset):
        i, j = iota((LANES, own), 0), iota((LANES, own), 1)
        return jnp.where(i == j + own * g + offset, 1.0, 0.0)

    pick_u, pick_v = picking(0), picking(NLEV)

    def give(out, pick, values):
        for r in range(tile_x):
            out[:, r, :] = dot_on(pick, values[r * tile_y : (r + 1) * tile_y], 0, 1)

    give(du_out, pick_u, drift_all)
    give(dv_out, pick_v, drift_all)
    second = flat + ocean_step * (coriolis * swapped(flat + drift_all) + viscosity * neighbours(0, ocean))
    final = mixed(second, wet_n)
    give(u_out, pick_u, final)
    give(v_out, pick_v, final)
    with jax.named_scope("back"):
        for m in back:
            m.wait_recv()
    sent = [to_grp] + back + all_moves[-1] + to_pair + straight + across + edges_first + share_moves + drift_moves + sea_second
    for m in sent:
        m.wait_send()


def store_kernel(*refs):
    count = (len(refs) - 1) // 2
    copies = [pltpu.make_async_copy(refs[i], refs[count + i], refs[-1].at[i]) for i in range(count)]
    for copy in copies:
        copy.start()
    for copy in copies:
        copy.wait()


def solution(mesh):
    sizes = (mesh.shape["gx"], mesh.shape["gy"])
    theta = 2.0 * np.pi * np.arange(ND) / ND
    table = np.zeros((8, ND * NFL), np.float32)
    table[0] = np.repeat(np.cos(theta), NFL)
    table[1] = np.repeat(np.sin(theta), NFL)

    def body(spectrum, wet_mask, ocean_source, ocean_u, ocean_v, current_weights, drift_weights, inter_left, inter_right, inter_out, mixing):
        tile_x, tile_y, bins = spectrum.shape
        half, rows = tile_y // 2, 2 * tile_x
        own = ocean_u.shape[2]
        columns = tile_x * tile_y
        f32 = jnp.float32
        vmem = pl.BlockSpec(memory_space=pltpu.VMEM)
        sea = (tile_x, tile_y, LANES)
        sections = WAVE_SECTIONS
        wave = (rows, half, bins)

        def V(*shape):
            return pltpu.VMEM(shape, f32)

        def D(*shape):
            return pltpu.SemaphoreType.DMA(shape)

        outs = (jax.ShapeDtypeStruct(spectrum.shape, f32),) + (
            jax.ShapeDtypeStruct((own, tile_x, tile_y), f32),
        ) * 4
        anywhere = pl.BlockSpec(memory_space=pl.ANY)
        results = pl.pallas_call(
            functools.partial(kernel, sizes),
            out_shape=tuple(pltpu.VMEM(a.shape, a.dtype) for a in outs),
            in_specs=[anywhere] * 12,
            out_specs=(vmem,) * 5,
            scratch_shapes=[
                V(tile_x, tile_y, bins),
                pltpu.VMEM(wet_mask.shape, wet_mask.dtype),
                pltpu.VMEM(ocean_source.shape, ocean_source.dtype),
                V(own, tile_x, tile_y),
                V(own, tile_x, tile_y),
                V(*table.shape),
                V(*current_weights.shape[::-1]),
                V(*drift_weights.shape[::-1]),
                pltpu.VMEM(inter_left.shape, inter_left.dtype),
                pltpu.VMEM(inter_right.shape, inter_right.dtype),
                pltpu.VMEM(inter_out.shape[::-1], inter_out.dtype),
                V(*mixing.shape[::-1]),
                D(12),
                V(columns + NLEV, LANES),
                V(LANES, LANES),
                V(LANES, bins),
                V(tile_x, tile_y, bins),
                V(columns + NLEV, LANES),
                V(2, tile_y, LANES),
                V(2, 2, half + 8, LANES),
                V(2, 2, 8, LANES),
                V(rows, half, LANES),
                V(4, 2 * tile_x, bins),
                V(2, 2, 2 * tile_x, bins),
                V(2, *wave),
                V(sections, 2, 8, bins),
                V(sections, 2, 2, half, bins),
                V(sections, 2, 8, bins),
                V(sections, 2, 2, 4, bins),
                V(sections, 2, 2, 4, bins),
                V(*wave),
                V(*wave),
                V(*wave),
                V(8, bins),
                V(8, bins),
                V(rows, half + 16, bins),
                V(*wave),
                V(LANES, LANES),
                V(*sea),
                V(*sea),
                V(2, 2, tile_y, LANES),
                V(2, 2, 8, LANES),
                V(2, 2, 8, LANES),
                V(rows, half, LANES),
                V(2, tile_x + 2, tile_y, LANES),
                V(2, 2, tile_x, 8, LANES),
                D(11),
                D(11),
                D(15),
                D(15),
                D(sections, 10),
                D(sections, 10),
                D(2, 4),
                D(2, 4),
                D(8),
                D(8),
            ],
            compiler_params=pltpu.CompilerParams(collective_id=0, has_side_effects=True),
        )(
            spectrum,
            wet_mask,
            ocean_source,
            jnp.transpose(ocean_u, (2, 0, 1)),
            jnp.transpose(ocean_v, (2, 0, 1)),
            jnp.asarray(table),
            current_weights.T,
            drift_weights.T,
            inter_left,
            inter_right,
            inter_out.T,
            mixing.T,
        )
        results = pl.pallas_call(
            store_kernel,
            out_shape=outs,
            in_specs=[anywhere] * 5,
            out_specs=(anywhere,) * 5,
            scratch_shapes=[D(5)],
        )(*(pltpu.with_memory_space_constraint(a, pltpu.VMEM) for a in results))
        return (results[0],) + tuple(jnp.transpose(a, (1, 2, 0)) for a in results[1:])

    tile = P("gx", "gy", "grp")
    in_specs = (
        tile,
        P("gx", "gy"),
        P("gx", "gy"),
        tile,
        tile,
        P(),
        P(),
        P("grp", None),
        P("grp", None),
        P(None, "grp"),
        P(None, "grp"),
    )
    return jax.shard_map(body, mesh=mesh, in_specs=in_specs, out_specs=(tile,) * 5, check_vma=False)
```

```python
import functools

import jax
import jax.numpy as jnp
import numpy as np
from jax import lax
from jax.experimental import pallas as pl
from jax.experimental.pallas import tpu as pltpu
from jax.sharding import PartitionSpec as P

NF = 32
ND = 36
NLEV = 40
WAVE_SECTIONS = 3
NFL = 16
LANES = 128
SENDS, RECEIVES = 25, 41
MESH = pl.DeviceIdType.MESH

highest = lax.Precision.HIGHEST
inter_step = 0.1
ocean_step = 0.4
coriolis = 0.5
viscosity = 0.1


def exact_dot(a, b):
    return jnp.dot(a, b, precision=highest, preferred_element_type=jnp.float32)


def dot_on(a, b, dim_a, dim_b, precision=highest):
    return lax.dot_general(
        a, b, (((dim_a,), (dim_b,)), ((), ())), precision=precision, preferred_element_type=jnp.float32
    )


def halves(a):
    high = a.astype(jnp.bfloat16)
    return high, (a - high.astype(jnp.float32)).astype(jnp.bfloat16)


def split_dot(a, both, dim):
    high, low = halves(a)
    result = dot_on(high, both, 1, dim, None) + dot_on(low, both, 1, dim, None)
    half = result.shape[1] // 2
    return result[:, :half] + result[:, half:]


def sweep(centre, back_one, back_two, next_one, next_two, velocity):
    up = velocity >= 0.0
    one = jnp.where(up, back_one, next_one)
    two = jnp.where(up, back_two, next_two)
    size = jnp.abs(velocity)
    half = 0.5 * size
    return centre - half * (3.0 * centre - 4.0 * one + two) + half * size * (centre - 2.0 * one + two)


def iota(shape, dim):
    return lax.broadcasted_iota(jnp.int32, shape, dim)


class Move:
    def __init__(self, src, dst, send, recv, device, sends, receives):
        self.copy = pltpu.make_async_remote_copy(
            src_ref=src, dst_ref=dst, send_sem=send, recv_sem=recv, device_id=device, device_id_type=MESH
        )
        self.sends, self.receives = sends, receives

    def when(self, cond, act):
        if cond is True:
            act()
        elif cond is not False:
            pl.when(cond)(act)

    def start(self):
        self.when(self.sends, self.copy.start)

    def wait_send(self):
        self.when(self.sends, self.copy.wait_send)

    def wait_recv(self):
        self.when(self.receives, self.copy.wait_recv)


def kernel(
    sizes,
    spectrum_hbm,
    wet_mask_hbm,
    ocean_source_hbm,
    ocean_u_hbm,
    ocean_v_hbm,
    angles_hbm,
    cw_hbm,
    dw_hbm,
    left_hbm,
    right_hbm,
    out_hbm,
    mixing_hbm,
    spec_out,
    u_out,
    v_out,
    du_out,
    dv_out,
    spectrum,
    wet_mask,
    ocean_source,
    ocean_u,
    ocean_v,
    angles,
    cw,
    dw,
    left,
    right,
    out_map,
    mixing,
    load_sem,
    pack,
    currents,
    profile,
    masked,
    packs,
    shares,
    share_in,
    seam_in,
    flow,
    edge_first,
    halo_first,
    field,
    edge,
    halo_x,
    halo_y,
    corner,
    halo_c,
    speed_x,
    speed_y,
    turn,
    speed_l,
    speed_r,
    wide,
    source,
    mix,
    finals,
    ocean,
    ocean_next,
    row_halo,
    col_edge,
    col_halo,
    drift_q,
    drift_n,
    drift_c,
    send_sem,
    recv_sem,
):
    nx, ny = sizes

    def sent_at(k):
        if k < 8:
            return load_sem.at[k]
        return send_sem.at[k - 8] if k < SENDS else load_sem.at[8 + k - SENDS]

    def got_at(k):
        return recv_sem.at[k]

    loads = [
        pltpu.make_async_copy(src, dst, load_sem.at[k])
        for k, (src, dst) in enumerate(
            (
                (spectrum_hbm, spectrum),
                (wet_mask_hbm, wet_mask),
                (ocean_source_hbm, ocean_source),
                (ocean_u_hbm, ocean_u),
                (ocean_v_hbm, ocean_v),
                (cw_hbm, cw),
                (mixing_hbm, mixing),
                (angles_hbm, angles),
                (dw_hbm, dw),
                (left_hbm, left),
                (right_hbm, right),
                (out_hbm, out_map),
            )
        )
    ]
    for load in loads[:2]:
        load.start()
    tile_x, tile_y, bins = spectrum.shape
    half = tile_y // 2
    own = u_out.shape[0]
    rows = 2 * tile_x
    g, gx, gy = lax.axis_index("grp"), lax.axis_index("gx"), lax.axis_index("gy")
    z, y = gx // 2, gx % 2
    flip = (y + gy) % 2
    q = 2 * gy + flip
    late = gy % 2 == 1
    nz, nq = nx // 2, 2 * ny

    def at(dg=0, x=gx, c=gy):
        return {"grp": (g + dg) % 2, "gx": x, "gy": c}

    pair = 2 * z + 1 - y

    def q_at(dz, dq):
        qq = q + dq
        return at(0, 2 * (z + dz) + (qq + qq // 2) % 2, qq // 2)

    def inside(value, step, limit):
        return value + step >= 0 if step < 0 else value + step < limit

    def both(dz, dq):
        cond = inside(q, dq, nq)
        return cond if dz == 0 else cond & inside(z, dz, nz)

    def near(dg, dz, yy, dc):
        return {"grp": (g + dg) % 2, "gx": 2 * (z + dz) + yy, "gy": gy + dc}

    barrier = pltpu.get_barrier_semaphore()
    total = 0
    for dz in (-1, 0, 1):
        for dc in (-1, 0, 1):
            friends = [at(1), at(0, pair), at(1, pair)]
            if dz or dc:
                groups = (0,) if dz and dc else (0, 1)
                friends = [near(dg, dz, yy, dc) for dg in groups for yy in (0, 1)]
            cond = inside(z, dz, nz) & inside(gy, dc, ny)

            @pl.when(cond)
            def _():
                for device in friends:
                    pl.semaphore_signal(barrier, inc=1, device_id=device, device_id_type=MESH)

            total = total + jnp.where(cond, len(friends), 0)

    for load in loads[2:]:
        load.start()
    columns = tile_x * tile_y

    def as_columns(table):
        ones = jnp.ones((1, LANES), jnp.float32)
        values = table[...].astype(jnp.float32)
        exact = None if columns <= 256 else highest
        return jnp.concatenate([dot_on(values[r : r + 1], ones, 0, 0, exact) for r in range(tile_x)], axis=0)

    loads[1].wait()
    wet_wide = as_columns(wet_mask)
    wet_n = wet_wide[:, 0:1]

    away = pl.ds(pl.multiple_of(half * (1 - flip), 8), half)
    mine = pl.ds(pl.multiple_of(half * flip, 8), half)
    my_rows = pl.ds(tile_x * y, tile_x)

    reaches = jnp.where(y == 0, z > 0, z < nz - 1)

    @pl.when(jnp.logical_not(reaches))
    def _():
        drift_n[:, (tile_x + 1) * y] = jnp.zeros_like(drift_n[:, 0])

    @pl.when(z == 0)
    def _():
        halo_x[:, 0] = jnp.zeros_like(halo_x[:, 0])

    @pl.when(z == nz - 1)
    def _():
        halo_x[:, 1] = jnp.zeros_like(halo_x[:, 1])

    for side, dq in ((0, -1), (1, 1)):

        @pl.when(jnp.logical_not(inside(q, dq, nq)))
        def _():
            halo_y[:, side] = jnp.zeros_like(halo_y[:, side])
            halo_c[:, side] = jnp.zeros_like(halo_c[:, side])
            halo_first[side] = jnp.zeros_like(halo_first[side])
            seam_in[...] = jnp.zeros_like(seam_in)

        for slot, dz in ((0, -1), (1, 1)):

            @pl.when(inside(q, dq, nq) & jnp.logical_not(inside(z, dz, nz)))
            def _():
                halo_c[:, side, slot] = jnp.zeros_like(halo_c[:, side, slot])

    for side, d in ((0, -1), (1, 1)):

        @pl.when(jnp.logical_not(inside(gx, d, nx)))
        def _():
            row_halo[:, side] = jnp.zeros_like(row_halo[:, side])

        @pl.when(jnp.logical_not(inside(gy, d, ny)))
        def _():
            col_halo[:, side] = jnp.zeros_like(col_halo[:, side])
            drift_c[:, side] = jnp.zeros_like(drift_c[:, side])

    loads[0].wait()
    masked[...] = (spectrum[...].reshape(columns, bins) * wet_n).reshape(tile_x, tile_y, bins)

    for k, first in enumerate((0, half - 2, half, tile_y - 2)):
        for r in range(tile_x):
            edge_first[k, 2 * r : 2 * r + 2, :] = masked[r, first : first + 2, :]

    for load in loads[2:8]:
        load.wait()
    place_i, place_j = iota((own, LANES), 0), iota((own, LANES), 1)
    place_u = jnp.where(place_j == place_i + own * g, 1.0, 0.0)
    place_v = jnp.where(place_j == place_i + own * g + NLEV, 1.0, 0.0)

    def placed(pieces):
        values = jnp.concatenate([part.astype(jnp.float32) for a, _ in pieces for part in halves(a)], axis=0)
        places = jnp.concatenate([p for _, p in pieces for _ in range(2)], axis=0)
        return dot_on(values.astype(jnp.bfloat16), places.astype(jnp.bfloat16), 0, 0, None)

    for r in range(tile_x):
        pack[r * tile_y : (r + 1) * tile_y] = placed([(ocean_u[:, r, :], place_u), (ocean_v[:, r, :], place_v)])
    pack[columns:] = placed([(mixing[...], place_u)])
    chosen_at = as_columns(ocean_source)[:, 0:1]
    chosen = jnp.where(iota((columns, columns), 1).astype(jnp.float32) == chosen_at, 1.0, 0.0)
    currents[...] = jnp.zeros_like(currents)
    for b in range(NF // NFL):
        at_u = 2 * NFL * b
        currents[at_u : at_u + NFL, 0:NLEV] = cw[b * NFL : (b + 1) * NFL]
        currents[at_u + NFL : at_u + 2 * NFL] = pltpu.roll(currents[at_u : at_u + NFL], NLEV, 1)
    own_share = split_dot(pack[:columns], jnp.concatenate(halves(currents[...]), axis=0), 1)
    felt_parts = dot_on(chosen.astype(jnp.bfloat16), jnp.concatenate(halves(own_share), axis=1), 1, 0, None)
    felt = felt_parts[:, :LANES] + felt_parts[:, LANES:]
    lane_t = iota((tile_y, LANES), 1)
    row_lanes = 2 * NFL
    for b in range(NF // NFL):
        share = jnp.zeros((tile_y, LANES), jnp.float32)
        for r in range(tile_x):
            own_row = felt[r * tile_y : (r + 1) * tile_y]
            shift = (r - b) * row_lanes % LANES
            own_row = pltpu.roll(own_row, shift, 1) if shift else own_row
            share = jnp.where((lane_t >= r * row_lanes) & (lane_t < (r + 1) * row_lanes), own_row, share)
            wet_lane = lane_t == jnp.where(g == b, tile_x * row_lanes + r, LANES)
            share = jnp.where(wet_lane, wet_wide[r * tile_y : (r + 1) * tile_y], share)
        shares[b] = share
    field[0, my_rows] = masked[:, mine, :]
    with jax.named_scope("barrier"):
        pl.semaphore_wait(barrier, total)

    to_pair = [
        Move(
            masked.at[row, away, :],
            field.at[0, tile_x * y + row],
            sent_at(k),
            got_at(k),
            at(0, pair),
            True,
            True,
        )
        for k, row in ((1, y), (2, 1 - y))
    ]
    dz_first = 2 * y - 1
    reaches_back = jnp.where(y == 0, z < nz - 1, z > 0)

    def layer(k, source_ref, row, owner, device, cond):
        return Move(
            source_ref,
            halo_x.at[0, 1 - owner, row],
            sent_at(k),
            got_at(6 + 2 * (1 - owner) + row),
            device,
            cond,
            False,
        )

    straight = [
        layer(k, masked.at[row, mine, :], row, y, near(0, dz_first, y, 0), reaches) for k, row in ((10, y), (11, 1 - y))
    ]
    across = [
        layer(k, masked.at[row, away, :], row, y, near(0, dz_first, 1 - y, 0), reaches & jnp.logical_not(late))
        for k, row in ((12, y), (13, 1 - y))
    ]
    passed_on = [
        layer(k, field.at[0, tile_x * (1 - y) + row], row, 1 - y, near(0, -dz_first, y, 0), reaches_back & late)
        for k, row in ((12, 1 - y), (13, y))
    ]
    def strip_at(dz, strip):
        return near(0, dz, (strip + strip // 2) % 2, strip // 2 - gy)

    left_tile, right_tile = gy > 0, gy < ny - 1
    edges_first = [
        Move(
            edge_first.at[1 + flip],
            halo_first.at[flip, y],
            sent_at(14),
            got_at(12),
            at(0, pair),
            True,
            True,
        )
    ]
    after = 1 - y
    for k, (cond, strip, side) in enumerate(
        ((left_tile, 2 * gy - 1, 1), (True, 2 * gy + 1, 0), (True, 2 * gy, 1), (right_tile, 2 * gy + 2, 0))
    ):
        if cond is not True:
            edges_first.append(
                Move(
                    edge_first.at[k],
                    halo_first.at[side, y],
                    sent_at(15 + side),
                    got_at(10 + y),
                    strip_at(0, strip),
                    cond,
                    False,
                )
            )
        edges_first.append(
            Move(
                edge_first.at[k],
                halo_c.at[0, side, after],
                sent_at(17 + k),
                got_at((13 if cond is True else 15) + after),
                strip_at(dz_first, strip),
                reaches if cond is True else reaches & cond,
                False,
            )
        )
    halo_first[1 - flip, y] = edge_first[2 - flip]

    def wave_moves(s):
        moves = []
        sends_from, got_from = ((1, 21), (11, 6))[(s - 1) % 2]
        for near in (True, False):
            for side, dz in ((0, -1), (1, 1)):
                layer = 0 if near == (dz < 0) else 1
                moves.append(
                    Move(
                        field.at[s % 2, layer if dz < 0 else rows - 2 + layer],
                        halo_x.at[s, 1 - side, layer],
                        sent_at(sends_from + len(moves)),
                        got_at(got_from + len(moves)),
                        at(0, gx + 2 * dz),
                        inside(z, dz, nz),
                        inside(z, -dz, nz),
                    )
                )
        k = 4
        for side, dq in ((0, -1), (1, 1)):
            for dz in (-1, 0, 1):
                moves.append(
                    Move(
                        edge.at[s, side] if dz == 0 else corner.at[s, side, (1 + dz) // 2],
                        halo_y.at[s, 1 - side] if dz == 0 else halo_c.at[s, 1 - side, (1 - dz) // 2],
                        sent_at(sends_from + k),
                        got_at(got_from + k),
                        q_at(dz, dq),
                        both(dz, dq),
                        both(-dz, -dq),
                    )
                )
                k += 1
        return moves

    wider = half + 8

    def wide_strip(f):
        return pl.ds(pl.multiple_of((tile_y - wider) * f, 8), wider)

    share_moves = [
        Move(
            shares.at[(g + dg) % 2, wide_strip(f), :],
            share_in.at[g, y],
            sent_at(3 + k),
            got_at(3 + k),
            device,
            True,
            True,
        )
        for k, (dg, f, device) in enumerate(
            ((1, 1 - flip, at(1, pair)), (1, flip, at(1)), (0, 1 - flip, at(0, pair)))
        )
    ]
    for dg in (1, 0):
        for side, (cond, strip, block) in enumerate(
            ((left_tile, 2 * gy - 1, pl.ds(0, 8)), (right_tile, 2 * gy + 2, pl.ds(tile_y - 8, 8)))
        ):
            share_moves.append(
                Move(
                    shares.at[(g + dg) % 2, block, :],
                    seam_in.at[g, y],
                    sent_at(6 + 2 * dg + side),
                    got_at(17 + 2 * dg + y),
                    {**strip_at(0, strip), "grp": (g + dg) % 2},
                    cond,
                    False,
                )
            )
    for m in share_moves + to_pair + straight + edges_first + across:
        m.start()
    share_in[g, y] = shares[g, wide_strip(flip), :]
    to_grp = Move(pack, packs, sent_at(0), got_at(0), at(1), True, True)
    to_grp.start()

    def arrived(ref, sem, cond=True):
        Move(ref, ref, sem, sem, at(0, pair), False, cond).wait_recv()

    outer = jnp.where(flip == 0, left_tile, right_tile)
    above, below = z > 0, z < nz - 1

    def edges_arrived():
        edges_first[0].wait_recv()
        for yy in range(2):
            arrived(halo_first.at[flip, yy], got_at(10 + yy), outer)
        for i, cond in enumerate((above, below)):
            arrived(halo_c.at[0, 1 - flip, i], got_at(13 + i), cond)
            arrived(halo_c.at[0, flip, i], got_at(15 + i), cond & outer)

    def layers_arrived(first):
        for side, cond, layer in ((0, above, 1 if first else 0), (1, below, 0 if first else 1)):
            arrived(halo_x.at[0, side, layer], got_at(6 + 2 * side + layer), cond)

    def sea_moves(k, array):
        moves = []
        sends_from, got_from = ((21, 31), (1, 16))[k]
        for side, d in ((0, -1), (1, 1)):
            moves.append(
                Move(
                    array.at[0 if d < 0 else tile_x - 1],
                    row_halo.at[k, 1 - side],
                    sent_at(sends_from + side),
                    got_at(got_from + side),
                    at(0, gx + d),
                    inside(gx, d, nx),
                    inside(gx, -d, nx),
                )
            )
            moves.append(
                Move(
                    col_edge.at[k, side],
                    col_halo.at[k, 1 - side],
                    sent_at(sends_from + 2 + side),
                    got_at(got_from + 2 + side),
                    at(0, gx, gy + d),
                    inside(gy, d, ny),
                    inside(gy, -d, ny),
                )
            )
        return moves

    def set_col_edges(k, array):
        for side, column in ((0, 0), (1, tile_y - 1)):
            for r in range(tile_x):
                col_edge[k, side, r : r + 1, :] = array[r, column : column + 1, :]

    lane = iota((1, bins), 1)
    frequency = (g * NFL + (lane & (NFL - 1))).astype(jnp.float32)
    group_speed = 0.2 + 0.4 * (NF - 1 - frequency) / (NF - 1)
    turning = 0.5 * (frequency + 1.0) / NF
    cosine, sine = angles[0:1, :], angles[1:2, :]
    spread_f = g * NFL + (iota((NF, bins), 1) & (NFL - 1))
    spread = jnp.where(iota((NF, bins), 0) == spread_f, 1.0, 0.0)

    def repeated(values, start):
        place = iota(values.shape, 1)
        values = pltpu.roll(values, LANES - start, 1) if start else values
        width = NFL
        while width < LANES:
            values = jnp.where(place < width, values, pltpu.roll(values, width, 1))
            width *= 2
        return jnp.concatenate([values] * (-(-bins // LANES)), axis=1)[:, :bins]

    def set_edges(s, r, values):
        for side, first in ((0, 0), (1, half - 2)):
            pair_of = values[first : first + 2]
            edge[s, side, 2 * r : 2 * r + 2, :] = pair_of
            corner[s, side, r // 2, 2 * (r % 2) : 2 * (r % 2) + 2, :] = pair_of

    def interaction(s):
        now = field[s % 2].reshape(rows * half, bins).astype(jnp.bfloat16)
        product = jnp.dot(now, left[...], preferred_element_type=jnp.float32) * jnp.dot(
            now, right[...], preferred_element_type=jnp.float32
        )
        result = dot_on(product.astype(jnp.bfloat16), out_map[...], 1, 1, None)
        source[...] = (inter_step * result).reshape(source.shape)

    def finish(s, edges_in, layers_in, edge_of, written):
        with jax.named_scope("wait_edges"):
            edges_in()
        for side, speed, start in ((0, speed_l, 6), (1, speed_r, half + 8)):
            here = edge_of(side)
            before, after = (jnp.concatenate([halo_c[s, side, i]] * 2, axis=0) for i in range(2))
            low = iota((8, bins), 0)

            def joined(a, b, n):
                return jnp.where(low < n, pltpu.roll(a, n, 0), pltpu.roll(b, n, 0))

            packed = sweep(
                here,
                joined(before, here, 2),
                joined(before, here, 4),
                joined(here, after, 6),
                joined(here, after, 4),
                speed[...],
            )
            for r in range(rows):
                wide[r, start : start + 2, :] = packed[2 * r : 2 * r + 2]

        def line(r):
            if r < 0:
                return halo_x[s, 0, r + 2]
            if r >= rows:
                return halo_x[s, 1, r - rows]
            return field[s % 2, r]

        for r in [*range(1, rows - 1), 0, rows - 1]:
            if r < 2:
                with jax.named_scope("wait_layers"):
                    layers_in(r == 1)
            wide[r, 8 : 8 + half, :] = sweep(
                line(r), line(r - 1), line(r - 2), line(r + 1), line(r + 2), speed_x[r]
            )
            b = sweep(
                wide[r, 8 : 8 + half, :],
                wide[r, 7 : 7 + half, :],
                wide[r, 6 : 6 + half, :],
                wide[r, 9 : 9 + half, :],
                wide[r, 10 : 10 + half, :],
                speed_y[r],
            )
            t = turn[r]
            behind = jnp.concatenate([b[:, bins - NFL :], b[:, : bins - NFL]], axis=1)
            ahead = jnp.concatenate([b[:, NFL:], b[:, :NFL]], axis=1)
            c = b - jnp.abs(t) * (b - jnp.where(t >= 0.0, behind, ahead))
            wet_at = tile_x * row_lanes + r % tile_x
            values = flow[r, :, wet_at : wet_at + 1] * (c + source[r])
            field[(s + 1) % 2, r] = values
            if s + 1 < WAVE_SECTIONS:
                set_edges(s + 1, r, values)
            if r in (rows - 2, rows - 1):
                written(r == rows - 2)

    with jax.named_scope("flow_wait"):
        for m in share_moves[:3]:
            m.wait_recv()
        for dg in range(2):
            for yy in range(2):
                arrived(seam_in.at[(g + dg) % 2, yy], got_at(17 + 2 * dg + yy), outer)
    side_f = [[], []]
    low = iota((8, LANES), 0)
    for yy in range(2):
        felt_here = share_in[0, yy, pl.ds(pl.multiple_of(8 * flip, 8), half), :] + share_in[
            1, yy, pl.ds(pl.multiple_of(8 * flip, 8), half), :
        ]
        inner = pl.ds(pl.multiple_of(half * (1 - flip), 8), 8)
        inner_f = share_in[0, yy, inner, :] + share_in[1, yy, inner, :]
        seam_f = seam_in[0, yy] + seam_in[1, yy]
        for r in range(tile_x):
            row = tile_x * yy + r
            flow[row] = felt_here
            fx, fy = (repeated(felt_here, r * row_lanes + k * NFL) for k in (0, 1))
            speed_x[row] = group_speed * cosine + fx
            speed_y[row] = group_speed * sine + fy
            turn[row] = turning * (sine * fx - cosine * fy)
        side_f[0].append(jnp.where(flip == 0, seam_f, inner_f))
        side_f[1].append(jnp.where(flip == 0, inner_f, seam_f))
    for side, speed in ((0, speed_l), (1, speed_r)):
        packed_f = jnp.zeros((8, LANES), jnp.float32)
        for yy in range(2):
            for r in range(tile_x):
                at_row = 2 * (tile_x * yy + r)
                piece = side_f[side][yy]
                shift = (at_row - (6 if side == 0 else 0)) % 8
                piece = pltpu.roll(piece, shift, 0) if shift else piece
                piece = pltpu.roll(piece, LANES - r * row_lanes, 1) if r else piece
                packed_f = jnp.where((low >= at_row) & (low < at_row + 2), piece, packed_f)
        speed[...] = group_speed * cosine + repeated(packed_f, 0)
    column_n = iota((tile_y, LANES), 0)

    def neighbours(k, array):
        result = []
        for r in range(tile_x):
            a = array[r]
            below = array[r - 1] if r > 0 else row_halo[k, 0]
            above = array[r + 1] if r < tile_x - 1 else row_halo[k, 1]
            lower = jnp.where(column_n == 0, col_halo[k, 0, r : r + 1, :], pltpu.roll(a, 1, 0))
            upper = jnp.where(column_n == tile_y - 1, col_halo[k, 1, r : r + 1, :], pltpu.roll(a, tile_y - 1, 0))
            result.append(above + below + upper + lower - 4.0 * a)
        return jnp.concatenate(result, axis=0)

    def swapped(a):
        lane_n = iota(a.shape, 1)
        from_v = pltpu.roll(a, LANES - NLEV, 1)
        from_u = pltpu.roll(a, NLEV, 1)
        return jnp.where(lane_n < NLEV, from_v, jnp.where(lane_n < 2 * NLEV, -from_u, 0.0))

    def mixed(first):
        return first + split_dot(first, mix[...], 0)

    pick_rows = -(-own // 8) * 8

    def with_wet(a):
        return jnp.where(iota(a.shape, 1) == 2 * NLEV, wet_wide, a)

    sea_first = sea_moves(0, ocean)
    sea_second = sea_moves(1, ocean_next)

    def ocean_gather():
        to_grp.wait_send()
        to_grp.wait_recv()
        everything = pack[...] + packs[...]
        ocean[...] = with_wet(everything[:columns]).reshape(ocean.shape)
        levels = everything[columns:]
        mixer = jnp.concatenate(
            [levels, pltpu.roll(levels, NLEV, 1), jnp.zeros((LANES - 2 * NLEV, LANES), jnp.float32)], axis=0
        )
        mix[...] = jnp.concatenate(halves(mixer), axis=1)
        i, j = iota((LANES, 2 * pick_rows), 0), iota((LANES, 2 * pick_rows), 1)
        level = j % pick_rows
        pick = jnp.where((level < own) & (i == level + own * g + NLEV * (j // pick_rows)), 1.0, 0.0)
        last_mix = pick + exact_dot(mixer, pick)
        high, low = halves(last_mix)
        finals[0] = jnp.concatenate([pick.astype(jnp.bfloat16)] * 2 + [jnp.zeros_like(high)], axis=0)
        finals[1] = jnp.concatenate([high, high, low], axis=0)
        set_col_edges(0, ocean)
        for m in sea_first:
            m.start()

    def ocean_prepare():
        for m in sea_first:
            m.wait_recv()
        flat = ocean[...].reshape(columns, LANES)
        plain = flat + ocean_step * (coriolis * swapped(flat) + viscosity * neighbours(0, ocean))
        ocean_next[...] = with_wet(plain).reshape(ocean.shape)
        set_col_edges(1, ocean_next)
        for m in sea_second:
            m.start()
        for m in sea_first:
            m.wait_send()

    def wave_profile():
        depth = dot_on(dw[...], spread, 0, 0)
        rest = jnp.zeros((LANES - 2 * NLEV, bins), jnp.float32)
        high, low = halves(jnp.concatenate([depth * cosine, depth * sine, rest], axis=0))
        profile[...] = jnp.concatenate([high, low], axis=0)

    all_moves = [None] + [wave_moves(s) for s in range(1, WAVE_SECTIONS)]

    def next_written(s):
        def written(interior):
            moves = all_moves[s]
            if interior:

                @pl.when(late)
                def _():
                    for m in moves[2:4]:
                        m.start()

            else:
                for m in moves[4:]:
                    m.start()
                for m in moves[:2]:
                    m.start()

                @pl.when(jnp.logical_not(late))
                def _():
                    for m in moves[2:4]:
                        m.start()

        return written

    their = tile_x * (1 - y)
    back = [
        Move(
            field.at[WAVE_SECTIONS % 2, their + row],
            spec_out.at[row, mine, :],
            sent_at(21 + k),
            got_at(21 + k),
            at(0, pair),
            True,
            True,
        )
        for k, row in enumerate((y, 1 - y))
    ]

    def last_written(interior):
        if interior:
            back[0].start()

    with jax.named_scope("pair"):
        for m, onward in zip(to_pair, passed_on):
            m.wait_recv()
            onward.start()
    with jax.named_scope("load_rest"):
        for load in loads[8:]:
            load.wait()
    with jax.named_scope("inter"):
        interaction(0)
    with jax.named_scope("wait_send"):
        for m in to_pair + share_moves + straight + edges_first:
            m.wait_send()
    finish(
        0,
        edges_arrived,
        layers_arrived,
        lambda side: jnp.concatenate([halo_first[side, 0], halo_first[side, 1]], axis=0),
        next_written(1),
    )

    def section(s, meanwhile):
        moves = all_moves[s]
        with jax.named_scope("inter"):
            interaction(s)


        with jax.named_scope("wait_send"):
            for m in all_moves[s - 1] if s > 1 else passed_on + across:
                m.wait_send()
        for work in meanwhile:
            work()

        def edges_in():
            for m in moves[4:]:
                m.wait_recv()

        def layers_in(first):
            for m in moves[0:2] if first else moves[2:4]:
                m.wait_recv()

        written = next_written(s + 1) if s + 1 < WAVE_SECTIONS else last_written
        finish(s, edges_in, layers_in, lambda side: halo_y[s, side], written)

    for s in range(1, WAVE_SECTIONS):
        section(s, {1: (ocean_gather, wave_profile), 2: (ocean_prepare,)}.get(s, ()))

    last = field.at[WAVE_SECTIONS % 2]
    drift = split_dot(last[...].reshape(rows * half, bins), profile[...], 1)
    drift_q[...] = drift.reshape(drift_q.shape)
    drift_moves = [
        Move(
            drift_q.at[pl.ds((tile_x - 1) * yy, tile_x + 1)],
            drift_n.at[g, pl.ds(1 - yy, tile_x + 1), mine, :],
            sent_at(5 + k),
            got_at(got),
            device,
            True,
            True,
        )
        for k, (got, yy, device) in enumerate(((35, 1 - y, at(1, pair)), (23, 1 - y, at(0, pair)), (36, y, at(1))))
    ]
    to_side = 1 - 2 * flip
    for dg in (1, 0):
        for side, (row, at_row, device, cond) in enumerate(
            ((0, tile_x + 1, near(dg, -1, 1, 0), above), (rows - 1, 0, near(dg, 1, 0, 0), below))
        ):
            drift_moves.append(
                Move(
                    drift_q.at[row],
                    drift_n.at[g, at_row, mine, :],
                    sent_at((8, 9, 10, 23)[2 * dg + side]),
                    got_at((24, 37)[dg] + y),
                    device,
                    cond,
                    False,
                )
            )
        for yy in range(2):
            drift_moves.append(
                Move(
                    drift_q.at[pl.ds(tile_x * yy, tile_x), pl.ds(pl.multiple_of((half - 8) * flip, 8), 8), :],
                    drift_c.at[g, 1 - flip],
                    sent_at((24, 0, 25, 26)[2 * dg + yy]),
                    got_at((1, 39)[dg] + 1 - flip),
                    near(dg, 0, yy, -to_side),
                    outer,
                    False,
                )
            )
    for m in drift_moves:
        m.start()
    back[1].start()
    spec_out[:, mine, :] = last[my_rows]
    drift_n[g, pl.ds(1 - y, tile_x + 1), mine, :] = drift_q[pl.ds((tile_x - 1) * y, tile_x + 1)]
    with jax.named_scope("sea_second"):
        for m in sea_second:
            m.wait_recv()
    plain = jnp.concatenate(
        [row_halo[1, 0]] + [ocean_next[r] for r in range(tile_x)] + [row_halo[1, 1], col_halo[1, 0], col_halo[1, 1]], axis=0
    )
    plain_mixed = mixed(plain)
    with jax.named_scope("drift_wait"):
        for m in drift_moves[:3]:
            m.wait_recv()
        for dg in range(2):
            for yy in range(2):
                strip_cols = pl.ds(pl.multiple_of(half * ((yy + gy) % 2), 8), half)
                arrived(
                    drift_n.at[(g + dg) % 2, (tile_x + 1) * y, strip_cols, :], got_at((24, 37)[dg] + yy), reaches
                )
            for side, cond in enumerate((left_tile, right_tile)):
                arrived(drift_c.at[(g + dg) % 2, side], got_at((1, 39)[dg] + side), cond)
    drift_rows = (drift_n[0] + drift_n[1]).reshape((tile_x + 2) * tile_y, LANES)
    low_n = iota((8, LANES), 0)
    parts, drifts = [], [drift_rows]
    for side in range(2):
        beside = drift_c[0, side] + drift_c[1, side]
        packed = jnp.zeros((8, LANES), jnp.float32)
        for r in range(tile_x):
            shift = (r + 1) % 8 if side == 0 else r
            piece = pltpu.roll(beside[r], shift, 0) if shift else beside[r]
            packed = jnp.where(low_n == r, piece, packed)
        drifts.append(packed)
    pulled = ocean_step * coriolis * swapped(jnp.concatenate(drifts, axis=0))
    after_one = plain[:, 2 * NLEV : 2 * NLEV + 1] * (plain_mixed + mixed(pulled))
    sea = (tile_x + 2) * tile_y
    row_halo[0, 0] = after_one[:tile_y]
    flat = after_one[tile_y : sea - tile_y]
    ocean[...] = flat.reshape(ocean.shape)
    row_halo[0, 1] = after_one[sea - tile_y : sea]
    col_halo[0, 0] = after_one[sea : sea + 8]
    col_halo[0, 1] = after_one[sea + 8 :]
    drift_all = drift_rows[tile_y : sea - tile_y]

    def give(out_u, out_v, which, values, wet):
        for r in range(tile_x):
            high, low = halves(values[r * tile_y : (r + 1) * tile_y])
            result = dot_on(finals[which], jnp.concatenate([high, low, high], axis=1), 0, 1, None)
            if wet:
                result = result * wet_mask[r : r + 1, :].astype(jnp.float32)
            out_u[:, r, :] = result[:own]
            out_v[:, r, :] = result[pick_rows : pick_rows + own]

    second = flat + ocean_step * (coriolis * swapped(flat + drift_all) + viscosity * neighbours(0, ocean))
    give(u_out, v_out, 1, second, True)
    give(du_out, dv_out, 0, drift_all, False)
    with jax.named_scope("back"):
        for m in back:
            m.wait_recv()
    for m in back + all_moves[-1] + drift_moves + sea_second:
        m.wait_send()


def store_kernel(*refs):
    count = (len(refs) - 1) // 2
    copies = [pltpu.make_async_copy(refs[i], refs[count + i], refs[-1].at[i]) for i in range(count)]
    for copy in copies:
        copy.start()
    for copy in copies:
        copy.wait()


def solution(mesh):
    sizes = (mesh.shape["gx"], mesh.shape["gy"])
    theta = 2.0 * np.pi * np.arange(ND) / ND
    table = np.zeros((8, ND * NFL), np.float32)
    table[0] = np.repeat(np.cos(theta), NFL)
    table[1] = np.repeat(np.sin(theta), NFL)

    def body(spectrum, wet_mask, ocean_source, ocean_u, ocean_v, current_weights, drift_weights, inter_left, inter_right, inter_out, mixing):
        tile_x, tile_y, bins = spectrum.shape
        half, rows = tile_y // 2, 2 * tile_x
        own = ocean_u.shape[2]
        columns = tile_x * tile_y
        f32 = jnp.float32
        vmem = pl.BlockSpec(memory_space=pltpu.VMEM)
        sea = (tile_x, tile_y, LANES)
        sections = WAVE_SECTIONS
        wave = (rows, half, bins)

        def V(*shape):
            return pltpu.VMEM(shape, f32)

        def D(*shape):
            return pltpu.SemaphoreType.DMA(shape)

        outs = (jax.ShapeDtypeStruct(spectrum.shape, f32),) + (
            jax.ShapeDtypeStruct((own, tile_x, tile_y), f32),
        ) * 4
        anywhere = pl.BlockSpec(memory_space=pl.ANY)
        results = pl.pallas_call(
            functools.partial(kernel, sizes),
            out_shape=tuple(pltpu.VMEM(a.shape, a.dtype) for a in outs),
            in_specs=[anywhere] * 12,
            out_specs=(vmem,) * 5,
            scratch_shapes=[
                V(tile_x, tile_y, bins),
                pltpu.VMEM(wet_mask.shape, wet_mask.dtype),
                pltpu.VMEM(ocean_source.shape, ocean_source.dtype),
                V(own, tile_x, tile_y),
                V(own, tile_x, tile_y),
                V(*table.shape),
                V(*current_weights.shape[::-1]),
                V(*drift_weights.shape[::-1]),
                pltpu.VMEM(inter_left.shape, inter_left.dtype),
                pltpu.VMEM(inter_right.shape, inter_right.dtype),
                pltpu.VMEM(inter_out.shape[::-1], inter_out.dtype),
                V(*mixing.shape[::-1]),
                D(12),
                V(columns + NLEV, LANES),
                V(LANES, LANES),
                pltpu.VMEM((2 * LANES, bins), jnp.bfloat16),
                V(tile_x, tile_y, bins),
                V(columns + NLEV, LANES),
                V(2, tile_y, LANES),
                V(2, 2, half + 8, LANES),
                V(2, 2, 8, LANES),
                V(rows, half, LANES),
                V(4, 2 * tile_x, bins),
                V(2, 2, 2 * tile_x, bins),
                V(2, *wave),
                V(sections, 2, 8, bins),
                V(sections, 2, 2, half, bins),
                V(sections, 2, 8, bins),
                V(sections, 2, 2, 4, bins),
                V(sections, 2, 2, 4, bins),
                V(*wave),
                V(*wave),
                V(*wave),
                V(8, bins),
                V(8, bins),
                V(rows, half + 16, bins),
                V(*wave),
                pltpu.VMEM((LANES, 2 * LANES), jnp.bfloat16),
                pltpu.VMEM((2, 3 * LANES, -(-own // 8) * 16), jnp.bfloat16),
                V(*sea),
                V(*sea),
                V(2, 2, tile_y, LANES),
                V(2, 2, 8, LANES),
                V(2, 2, 8, LANES),
                V(rows, half, LANES),
                V(2, tile_x + 2, tile_y, LANES),
                V(2, 2, tile_x, 8, LANES),
                D(SENDS - 8),
                D(RECEIVES),
            ],
            compiler_params=pltpu.CompilerParams(collective_id=0, has_side_effects=True),
        )(
            spectrum,
            wet_mask,
            ocean_source,
            jnp.transpose(ocean_u, (2, 0, 1)),
            jnp.transpose(ocean_v, (2, 0, 1)),
            jnp.asarray(table),
            current_weights.T,
            drift_weights.T,
            inter_left,
            inter_right,
            inter_out.T,
            mixing.T,
        )
        results = pl.pallas_call(
            store_kernel,
            out_shape=outs,
            in_specs=[anywhere] * 5,
            out_specs=(anywhere,) * 5,
            scratch_shapes=[D(5)],
        )(*(pltpu.with_memory_space_constraint(a, pltpu.VMEM) for a in results))
        return (results[0],) + tuple(jnp.transpose(a, (1, 2, 0)) for a in results[1:])

    tile = P("gx", "gy", "grp")
    in_specs = (
        tile,
        P("gx", "gy"),
        P("gx", "gy"),
        tile,
        tile,
        P(),
        P(),
        P("grp", None),
        P("grp", None),
        P(None, "grp"),
        P(None, "grp"),
    )
    return jax.shard_map(body, mesh=mesh, in_specs=in_specs, out_specs=(tile,) * 5, check_vma=False)
```

```python
import functools

import jax
import jax.numpy as jnp
import numpy as np
from jax import lax
from jax.experimental import pallas as pl
from jax.experimental.pallas import tpu as pltpu
from jax.sharding import PartitionSpec as P

NF = 32
ND = 36
NLEV = 40
WAVE_SECTIONS = 3
NFL = 16
LANES = 128
SENDS, RECEIVES = 25, 41
MESH = pl.DeviceIdType.MESH

highest = lax.Precision.HIGHEST
inter_step = 0.1
ocean_step = 0.4
coriolis = 0.5
viscosity = 0.1


def exact_dot(a, b):
    return jnp.dot(a, b, precision=highest, preferred_element_type=jnp.float32)


def dot_on(a, b, dim_a, dim_b, precision=highest):
    return lax.dot_general(
        a, b, (((dim_a,), (dim_b,)), ((), ())), precision=precision, preferred_element_type=jnp.float32
    )


def halves(a):
    high = a.astype(jnp.bfloat16)
    return high, (a - high.astype(jnp.float32)).astype(jnp.bfloat16)


def split_dot(a, both, dim):
    high, low = halves(a)
    result = dot_on(high, both, 1, dim, None) + dot_on(low, both, 1, dim, None)
    half = result.shape[1] // 2
    return result[:, :half] + result[:, half:]


def sweep(centre, back_one, back_two, next_one, next_two, velocity, rest):
    up = velocity >= 0.0
    one = jnp.where(up, back_one, next_one)
    two = jnp.where(up, back_two, next_two)
    step = centre - one
    return centre - jnp.abs(velocity) * (step + rest * (step - (one - two)))


def rest_of(velocity):
    return 0.5 - 0.5 * jnp.abs(velocity)


def iota(shape, dim):
    return lax.broadcasted_iota(jnp.int32, shape, dim)


class Move:
    def __init__(self, src, dst, send, recv, device, sends, receives):
        self.copy = pltpu.make_async_remote_copy(
            src_ref=src, dst_ref=dst, send_sem=send, recv_sem=recv, device_id=device, device_id_type=MESH
        )
        self.sends, self.receives = sends, receives

    def when(self, cond, act):
        if cond is True:
            act()
        elif cond is not False:
            pl.when(cond)(act)

    def start(self):
        self.when(self.sends, self.copy.start)

    def wait_send(self):
        self.when(self.sends, self.copy.wait_send)

    def wait_recv(self):
        self.when(self.receives, self.copy.wait_recv)


def kernel(
    sizes,
    spectrum_hbm,
    wet_mask_hbm,
    ocean_source_hbm,
    ocean_u_hbm,
    ocean_v_hbm,
    angles_hbm,
    cw_hbm,
    dw_hbm,
    left_hbm,
    right_hbm,
    out_hbm,
    mixing_hbm,
    spec_out,
    u_out,
    v_out,
    du_out,
    dv_out,
    spectrum,
    wet_mask,
    ocean_source,
    ocean_u,
    ocean_v,
    angles,
    cw,
    dw,
    left,
    right,
    out_map,
    mixing,
    load_sem,
    pack,
    currents,
    profile,
    masked,
    packs,
    shares,
    share_in,
    seam_in,
    flow,
    edge_first,
    halo_first,
    field,
    edge,
    halo_x,
    halo_y,
    corner,
    halo_c,
    speed_x,
    speed_y,
    rest_x,
    rest_y,
    turn,
    speed_l,
    speed_r,
    wide,
    source,
    mix,
    finals,
    ocean,
    ocean_next,
    row_halo,
    col_edge,
    col_halo,
    drift_q,
    drift_p,
    drift_s,
    drift_n,
    drift_z,
    drift_c,
    send_sem,
    recv_sem,
):
    nx, ny = sizes

    def sent_at(k):
        if k < 8:
            return load_sem.at[k]
        return send_sem.at[k - 8] if k < SENDS else load_sem.at[8 + k - SENDS]

    def got_at(k):
        return recv_sem.at[k]

    loads = [
        pltpu.make_async_copy(src, dst, load_sem.at[k])
        for k, (src, dst) in enumerate(
            (
                (spectrum_hbm, spectrum),
                (wet_mask_hbm, wet_mask),
                (ocean_source_hbm, ocean_source),
                (ocean_u_hbm, ocean_u),
                (ocean_v_hbm, ocean_v),
                (cw_hbm, cw),
                (mixing_hbm, mixing),
                (angles_hbm, angles),
                (dw_hbm, dw),
                (left_hbm, left),
                (right_hbm, right),
                (out_hbm, out_map),
            )
        )
    ]
    for load in loads[:2]:
        load.start()
    tile_x, tile_y, bins = spectrum.shape
    half = tile_y // 2
    own = u_out.shape[0]
    rows = 2 * tile_x
    g, gx, gy = lax.axis_index("grp"), lax.axis_index("gx"), lax.axis_index("gy")
    z, y = gx // 2, gx % 2
    flip = (y + gy) % 2
    q = 2 * gy + flip
    late = gy % 2 == 1
    nz, nq = nx // 2, 2 * ny

    def at(dg=0, x=gx, c=gy):
        return {"grp": (g + dg) % 2, "gx": x, "gy": c}

    pair = 2 * z + 1 - y

    def q_at(dz, dq):
        qq = q + dq
        return at(0, 2 * (z + dz) + (qq + qq // 2) % 2, qq // 2)

    def inside(value, step, limit):
        return value + step >= 0 if step < 0 else value + step < limit

    def both(dz, dq):
        cond = inside(q, dq, nq)
        return cond if dz == 0 else cond & inside(z, dz, nz)

    def near(dg, dz, yy, dc):
        return {"grp": (g + dg) % 2, "gx": 2 * (z + dz) + yy, "gy": gy + dc}

    barrier = pltpu.get_barrier_semaphore()
    total = 0
    for dz in (-1, 0, 1):
        for dc in (-1, 0, 1):
            friends = [at(1), at(0, pair), at(1, pair)]
            if dz or dc:
                groups = (0,) if dz and dc else (0, 1)
                friends = [near(dg, dz, yy, dc) for dg in groups for yy in (0, 1)]
            cond = inside(z, dz, nz) & inside(gy, dc, ny)

            @pl.when(cond)
            def _():
                for device in friends:
                    pl.semaphore_signal(barrier, inc=1, device_id=device, device_id_type=MESH)

            total = total + jnp.where(cond, len(friends), 0)

    for load in loads[2:]:
        load.start()
    columns = tile_x * tile_y

    def as_columns(table):
        ones = jnp.ones((1, LANES), jnp.float32)
        values = table[...].astype(jnp.float32)
        exact = None if columns <= 256 else highest
        return jnp.concatenate([dot_on(values[r : r + 1], ones, 0, 0, exact) for r in range(tile_x)], axis=0)

    loads[1].wait()
    wet_wide = as_columns(wet_mask)
    wet_n = wet_wide[:, 0:1]

    away = pl.ds(pl.multiple_of(half * (1 - flip), 8), half)
    mine = pl.ds(pl.multiple_of(half * flip, 8), half)
    my_rows = pl.ds(tile_x * y, tile_x)

    reaches = jnp.where(y == 0, z > 0, z < nz - 1)

    @pl.when(jnp.logical_not(reaches))
    def _():
        drift_z[...] = jnp.zeros_like(drift_z)

    @pl.when(z == 0)
    def _():
        halo_x[:, 0] = jnp.zeros_like(halo_x[:, 0])

    @pl.when(z == nz - 1)
    def _():
        halo_x[:, 1] = jnp.zeros_like(halo_x[:, 1])

    for side, dq in ((0, -1), (1, 1)):

        @pl.when(jnp.logical_not(inside(q, dq, nq)))
        def _():
            halo_y[:, side] = jnp.zeros_like(halo_y[:, side])
            halo_c[:, side] = jnp.zeros_like(halo_c[:, side])
            halo_first[side] = jnp.zeros_like(halo_first[side])
            seam_in[...] = jnp.zeros_like(seam_in)

        for slot, dz in ((0, -1), (1, 1)):

            @pl.when(inside(q, dq, nq) & jnp.logical_not(inside(z, dz, nz)))
            def _():
                halo_c[:, side, slot] = jnp.zeros_like(halo_c[:, side, slot])

    for side, d in ((0, -1), (1, 1)):

        @pl.when(jnp.logical_not(inside(gx, d, nx)))
        def _():
            row_halo[:, side] = jnp.zeros_like(row_halo[:, side])

        @pl.when(jnp.logical_not(inside(gy, d, ny)))
        def _():
            col_halo[:, side] = jnp.zeros_like(col_halo[:, side])
            drift_c[:, side] = jnp.zeros_like(drift_c[:, side])

    loads[0].wait()
    masked[...] = (spectrum[...].reshape(columns, bins) * wet_n).reshape(tile_x, tile_y, bins)

    for k, first in enumerate((0, half - 2, half, tile_y - 2)):
        for r in range(tile_x):
            edge_first[k, 2 * r : 2 * r + 2, :] = masked[r, first : first + 2, :]

    for load in loads[2:8]:
        load.wait()
    place_i, place_j = iota((own, LANES), 0), iota((own, LANES), 1)
    place_u = jnp.where(place_j == place_i + own * g, 1.0, 0.0)
    place_v = jnp.where(place_j == place_i + own * g + NLEV, 1.0, 0.0)

    def placed(pieces):
        values = jnp.concatenate([part.astype(jnp.float32) for a, _ in pieces for part in halves(a)], axis=0)
        places = jnp.concatenate([p for _, p in pieces for _ in range(2)], axis=0)
        return dot_on(values.astype(jnp.bfloat16), places.astype(jnp.bfloat16), 0, 0, None)

    for r in range(tile_x):
        pack[r * tile_y : (r + 1) * tile_y] = placed([(ocean_u[:, r, :], place_u), (ocean_v[:, r, :], place_v)])
    pack[columns:] = placed([(mixing[...], place_u)])
    chosen_at = as_columns(ocean_source)[:, 0:1]
    chosen = jnp.where(iota((columns, columns), 1).astype(jnp.float32) == chosen_at, 1.0, 0.0)
    currents[...] = jnp.zeros_like(currents)
    for b in range(NF // NFL):
        at_u = 2 * NFL * b
        currents[at_u : at_u + NFL, 0:NLEV] = cw[b * NFL : (b + 1) * NFL]
        currents[at_u + NFL : at_u + 2 * NFL] = pltpu.roll(currents[at_u : at_u + NFL], NLEV, 1)
    own_share = split_dot(pack[:columns], jnp.concatenate(halves(currents[...]), axis=0), 1)
    felt_parts = dot_on(chosen.astype(jnp.bfloat16), jnp.concatenate(halves(own_share), axis=1), 1, 0, None)
    felt = felt_parts[:, :LANES] + felt_parts[:, LANES:]
    lane_t = iota((tile_y, LANES), 1)
    row_lanes = 2 * NFL
    for b in range(NF // NFL):
        share = jnp.zeros((tile_y, LANES), jnp.float32)
        for r in range(tile_x):
            own_row = felt[r * tile_y : (r + 1) * tile_y]
            shift = (r - b) * row_lanes % LANES
            own_row = pltpu.roll(own_row, shift, 1) if shift else own_row
            share = jnp.where((lane_t >= r * row_lanes) & (lane_t < (r + 1) * row_lanes), own_row, share)
            wet_lane = lane_t == jnp.where(g == b, tile_x * row_lanes + r, LANES)
            share = jnp.where(wet_lane, wet_wide[r * tile_y : (r + 1) * tile_y], share)
        shares[b] = share
    field[0, my_rows] = masked[:, mine, :]
    with jax.named_scope("barrier"):
        pl.semaphore_wait(barrier, total)

    to_pair = [
        Move(
            masked.at[row, away, :],
            field.at[0, tile_x * y + row],
            sent_at(k),
            got_at(k),
            at(0, pair),
            True,
            True,
        )
        for k, row in ((1, y), (2, 1 - y))
    ]
    dz_first = 2 * y - 1
    reaches_back = jnp.where(y == 0, z < nz - 1, z > 0)

    def layer(k, source_ref, row, owner, device, cond):
        return Move(
            source_ref,
            halo_x.at[0, 1 - owner, row],
            sent_at(k),
            got_at(6 + 2 * (1 - owner) + row),
            device,
            cond,
            False,
        )

    straight = [
        layer(k, masked.at[row, mine, :], row, y, near(0, dz_first, y, 0), reaches) for k, row in ((10, y), (11, 1 - y))
    ]
    across = [
        layer(k, masked.at[row, away, :], row, y, near(0, dz_first, 1 - y, 0), reaches & jnp.logical_not(late))
        for k, row in ((12, y), (13, 1 - y))
    ]
    passed_on = [
        layer(k, field.at[0, tile_x * (1 - y) + row], row, 1 - y, near(0, -dz_first, y, 0), reaches_back & late)
        for k, row in ((12, 1 - y), (13, y))
    ]
    def strip_at(dz, strip):
        return near(0, dz, (strip + strip // 2) % 2, strip // 2 - gy)

    left_tile, right_tile = gy > 0, gy < ny - 1
    edges_first = [
        Move(
            edge_first.at[1 + flip],
            halo_first.at[flip, y],
            sent_at(14),
            got_at(12),
            at(0, pair),
            True,
            True,
        )
    ]
    after = 1 - y
    for k, (cond, strip, side) in enumerate(
        ((left_tile, 2 * gy - 1, 1), (True, 2 * gy + 1, 0), (True, 2 * gy, 1), (right_tile, 2 * gy + 2, 0))
    ):
        if cond is not True:
            edges_first.append(
                Move(
                    edge_first.at[k],
                    halo_first.at[side, y],
                    sent_at(15 + side),
                    got_at(10 + y),
                    strip_at(0, strip),
                    cond,
                    False,
                )
            )
        edges_first.append(
            Move(
                edge_first.at[k],
                halo_c.at[0, side, after],
                sent_at(17 + k),
                got_at((13 if cond is True else 15) + after),
                strip_at(dz_first, strip),
                reaches if cond is True else reaches & cond,
                False,
            )
        )
    halo_first[1 - flip, y] = edge_first[2 - flip]

    def wave_moves(s):
        moves = []
        sends_from, got_from = ((1, 21), (11, 6))[(s - 1) % 2]
        for near in (True, False):
            for side, dz in ((0, -1), (1, 1)):
                layer = 0 if near == (dz < 0) else 1
                moves.append(
                    Move(
                        field.at[s % 2, layer if dz < 0 else rows - 2 + layer],
                        halo_x.at[s, 1 - side, layer],
                        sent_at(sends_from + len(moves)),
                        got_at(got_from + len(moves)),
                        at(0, gx + 2 * dz),
                        inside(z, dz, nz),
                        inside(z, -dz, nz),
                    )
                )
        k = 4
        for side, dq in ((0, -1), (1, 1)):
            for dz in (-1, 0, 1):
                moves.append(
                    Move(
                        edge.at[s, side] if dz == 0 else corner.at[s, side, (1 + dz) // 2],
                        halo_y.at[s, 1 - side] if dz == 0 else halo_c.at[s, 1 - side, (1 - dz) // 2],
                        sent_at(sends_from + k),
                        got_at(got_from + k),
                        q_at(dz, dq),
                        both(dz, dq),
                        both(-dz, -dq),
                    )
                )
                k += 1
        return moves

    wider = half + 8

    def wide_strip(f):
        return pl.ds(pl.multiple_of((tile_y - wider) * f, 8), wider)

    share_moves = [
        Move(
            shares.at[(g + dg) % 2, wide_strip(f), :],
            share_in.at[g, y],
            sent_at(3 + k),
            got_at(3 + k),
            device,
            True,
            True,
        )
        for k, (dg, f, device) in enumerate(
            ((1, 1 - flip, at(1, pair)), (1, flip, at(1)), (0, 1 - flip, at(0, pair)))
        )
    ]
    for dg in (1, 0):
        for side, (cond, strip, block) in enumerate(
            ((left_tile, 2 * gy - 1, pl.ds(0, 8)), (right_tile, 2 * gy + 2, pl.ds(tile_y - 8, 8)))
        ):
            share_moves.append(
                Move(
                    shares.at[(g + dg) % 2, block, :],
                    seam_in.at[g, y],
                    sent_at(6 + 2 * dg + side),
                    got_at(17 + 2 * dg + y),
                    {**strip_at(0, strip), "grp": (g + dg) % 2},
                    cond,
                    False,
                )
            )
    for m in share_moves + to_pair + straight + edges_first:
        m.start()
    share_in[g, y] = shares[g, wide_strip(flip), :]
    to_grp = Move(pack, packs, sent_at(0), got_at(0), at(1), True, True)
    to_grp.start()

    def arrived(ref, sem, cond=True):
        Move(ref, ref, sem, sem, at(0, pair), False, cond).wait_recv()

    outer = jnp.where(flip == 0, left_tile, right_tile)
    above, below = z > 0, z < nz - 1

    def edges_arrived():
        edges_first[0].wait_recv()
        for yy in range(2):
            arrived(halo_first.at[flip, yy], got_at(10 + yy), outer)
        for i, cond in enumerate((above, below)):
            arrived(halo_c.at[0, 1 - flip, i], got_at(13 + i), cond)
            arrived(halo_c.at[0, flip, i], got_at(15 + i), cond & outer)

    def layers_arrived(first):
        for side, cond, layer in ((0, above, 1 if first else 0), (1, below, 0 if first else 1)):
            arrived(halo_x.at[0, side, layer], got_at(6 + 2 * side + layer), cond)

    def sea_moves(k, array):
        moves = []
        sends_from, got_from = ((21, 31), (1, 16))[k]
        for side, d in ((0, -1), (1, 1)):
            moves.append(
                Move(
                    array.at[0 if d < 0 else tile_x - 1],
                    row_halo.at[k, 1 - side],
                    sent_at(sends_from + side),
                    got_at(got_from + side),
                    at(0, gx + d),
                    inside(gx, d, nx),
                    inside(gx, -d, nx),
                )
            )
            moves.append(
                Move(
                    col_edge.at[k, side],
                    col_halo.at[k, 1 - side],
                    sent_at(sends_from + 2 + side),
                    got_at(got_from + 2 + side),
                    at(0, gx, gy + d),
                    inside(gy, d, ny),
                    inside(gy, -d, ny),
                )
            )
        return moves

    def set_col_edges(k, array):
        for side, column in ((0, 0), (1, tile_y - 1)):
            for r in range(tile_x):
                col_edge[k, side, r : r + 1, :] = array[r, column : column + 1, :]

    lane = iota((1, bins), 1)
    frequency = (g * NFL + (lane & (NFL - 1))).astype(jnp.float32)
    group_speed = 0.2 + 0.4 * (NF - 1 - frequency) / (NF - 1)
    turning = 0.5 * (frequency + 1.0) / NF
    cosine, sine = angles[0:1, :], angles[1:2, :]
    spread_f = g * NFL + (iota((NF, bins), 1) & (NFL - 1))
    spread = jnp.where(iota((NF, bins), 0) == spread_f, 1.0, 0.0)

    def repeated(values, start):
        place = iota(values.shape, 1)
        values = pltpu.roll(values, LANES - start, 1) if start else values
        width = NFL
        while width < LANES:
            values = jnp.where(place < width, values, pltpu.roll(values, width, 1))
            width *= 2
        return jnp.concatenate([values] * (-(-bins // LANES)), axis=1)[:, :bins]

    def set_edges(s, r, values):
        for side, first in ((0, 0), (1, half - 2)):
            pair_of = values[first : first + 2]
            edge[s, side, 2 * r : 2 * r + 2, :] = pair_of
            corner[s, side, r // 2, 2 * (r % 2) : 2 * (r % 2) + 2, :] = pair_of

    def interaction(s):
        now = field[s % 2].reshape(rows * half, bins).astype(jnp.bfloat16)
        product = jnp.dot(now, left[...], preferred_element_type=jnp.float32) * jnp.dot(
            now, right[...], preferred_element_type=jnp.float32
        )
        result = dot_on(product.astype(jnp.bfloat16), out_map[...], 1, 1, None)
        source[...] = (inter_step * result).reshape(source.shape)

    def finish(s, edges_in, layers_in, edge_of, written):
        with jax.named_scope("wait_edges"):
            edges_in()
        for side, speed, start in ((0, speed_l, 6), (1, speed_r, half + 8)):
            here = edge_of(side)
            before, after = (jnp.concatenate([halo_c[s, side, i]] * 2, axis=0) for i in range(2))
            low = iota((8, bins), 0)

            def joined(a, b, n):
                return jnp.where(low < n, pltpu.roll(a, n, 0), pltpu.roll(b, n, 0))

            packed = sweep(
                here,
                joined(before, here, 2),
                joined(before, here, 4),
                joined(here, after, 6),
                joined(here, after, 4),
                speed[...],
                rest_of(speed[...]),
            )
            for r in range(rows):
                wide[r, start : start + 2, :] = packed[2 * r : 2 * r + 2]

        def line(r):
            if r < 0:
                return halo_x[s, 0, r + 2]
            if r >= rows:
                return halo_x[s, 1, r - rows]
            return field[s % 2, r]

        for r in [*range(1, rows - 1), 0, rows - 1]:
            if r < 2:
                with jax.named_scope("wait_layers"):
                    layers_in(r == 1)
            wide[r, 8 : 8 + half, :] = sweep(
                line(r), line(r - 1), line(r - 2), line(r + 1), line(r + 2), speed_x[r], rest_x[r]
            )
            b = sweep(
                wide[r, 8 : 8 + half, :],
                wide[r, 7 : 7 + half, :],
                wide[r, 6 : 6 + half, :],
                wide[r, 9 : 9 + half, :],
                wide[r, 10 : 10 + half, :],
                speed_y[r],
                rest_y[r],
            )
            t = turn[r]
            behind = jnp.concatenate([b[:, bins - NFL :], b[:, : bins - NFL]], axis=1)
            ahead = jnp.concatenate([b[:, NFL:], b[:, :NFL]], axis=1)
            c = b - jnp.abs(t) * (b - jnp.where(t >= 0.0, behind, ahead))
            wet_at = tile_x * row_lanes + r % tile_x
            values = flow[r, :, wet_at : wet_at + 1] * (c + source[r])
            field[(s + 1) % 2, r] = values
            if s + 1 < WAVE_SECTIONS:
                set_edges(s + 1, r, values)
            if r in (rows - 2, rows - 1):
                written(r == rows - 2)

    with jax.named_scope("flow_wait"):
        for m in share_moves[:3]:
            m.wait_recv()
        for dg in range(2):
            for yy in range(2):
                arrived(seam_in.at[(g + dg) % 2, yy], got_at(17 + 2 * dg + yy), outer)
    for m in across:
        m.start()
    side_f = [[], []]
    low = iota((8, LANES), 0)
    for yy in range(2):
        felt_here = share_in[0, yy, pl.ds(pl.multiple_of(8 * flip, 8), half), :] + share_in[
            1, yy, pl.ds(pl.multiple_of(8 * flip, 8), half), :
        ]
        inner = pl.ds(pl.multiple_of(half * (1 - flip), 8), 8)
        inner_f = share_in[0, yy, inner, :] + share_in[1, yy, inner, :]
        seam_f = seam_in[0, yy] + seam_in[1, yy]
        for r in range(tile_x):
            row = tile_x * yy + r
            flow[row] = felt_here
            fx, fy = (repeated(felt_here, r * row_lanes + k * NFL) for k in (0, 1))
            speed_x[row] = group_speed * cosine + fx
            speed_y[row] = group_speed * sine + fy
            rest_x[row] = rest_of(speed_x[row])
            rest_y[row] = rest_of(speed_y[row])
            turn[row] = turning * (sine * fx - cosine * fy)
        side_f[0].append(jnp.where(flip == 0, seam_f, inner_f))
        side_f[1].append(jnp.where(flip == 0, inner_f, seam_f))
    for side, speed in ((0, speed_l), (1, speed_r)):
        packed_f = jnp.zeros((8, LANES), jnp.float32)
        for yy in range(2):
            for r in range(tile_x):
                at_row = 2 * (tile_x * yy + r)
                piece = side_f[side][yy]
                shift = (at_row - (6 if side == 0 else 0)) % 8
                piece = pltpu.roll(piece, shift, 0) if shift else piece
                piece = pltpu.roll(piece, LANES - r * row_lanes, 1) if r else piece
                packed_f = jnp.where((low >= at_row) & (low < at_row + 2), piece, packed_f)
        speed[...] = group_speed * cosine + repeated(packed_f, 0)
    column_n = iota((tile_y, LANES), 0)

    def neighbours(k, array):
        result = []
        for r in range(tile_x):
            a = array[r]
            below = array[r - 1] if r > 0 else row_halo[k, 0]
            above = array[r + 1] if r < tile_x - 1 else row_halo[k, 1]
            lower = jnp.where(column_n == 0, col_halo[k, 0, r : r + 1, :], pltpu.roll(a, 1, 0))
            upper = jnp.where(column_n == tile_y - 1, col_halo[k, 1, r : r + 1, :], pltpu.roll(a, tile_y - 1, 0))
            result.append(above + below + upper + lower - 4.0 * a)
        return jnp.concatenate(result, axis=0)

    def swapped(a):
        lane_n = iota(a.shape, 1)
        from_v = pltpu.roll(a, LANES - NLEV, 1)
        from_u = pltpu.roll(a, NLEV, 1)
        return jnp.where(lane_n < NLEV, from_v, jnp.where(lane_n < 2 * NLEV, -from_u, 0.0))

    def mixed(first):
        return first + split_dot(first, mix[...], 0)

    pick_rows = -(-own // 8) * 8

    def with_wet(a):
        return jnp.where(iota(a.shape, 1) == 2 * NLEV, wet_wide, a)

    sea_first = sea_moves(0, ocean)
    sea_second = sea_moves(1, ocean_next)

    def ocean_gather():
        to_grp.wait_send()
        to_grp.wait_recv()
        everything = pack[...] + packs[...]
        ocean[...] = with_wet(everything[:columns]).reshape(ocean.shape)
        levels = everything[columns:]
        mixer = jnp.concatenate(
            [levels, pltpu.roll(levels, NLEV, 1), jnp.zeros((LANES - 2 * NLEV, LANES), jnp.float32)], axis=0
        )
        mix[...] = jnp.concatenate(halves(mixer), axis=1)
        i, j = iota((LANES, 2 * pick_rows), 0), iota((LANES, 2 * pick_rows), 1)
        level = j % pick_rows
        pick = jnp.where((level < own) & (i == level + own * g + NLEV * (j // pick_rows)), 1.0, 0.0)
        last_mix = pick + exact_dot(mixer, pick)
        high, low = halves(last_mix)
        finals[0] = jnp.concatenate([pick.astype(jnp.bfloat16)] * 2 + [jnp.zeros_like(high)], axis=0)
        finals[1] = jnp.concatenate([high, high, low], axis=0)
        set_col_edges(0, ocean)
        for m in sea_first:
            m.start()

    def ocean_prepare():
        for m in sea_first:
            m.wait_recv()
        flat = ocean[...].reshape(columns, LANES)
        plain = flat + ocean_step * (coriolis * swapped(flat) + viscosity * neighbours(0, ocean))
        ocean_next[...] = with_wet(plain).reshape(ocean.shape)
        set_col_edges(1, ocean_next)
        for m in sea_second:
            m.start()
        for m in sea_first:
            m.wait_send()

    def wave_profile():
        depth = dot_on(dw[...], spread, 0, 0)
        rest = jnp.zeros((LANES - 2 * NLEV, bins), jnp.float32)
        high, low = halves(jnp.concatenate([depth * cosine, depth * sine, rest], axis=0))
        profile[...] = jnp.concatenate([high, low], axis=0)

    all_moves = [None] + [wave_moves(s) for s in range(1, WAVE_SECTIONS)]

    def next_written(s):
        def written(interior):
            moves = all_moves[s]
            if interior:

                @pl.when(late)
                def _():
                    for m in moves[2:4]:
                        m.start()

            else:
                for m in moves[4:]:
                    m.start()
                for m in moves[:2]:
                    m.start()

                @pl.when(jnp.logical_not(late))
                def _():
                    for m in moves[2:4]:
                        m.start()

        return written

    their = tile_x * (1 - y)
    back = [
        Move(
            field.at[WAVE_SECTIONS % 2, their + row],
            spec_out.at[row, mine, :],
            sent_at(21 + k),
            got_at(21 + k),
            at(0, pair),
            True,
            True,
        )
        for k, row in enumerate((y, 1 - y))
    ]

    def last_written(interior):
        if interior:
            back[0].start()

    with jax.named_scope("pair"):
        for m, onward in zip(to_pair, passed_on):
            m.wait_recv()
            onward.start()
    with jax.named_scope("load_rest"):
        for load in loads[8:]:
            load.wait()
    with jax.named_scope("inter"):
        interaction(0)
    with jax.named_scope("wait_send"):
        for m in to_pair + share_moves + straight + edges_first:
            m.wait_send()
    finish(
        0,
        edges_arrived,
        layers_arrived,
        lambda side: jnp.concatenate([halo_first[side, 0], halo_first[side, 1]], axis=0),
        next_written(1),
    )

    def section(s, meanwhile):
        moves = all_moves[s]
        with jax.named_scope("inter"):
            interaction(s)


        with jax.named_scope("wait_send"):
            for m in all_moves[s - 1] if s > 1 else passed_on + across:
                m.wait_send()
        for work in meanwhile:
            work()

        def edges_in():
            for m in moves[4:]:
                m.wait_recv()

        def layers_in(first):
            for m in moves[0:2] if first else moves[2:4]:
                m.wait_recv()

        written = next_written(s + 1) if s + 1 < WAVE_SECTIONS else last_written
        finish(s, edges_in, layers_in, lambda side: halo_y[s, side], written)

    for s in range(1, WAVE_SECTIONS):
        section(s, {1: (ocean_gather, wave_profile), 2: (ocean_prepare,)}.get(s, ()))

    last = field.at[WAVE_SECTIONS % 2]
    drift = split_dot(last[...].reshape(rows * half, bins), profile[...], 1)
    drift_q[...] = drift.reshape(drift_q.shape)
    lane_s = iota((half, LANES), 1)

    def turned(a, shift):
        shift %= LANES
        return pltpu.roll(a, shift, 1) if shift else a

    by_row = [drift[r * half : (r + 1) * half] for r in range(rows)]
    low_s = iota((8, LANES), 0)
    for yy in range(2):
        for part in range(2):
            packed = jnp.zeros((half, LANES), jnp.float32)
            for k in range(tile_x + 1):
                piece = turned(by_row[(tile_x - 1) * yy + k], NLEV * (k - part))
                packed = jnp.where((lane_s >= NLEV * k) & (lane_s < NLEV * (k + 1)), piece, packed)
            drift_p[yy, part] = packed
        packed = jnp.zeros((8, LANES), jnp.float32)
        for r in range(tile_x):
            values = by_row[tile_x * yy + r]
            piece = jnp.where(flip == 0, values[:8], pltpu.roll(values[half - 8 :], 1, 0))
            packed = jnp.where(low_s == r, pltpu.roll(piece, r, 0) if r else piece, packed)
        drift_s[yy] = packed
    drift_moves = [
        Move(
            drift_p.at[yy],
            drift_n.at[g, :, mine, :],
            sent_at(5 + k),
            got_at(got),
            device,
            True,
            True,
        )
        for k, (got, yy, device) in enumerate(((35, 1 - y, at(1, pair)), (23, 1 - y, at(0, pair)), (36, y, at(1))))
    ]
    to_side = 1 - 2 * flip
    for dg in (1, 0):
        for side, (row, device, cond) in enumerate(
            ((0, near(dg, -1, 1, 0), above), (rows - 1, near(dg, 1, 0, 0), below))
        ):
            drift_moves.append(
                Move(
                    drift_q.at[row],
                    drift_z.at[g, mine, :],
                    sent_at((8, 9, 10, 23)[2 * dg + side]),
                    got_at((24, 37)[dg] + y),
                    device,
                    cond,
                    False,
                )
            )
        for yy in range(2):
            drift_moves.append(
                Move(
                    drift_s.at[yy],
                    drift_c.at[g, 1 - flip],
                    sent_at((24, 0, 25, 26)[2 * dg + yy]),
                    got_at((1, 39)[dg] + 1 - flip),
                    near(dg, 0, yy, -to_side),
                    outer,
                    False,
                )
            )
    for m in drift_moves:
        m.start()
    back[1].start()
    spec_out[:, mine, :] = last[my_rows]
    drift_n[g, :, mine, :] = drift_p[y]
    with jax.named_scope("sea_second"):
        for m in sea_second:
            m.wait_recv()
    plain = jnp.concatenate(
        [row_halo[1, 0]] + [ocean_next[r] for r in range(tile_x)] + [row_halo[1, 1], col_halo[1, 0], col_halo[1, 1]], axis=0
    )
    plain_mixed = mixed(plain)
    with jax.named_scope("drift_wait"):
        for m in drift_moves[:3]:
            m.wait_recv()
        for dg in range(2):
            for yy in range(2):
                strip_cols = pl.ds(pl.multiple_of(half * ((yy + gy) % 2), 8), half)
                arrived(drift_z.at[(g + dg) % 2, strip_cols, :], got_at((24, 37)[dg] + yy), reaches)
            for side, cond in enumerate((left_tile, right_tile)):
                arrived(drift_c.at[(g + dg) % 2, side], got_at((1, 39)[dg] + side), cond)
    lane_r = iota((tile_y, LANES), 1)
    both_u, both_v = drift_n[0, 0] + drift_n[1, 0], drift_n[0, 1] + drift_n[1, 1]
    near_rows = [
        jnp.where(
            lane_r < NLEV,
            turned(both_u, -NLEV * k),
            jnp.where(lane_r < 2 * NLEV, turned(both_v, NLEV * (1 - k)), 0.0),
        )
        for k in range(tile_x + 1)
    ]
    beyond = drift_z[0] + drift_z[1]
    drift_rows = jnp.concatenate(
        [jnp.where(y == 0, a, b) for a, b in zip([beyond] + near_rows, near_rows + [beyond])], axis=0
    )
    drifts = [drift_rows, drift_c[0, 0] + drift_c[1, 0], drift_c[0, 1] + drift_c[1, 1]]
    pulled = ocean_step * coriolis * swapped(jnp.concatenate(drifts, axis=0))
    after_one = plain[:, 2 * NLEV : 2 * NLEV + 1] * (plain_mixed + mixed(pulled))
    sea = (tile_x + 2) * tile_y
    row_halo[0, 0] = after_one[:tile_y]
    flat = after_one[tile_y : sea - tile_y]
    ocean[...] = flat.reshape(ocean.shape)
    row_halo[0, 1] = after_one[sea - tile_y : sea]
    col_halo[0, 0] = after_one[sea : sea + 8]
    col_halo[0, 1] = after_one[sea + 8 :]
    drift_all = drift_rows[tile_y : sea - tile_y]

    def give(out_u, out_v, which, values, wet):
        for r in range(tile_x):
            high, low = halves(values[r * tile_y : (r + 1) * tile_y])
            result = dot_on(finals[which], jnp.concatenate([high, low, high], axis=1), 0, 1, None)
            if wet:
                result = result * wet_mask[r : r + 1, :].astype(jnp.float32)
            out_u[:, r, :] = result[:own]
            out_v[:, r, :] = result[pick_rows : pick_rows + own]

    second = flat + ocean_step * (coriolis * swapped(flat + drift_all) + viscosity * neighbours(0, ocean))
    give(u_out, v_out, 1, second, True)
    give(du_out, dv_out, 0, drift_all, False)
    with jax.named_scope("back"):
        for m in back:
            m.wait_recv()
    for m in back + all_moves[-1] + drift_moves + sea_second:
        m.wait_send()


def store_kernel(*refs):
    count = (len(refs) - 1) // 2
    copies = [pltpu.make_async_copy(refs[i], refs[count + i], refs[-1].at[i]) for i in range(count)]
    for copy in copies:
        copy.start()
    for copy in copies:
        copy.wait()


def solution(mesh):
    sizes = (mesh.shape["gx"], mesh.shape["gy"])
    theta = 2.0 * np.pi * np.arange(ND) / ND
    table = np.zeros((8, ND * NFL), np.float32)
    table[0] = np.repeat(np.cos(theta), NFL)
    table[1] = np.repeat(np.sin(theta), NFL)

    def body(spectrum, wet_mask, ocean_source, ocean_u, ocean_v, current_weights, drift_weights, inter_left, inter_right, inter_out, mixing):
        tile_x, tile_y, bins = spectrum.shape
        half, rows = tile_y // 2, 2 * tile_x
        own = ocean_u.shape[2]
        columns = tile_x * tile_y
        f32 = jnp.float32
        vmem = pl.BlockSpec(memory_space=pltpu.VMEM)
        sea = (tile_x, tile_y, LANES)
        sections = WAVE_SECTIONS
        wave = (rows, half, bins)

        def V(*shape):
            return pltpu.VMEM(shape, f32)

        def D(*shape):
            return pltpu.SemaphoreType.DMA(shape)

        outs = (jax.ShapeDtypeStruct(spectrum.shape, f32),) + (
            jax.ShapeDtypeStruct((own, tile_x, tile_y), f32),
        ) * 4
        anywhere = pl.BlockSpec(memory_space=pl.ANY)
        results = pl.pallas_call(
            functools.partial(kernel, sizes),
            out_shape=tuple(pltpu.VMEM(a.shape, a.dtype) for a in outs),
            in_specs=[anywhere] * 12,
            out_specs=(vmem,) * 5,
            scratch_shapes=[
                V(tile_x, tile_y, bins),
                pltpu.VMEM(wet_mask.shape, wet_mask.dtype),
                pltpu.VMEM(ocean_source.shape, ocean_source.dtype),
                V(own, tile_x, tile_y),
                V(own, tile_x, tile_y),
                V(*table.shape),
                V(*current_weights.shape[::-1]),
                V(*drift_weights.shape[::-1]),
                pltpu.VMEM(inter_left.shape, inter_left.dtype),
                pltpu.VMEM(inter_right.shape, inter_right.dtype),
                pltpu.VMEM(inter_out.shape[::-1], inter_out.dtype),
                V(*mixing.shape[::-1]),
                D(12),
                V(columns + NLEV, LANES),
                V(LANES, LANES),
                pltpu.VMEM((2 * LANES, bins), jnp.bfloat16),
                V(tile_x, tile_y, bins),
                V(columns + NLEV, LANES),
                V(2, tile_y, LANES),
                V(2, 2, half + 8, LANES),
                V(2, 2, 8, LANES),
                V(rows, half, LANES),
                V(4, 2 * tile_x, bins),
                V(2, 2, 2 * tile_x, bins),
                V(2, *wave),
                V(sections, 2, 8, bins),
                V(sections, 2, 2, half, bins),
                V(sections, 2, 8, bins),
                V(sections, 2, 2, 4, bins),
                V(sections, 2, 2, 4, bins),
                V(*wave),
                V(*wave),
                V(*wave),
                V(*wave),
                V(*wave),
                V(8, bins),
                V(8, bins),
                V(rows, half + 16, bins),
                V(*wave),
                pltpu.VMEM((LANES, 2 * LANES), jnp.bfloat16),
                pltpu.VMEM((2, 3 * LANES, -(-own // 8) * 16), jnp.bfloat16),
                V(*sea),
                V(*sea),
                V(2, 2, tile_y, LANES),
                V(2, 2, 8, LANES),
                V(2, 2, 8, LANES),
                V(rows, half, LANES),
                V(2, 2, half, LANES),
                V(2, 8, LANES),
                V(2, 2, tile_y, LANES),
                V(2, tile_y, LANES),
                V(2, 2, 8, LANES),
                D(SENDS - 8),
                D(RECEIVES),
            ],
            compiler_params=pltpu.CompilerParams(collective_id=0, has_side_effects=True),
        )(
            spectrum,
            wet_mask,
            ocean_source,
            jnp.transpose(ocean_u, (2, 0, 1)),
            jnp.transpose(ocean_v, (2, 0, 1)),
            jnp.asarray(table),
            current_weights.T,
            drift_weights.T,
            inter_left,
            inter_right,
            inter_out.T,
            mixing.T,
        )
        results = pl.pallas_call(
            store_kernel,
            out_shape=outs,
            in_specs=[anywhere] * 5,
            out_specs=(anywhere,) * 5,
            scratch_shapes=[D(5)],
        )(*(pltpu.with_memory_space_constraint(a, pltpu.VMEM) for a in results))
        return (results[0],) + tuple(jnp.transpose(a, (1, 2, 0)) for a in results[1:])

    tile = P("gx", "gy", "grp")
    in_specs = (
        tile,
        P("gx", "gy"),
        P("gx", "gy"),
        tile,
        tile,
        P(),
        P(),
        P("grp", None),
        P("grp", None),
        P(None, "grp"),
        P(None, "grp"),
    )
    return jax.shard_map(body, mesh=mesh, in_specs=in_specs, out_specs=(tile,) * 5, check_vma=False)
```

```python
import functools

import jax
import jax.numpy as jnp
import numpy as np
from jax import lax
from jax.experimental import pallas as pl
from jax.experimental.pallas import tpu as pltpu
from jax.sharding import PartitionSpec as P

NF = 32
ND = 36
NLEV = 40
WAVE_SECTIONS = 3
NFL = 16
LANES = 128
SENDS, RECEIVES = 25, 41
MESH = pl.DeviceIdType.MESH

highest = lax.Precision.HIGHEST
inter_step = 0.1
ocean_step = 0.4
coriolis = 0.5
viscosity = 0.1


def exact_dot(a, b):
    return jnp.dot(a, b, precision=highest, preferred_element_type=jnp.float32)


def dot_on(a, b, dim_a, dim_b, precision=highest):
    return lax.dot_general(
        a, b, (((dim_a,), (dim_b,)), ((), ())), precision=precision, preferred_element_type=jnp.float32
    )


def halves(a):
    high = a.astype(jnp.bfloat16)
    return high, (a - high.astype(jnp.float32)).astype(jnp.bfloat16)


def split_dot(a, both, dim):
    high, low = halves(a)
    result = dot_on(high, both, 1, dim, None) + dot_on(low, both, 1, dim, None)
    half = result.shape[1] // 2
    return result[:, :half] + result[:, half:]


def sweep(centre, back_one, back_two, next_one, next_two, velocity, rest):
    up = velocity >= 0.0
    one = jnp.where(up, back_one, next_one)
    two = jnp.where(up, back_two, next_two)
    step = centre - one
    return centre - jnp.abs(velocity) * (step + rest * (step - (one - two)))


def rest_of(velocity):
    return 0.5 - 0.5 * jnp.abs(velocity)


def iota(shape, dim):
    return lax.broadcasted_iota(jnp.int32, shape, dim)


class Move:
    def __init__(self, src, dst, send, recv, device, sends, receives):
        self.copy = pltpu.make_async_remote_copy(
            src_ref=src, dst_ref=dst, send_sem=send, recv_sem=recv, device_id=device, device_id_type=MESH
        )
        self.sends, self.receives = sends, receives

    def when(self, cond, act):
        if cond is True:
            act()
        elif cond is not False:
            pl.when(cond)(act)

    def start(self):
        self.when(self.sends, self.copy.start)

    def wait_send(self):
        self.when(self.sends, self.copy.wait_send)

    def wait_recv(self):
        self.when(self.receives, self.copy.wait_recv)


def kernel(
    sizes,
    spectrum_hbm,
    wet_mask_hbm,
    ocean_source_hbm,
    ocean_u_hbm,
    ocean_v_hbm,
    angles_hbm,
    cw_hbm,
    dw_hbm,
    left_hbm,
    right_hbm,
    out_hbm,
    mixing_hbm,
    spec_out,
    u_out,
    v_out,
    du_out,
    dv_out,
    spectrum,
    wet_mask,
    ocean_source,
    ocean_u,
    ocean_v,
    angles,
    cw,
    dw,
    left,
    right,
    out_map,
    mixing,
    load_sem,
    pack,
    currents,
    profile,
    masked,
    packs,
    shares,
    share_in,
    seam_in,
    flow,
    edge_first,
    halo_first,
    field,
    edge,
    halo_x,
    halo_y,
    corner,
    halo_c,
    speed_x,
    speed_y,
    rest_x,
    rest_y,
    turn,
    speed_l,
    speed_r,
    wide,
    source,
    mix,
    finals,
    ocean,
    ocean_next,
    row_halo,
    col_edge,
    col_halo,
    drift_q,
    drift_p,
    drift_s,
    drift_n,
    drift_z,
    drift_c,
    send_sem,
    recv_sem,
):
    nx, ny = sizes

    def sent_at(k):
        if k < 8:
            return load_sem.at[k]
        return send_sem.at[k - 8] if k < SENDS else load_sem.at[8 + k - SENDS]

    def got_at(k):
        return recv_sem.at[k]

    loads = [
        pltpu.make_async_copy(src, dst, load_sem.at[k])
        for k, (src, dst) in enumerate(
            (
                (spectrum_hbm, spectrum),
                (wet_mask_hbm, wet_mask),
                (ocean_source_hbm, ocean_source),
                (ocean_u_hbm, ocean_u),
                (ocean_v_hbm, ocean_v),
                (cw_hbm, cw),
                (mixing_hbm, mixing),
                (angles_hbm, angles),
                (dw_hbm, dw),
                (left_hbm, left),
                (right_hbm, right),
                (out_hbm, out_map),
            )
        )
    ]
    for load in loads[:2]:
        load.start()
    tile_x, tile_y, bins = spectrum.shape
    half = tile_y // 2
    own = u_out.shape[0]
    rows = 2 * tile_x
    g, gx, gy = lax.axis_index("grp"), lax.axis_index("gx"), lax.axis_index("gy")
    z, y = gx // 2, gx % 2
    flip = (y + gy + 1) % 2
    q = 2 * gy + flip
    late = gy % 2 == 1
    nz, nq = nx // 2, 2 * ny

    def at(dg=0, x=gx, c=gy):
        return {"grp": (g + dg) % 2, "gx": x, "gy": c}

    pair = 2 * z + 1 - y

    def q_at(dz, dq):
        qq = q + dq
        return at(0, 2 * (z + dz) + (qq + qq // 2 + 1) % 2, qq // 2)

    def inside(value, step, limit):
        return value + step >= 0 if step < 0 else value + step < limit

    def both(dz, dq):
        cond = inside(q, dq, nq)
        return cond if dz == 0 else cond & inside(z, dz, nz)

    def near(dg, dz, yy, dc):
        return {"grp": (g + dg) % 2, "gx": 2 * (z + dz) + yy, "gy": gy + dc}

    barrier = pltpu.get_barrier_semaphore()
    total = 0
    for dz in (-1, 0, 1):
        for dc in (-1, 0, 1):
            friends = [at(1), at(0, pair), at(1, pair)]
            if dz or dc:
                groups = (0,) if dz and dc else (0, 1)
                friends = [near(dg, dz, yy, dc) for dg in groups for yy in (0, 1)]
            cond = inside(z, dz, nz) & inside(gy, dc, ny)

            @pl.when(cond)
            def _():
                for device in friends:
                    pl.semaphore_signal(barrier, inc=1, device_id=device, device_id_type=MESH)

            total = total + jnp.where(cond, len(friends), 0)

    for load in loads[2:]:
        load.start()
    columns = tile_x * tile_y

    def as_columns(table):
        ones = jnp.ones((1, LANES), jnp.float32)
        values = table[...].astype(jnp.float32)
        exact = None if columns <= 256 else highest
        return jnp.concatenate([dot_on(values[r : r + 1], ones, 0, 0, exact) for r in range(tile_x)], axis=0)

    loads[1].wait()
    wet_wide = as_columns(wet_mask)
    wet_n = wet_wide[:, 0:1]

    away = pl.ds(pl.multiple_of(half * (1 - flip), 8), half)
    mine = pl.ds(pl.multiple_of(half * flip, 8), half)
    my_rows = pl.ds(tile_x * y, tile_x)

    reaches = jnp.where(y == 0, z > 0, z < nz - 1)

    @pl.when(jnp.logical_not(reaches))
    def _():
        drift_z[...] = jnp.zeros_like(drift_z)

    @pl.when(z == 0)
    def _():
        halo_x[:, 0] = jnp.zeros_like(halo_x[:, 0])

    @pl.when(z == nz - 1)
    def _():
        halo_x[:, 1] = jnp.zeros_like(halo_x[:, 1])

    for side, dq in ((0, -1), (1, 1)):

        @pl.when(jnp.logical_not(inside(q, dq, nq)))
        def _():
            halo_y[:, side] = jnp.zeros_like(halo_y[:, side])
            halo_c[:, side] = jnp.zeros_like(halo_c[:, side])
            halo_first[side] = jnp.zeros_like(halo_first[side])
            seam_in[...] = jnp.zeros_like(seam_in)

        for slot, dz in ((0, -1), (1, 1)):

            @pl.when(inside(q, dq, nq) & jnp.logical_not(inside(z, dz, nz)))
            def _():
                halo_c[:, side, slot] = jnp.zeros_like(halo_c[:, side, slot])

    for side, d in ((0, -1), (1, 1)):

        @pl.when(jnp.logical_not(inside(gx, d, nx)))
        def _():
            row_halo[:, side] = jnp.zeros_like(row_halo[:, side])

        @pl.when(jnp.logical_not(inside(gy, d, ny)))
        def _():
            col_halo[:, side] = jnp.zeros_like(col_halo[:, side])
            drift_c[:, side] = jnp.zeros_like(drift_c[:, side])

    loads[0].wait()
    masked[...] = (spectrum[...].reshape(columns, bins) * wet_n).reshape(tile_x, tile_y, bins)

    for k, first in enumerate((0, half - 2, half, tile_y - 2)):
        for r in range(tile_x):
            edge_first[k, 2 * r : 2 * r + 2, :] = masked[r, first : first + 2, :]

    for load in loads[2:8]:
        load.wait()
    place_i, place_j = iota((own, LANES), 0), iota((own, LANES), 1)
    place_u = jnp.where(place_j == place_i + own * g, 1.0, 0.0)
    place_v = jnp.where(place_j == place_i + own * g + NLEV, 1.0, 0.0)

    def placed(pieces):
        values = jnp.concatenate([part.astype(jnp.float32) for a, _ in pieces for part in halves(a)], axis=0)
        places = jnp.concatenate([p for _, p in pieces for _ in range(2)], axis=0)
        return dot_on(values.astype(jnp.bfloat16), places.astype(jnp.bfloat16), 0, 0, None)

    for r in range(tile_x):
        pack[r * tile_y : (r + 1) * tile_y] = placed([(ocean_u[:, r, :], place_u), (ocean_v[:, r, :], place_v)])
    pack[columns:] = placed([(mixing[...], place_u)])
    chosen_at = as_columns(ocean_source)[:, 0:1]
    chosen = jnp.where(iota((columns, columns), 1).astype(jnp.float32) == chosen_at, 1.0, 0.0)
    currents[...] = jnp.zeros_like(currents)
    for b in range(NF // NFL):
        at_u = 2 * NFL * b
        currents[at_u : at_u + NFL, 0:NLEV] = cw[b * NFL : (b + 1) * NFL]
        currents[at_u + NFL : at_u + 2 * NFL] = pltpu.roll(currents[at_u : at_u + NFL], NLEV, 1)
    own_share = split_dot(pack[:columns], jnp.concatenate(halves(currents[...]), axis=0), 1)
    felt_parts = dot_on(chosen.astype(jnp.bfloat16), jnp.concatenate(halves(own_share), axis=1), 1, 0, None)
    felt = felt_parts[:, :LANES] + felt_parts[:, LANES:]
    lane_t = iota((tile_y, LANES), 1)
    row_lanes = 2 * NFL
    for b in range(NF // NFL):
        share = jnp.zeros((tile_y, LANES), jnp.float32)
        for r in range(tile_x):
            own_row = felt[r * tile_y : (r + 1) * tile_y]
            shift = (r - b) * row_lanes % LANES
            own_row = pltpu.roll(own_row, shift, 1) if shift else own_row
            share = jnp.where((lane_t >= r * row_lanes) & (lane_t < (r + 1) * row_lanes), own_row, share)
            wet_lane = lane_t == jnp.where(g == b, tile_x * row_lanes + r, LANES)
            share = jnp.where(wet_lane, wet_wide[r * tile_y : (r + 1) * tile_y], share)
        shares[b] = share
    field[0, my_rows] = masked[:, mine, :]
    with jax.named_scope("barrier"):
        pl.semaphore_wait(barrier, total)

    to_pair = [
        Move(
            masked.at[row, away, :],
            field.at[0, tile_x * y + row],
            sent_at(k),
            got_at(k),
            at(0, pair),
            True,
            True,
        )
        for k, row in ((1, y), (2, 1 - y))
    ]
    dz_first = 2 * y - 1
    reaches_back = jnp.where(y == 0, z < nz - 1, z > 0)

    def layer(k, source_ref, row, owner, device, cond):
        return Move(
            source_ref,
            halo_x.at[0, 1 - owner, row],
            sent_at(k),
            got_at(6 + 2 * (1 - owner) + row),
            device,
            cond,
            False,
        )

    straight = [
        layer(k, masked.at[row, mine, :], row, y, near(0, dz_first, y, 0), reaches) for k, row in ((10, y), (11, 1 - y))
    ]
    across = [
        layer(k, masked.at[row, away, :], row, y, near(0, dz_first, 1 - y, 0), reaches & jnp.logical_not(late))
        for k, row in ((12, y), (13, 1 - y))
    ]
    passed_on = [
        layer(k, field.at[0, tile_x * (1 - y) + row], row, 1 - y, near(0, -dz_first, y, 0), reaches_back & late)
        for k, row in ((12, 1 - y), (13, y))
    ]
    def strip_at(dz, strip):
        return near(0, dz, (strip + strip // 2 + 1) % 2, strip // 2 - gy)

    left_tile, right_tile = gy > 0, gy < ny - 1
    edges_first = [
        Move(
            edge_first.at[1 + flip],
            halo_first.at[flip, y],
            sent_at(14),
            got_at(12),
            at(0, pair),
            True,
            True,
        )
    ]
    after = 1 - y
    for k, (cond, strip, side) in enumerate(
        ((left_tile, 2 * gy - 1, 1), (True, 2 * gy + 1, 0), (True, 2 * gy, 1), (right_tile, 2 * gy + 2, 0))
    ):
        if cond is not True:
            edges_first.append(
                Move(
                    edge_first.at[k],
                    halo_first.at[side, y],
                    sent_at(15 + side),
                    got_at(10 + y),
                    strip_at(0, strip),
                    cond,
                    False,
                )
            )
        edges_first.append(
            Move(
                edge_first.at[k],
                halo_c.at[0, side, after],
                sent_at(17 + k),
                got_at((13 if cond is True else 15) + after),
                strip_at(dz_first, strip),
                reaches if cond is True else reaches & cond,
                False,
            )
        )
    halo_first[1 - flip, y] = edge_first[2 - flip]

    def wave_moves(s):
        moves = []
        sends_from, got_from = ((1, 21), (11, 6))[(s - 1) % 2]
        for near in (True, False):
            for side, dz in ((0, -1), (1, 1)):
                layer = 0 if near == (dz < 0) else 1
                moves.append(
                    Move(
                        field.at[s % 2, layer if dz < 0 else rows - 2 + layer],
                        halo_x.at[s, 1 - side, layer],
                        sent_at(sends_from + len(moves)),
                        got_at(got_from + len(moves)),
                        at(0, gx + 2 * dz),
                        inside(z, dz, nz),
                        inside(z, -dz, nz),
                    )
                )
        k = 4
        for side, dq in ((0, -1), (1, 1)):
            for dz in (-1, 0, 1):
                moves.append(
                    Move(
                        edge.at[s, side] if dz == 0 else corner.at[s, side, (1 + dz) // 2],
                        halo_y.at[s, 1 - side] if dz == 0 else halo_c.at[s, 1 - side, (1 - dz) // 2],
                        sent_at(sends_from + k),
                        got_at(got_from + k),
                        q_at(dz, dq),
                        both(dz, dq),
                        both(-dz, -dq),
                    )
                )
                k += 1
        return moves

    wider = half + 8

    def wide_strip(f):
        return pl.ds(pl.multiple_of((tile_y - wider) * f, 8), wider)

    share_moves = [
        Move(
            shares.at[(g + dg) % 2, wide_strip(f), :],
            share_in.at[g, y],
            sent_at(3 + k),
            got_at(3 + k),
            device,
            True,
            True,
        )
        for k, (dg, f, device) in enumerate(
            ((1, 1 - flip, at(1, pair)), (1, flip, at(1)), (0, 1 - flip, at(0, pair)))
        )
    ]
    for dg in (1, 0):
        for side, (cond, strip, block) in enumerate(
            ((left_tile, 2 * gy - 1, pl.ds(0, 8)), (right_tile, 2 * gy + 2, pl.ds(tile_y - 8, 8)))
        ):
            share_moves.append(
                Move(
                    shares.at[(g + dg) % 2, block, :],
                    seam_in.at[g, y],
                    sent_at(6 + 2 * dg + side),
                    got_at(17 + 2 * dg + y),
                    {**strip_at(0, strip), "grp": (g + dg) % 2},
                    cond,
                    False,
                )
            )
    for m in share_moves + to_pair + straight + edges_first:
        m.start()
    share_in[g, y] = shares[g, wide_strip(flip), :]
    to_grp = Move(pack, packs, sent_at(0), got_at(0), at(1), True, True)
    to_grp.start()

    def arrived(ref, sem, cond=True):
        Move(ref, ref, sem, sem, at(0, pair), False, cond).wait_recv()

    outer = jnp.where(flip == 0, left_tile, right_tile)
    above, below = z > 0, z < nz - 1

    def edges_arrived():
        edges_first[0].wait_recv()
        for yy in range(2):
            arrived(halo_first.at[flip, yy], got_at(10 + yy), outer)
        for i, cond in enumerate((above, below)):
            arrived(halo_c.at[0, 1 - flip, i], got_at(13 + i), cond)
            arrived(halo_c.at[0, flip, i], got_at(15 + i), cond & outer)

    def layers_arrived(first):
        for side, cond, layer in ((0, above, 1 if first else 0), (1, below, 0 if first else 1)):
            arrived(halo_x.at[0, side, layer], got_at(6 + 2 * side + layer), cond)

    def sea_moves(k, array):
        moves = []
        sends_from, got_from = ((21, 31), (1, 16))[k]
        for side, d in ((0, -1), (1, 1)):
            moves.append(
                Move(
                    array.at[0 if d < 0 else tile_x - 1],
                    row_halo.at[k, 1 - side],
                    sent_at(sends_from + side),
                    got_at(got_from + side),
                    at(0, gx + d),
                    inside(gx, d, nx),
                    inside(gx, -d, nx),
                )
            )
            moves.append(
                Move(
                    col_edge.at[k, side],
                    col_halo.at[k, 1 - side],
                    sent_at(sends_from + 2 + side),
                    got_at(got_from + 2 + side),
                    at(0, gx, gy + d),
                    inside(gy, d, ny),
                    inside(gy, -d, ny),
                )
            )
        return moves

    def set_col_edges(k, array):
        for side, column in ((0, 0), (1, tile_y - 1)):
            for r in range(tile_x):
                col_edge[k, side, r : r + 1, :] = array[r, column : column + 1, :]

    lane = iota((1, bins), 1)
    frequency = (g * NFL + (lane & (NFL - 1))).astype(jnp.float32)
    group_speed = 0.2 + 0.4 * (NF - 1 - frequency) / (NF - 1)
    turning = 0.5 * (frequency + 1.0) / NF
    cosine, sine = angles[0:1, :], angles[1:2, :]
    spread_f = g * NFL + (iota((NF, bins), 1) & (NFL - 1))
    spread = jnp.where(iota((NF, bins), 0) == spread_f, 1.0, 0.0)

    def repeated(values, start):
        place = iota(values.shape, 1)
        values = pltpu.roll(values, LANES - start, 1) if start else values
        width = NFL
        while width < LANES:
            values = jnp.where(place < width, values, pltpu.roll(values, width, 1))
            width *= 2
        return jnp.concatenate([values] * (-(-bins // LANES)), axis=1)[:, :bins]

    def set_edges(s, r, values):
        for side, first in ((0, 0), (1, half - 2)):
            pair_of = values[first : first + 2]
            edge[s, side, 2 * r : 2 * r + 2, :] = pair_of
            corner[s, side, r // 2, 2 * (r % 2) : 2 * (r % 2) + 2, :] = pair_of

    def interaction(s):
        now = field[s % 2].reshape(rows * half, bins).astype(jnp.bfloat16)
        product = jnp.dot(now, left[...], preferred_element_type=jnp.float32) * jnp.dot(
            now, right[...], preferred_element_type=jnp.float32
        )
        result = dot_on(product.astype(jnp.bfloat16), out_map[...], 1, 1, None)
        source[...] = (inter_step * result).reshape(source.shape)

    def finish(s, edges_in, layers_in, edge_of, written):
        with jax.named_scope("wait_edges"):
            edges_in()
        for side, speed, start in ((0, speed_l, 6), (1, speed_r, half + 8)):
            here = edge_of(side)
            before, after = (jnp.concatenate([halo_c[s, side, i]] * 2, axis=0) for i in range(2))
            low = iota((8, bins), 0)

            def joined(a, b, n):
                return jnp.where(low < n, pltpu.roll(a, n, 0), pltpu.roll(b, n, 0))

            packed = sweep(
                here,
                joined(before, here, 2),
                joined(before, here, 4),
                joined(here, after, 6),
                joined(here, after, 4),
                speed[...],
                rest_of(speed[...]),
            )
            for r in range(rows):
                wide[r, start : start + 2, :] = packed[2 * r : 2 * r + 2]

        def line(r):
            if r < 0:
                return halo_x[s, 0, r + 2]
            if r >= rows:
                return halo_x[s, 1, r - rows]
            return field[s % 2, r]

        for r in [*range(1, rows - 1), 0, rows - 1]:
            if r < 2:
                with jax.named_scope("wait_layers"):
                    layers_in(r == 1)
            wide[r, 8 : 8 + half, :] = sweep(
                line(r), line(r - 1), line(r - 2), line(r + 1), line(r + 2), speed_x[r], rest_x[r]
            )
            b = sweep(
                wide[r, 8 : 8 + half, :],
                wide[r, 7 : 7 + half, :],
                wide[r, 6 : 6 + half, :],
                wide[r, 9 : 9 + half, :],
                wide[r, 10 : 10 + half, :],
                speed_y[r],
                rest_y[r],
            )
            t = turn[r]
            behind = jnp.concatenate([b[:, bins - NFL :], b[:, : bins - NFL]], axis=1)
            ahead = jnp.concatenate([b[:, NFL:], b[:, :NFL]], axis=1)
            c = b - jnp.abs(t) * (b - jnp.where(t >= 0.0, behind, ahead))
            wet_at = tile_x * row_lanes + r % tile_x
            values = flow[r, :, wet_at : wet_at + 1] * (c + source[r])
            field[(s + 1) % 2, r] = values
            if s + 1 < WAVE_SECTIONS:
                set_edges(s + 1, r, values)
            if r in (rows - 2, rows - 1):
                written(r == rows - 2)

    with jax.named_scope("flow_wait"):
        for m in share_moves[:3]:
            m.wait_recv()
        for dg in range(2):
            for yy in range(2):
                arrived(seam_in.at[(g + dg) % 2, yy], got_at(17 + 2 * dg + yy), outer)
    for m in across:
        m.start()
    side_f = [[], []]
    low = iota((8, LANES), 0)
    for yy in range(2):
        felt_here = share_in[0, yy, pl.ds(pl.multiple_of(8 * flip, 8), half), :] + share_in[
            1, yy, pl.ds(pl.multiple_of(8 * flip, 8), half), :
        ]
        inner = pl.ds(pl.multiple_of(half * (1 - flip), 8), 8)
        inner_f = share_in[0, yy, inner, :] + share_in[1, yy, inner, :]
        seam_f = seam_in[0, yy] + seam_in[1, yy]
        for r in range(tile_x):
            row = tile_x * yy + r
            flow[row] = felt_here
            fx, fy = (repeated(felt_here, r * row_lanes + k * NFL) for k in (0, 1))
            speed_x[row] = group_speed * cosine + fx
            speed_y[row] = group_speed * sine + fy
            rest_x[row] = rest_of(speed_x[row])
            rest_y[row] = rest_of(speed_y[row])
            turn[row] = turning * (sine * fx - cosine * fy)
        side_f[0].append(jnp.where(flip == 0, seam_f, inner_f))
        side_f[1].append(jnp.where(flip == 0, inner_f, seam_f))
    for side, speed in ((0, speed_l), (1, speed_r)):
        packed_f = jnp.zeros((8, LANES), jnp.float32)
        for yy in range(2):
            for r in range(tile_x):
                at_row = 2 * (tile_x * yy + r)
                piece = side_f[side][yy]
                shift = (at_row - (6 if side == 0 else 0)) % 8
                piece = pltpu.roll(piece, shift, 0) if shift else piece
                piece = pltpu.roll(piece, LANES - r * row_lanes, 1) if r else piece
                packed_f = jnp.where((low >= at_row) & (low < at_row + 2), piece, packed_f)
        speed[...] = group_speed * cosine + repeated(packed_f, 0)
    column_n = iota((tile_y, LANES), 0)

    def neighbours(k, array):
        result = []
        for r in range(tile_x):
            a = array[r]
            below = array[r - 1] if r > 0 else row_halo[k, 0]
            above = array[r + 1] if r < tile_x - 1 else row_halo[k, 1]
            lower = jnp.where(column_n == 0, col_halo[k, 0, r : r + 1, :], pltpu.roll(a, 1, 0))
            upper = jnp.where(column_n == tile_y - 1, col_halo[k, 1, r : r + 1, :], pltpu.roll(a, tile_y - 1, 0))
            result.append(above + below + upper + lower - 4.0 * a)
        return jnp.concatenate(result, axis=0)

    def swapped(a):
        lane_n = iota(a.shape, 1)
        from_v = pltpu.roll(a, LANES - NLEV, 1)
        from_u = pltpu.roll(a, NLEV, 1)
        return jnp.where(lane_n < NLEV, from_v, jnp.where(lane_n < 2 * NLEV, -from_u, 0.0))

    def mixed(first):
        return first + split_dot(first, mix[...], 0)

    pick_rows = -(-own // 8) * 8

    def with_wet(a):
        return jnp.where(iota(a.shape, 1) == 2 * NLEV, wet_wide, a)

    sea_first = sea_moves(0, ocean)
    sea_second = sea_moves(1, ocean_next)

    def ocean_gather():
        to_grp.wait_send()
        to_grp.wait_recv()
        everything = pack[...] + packs[...]
        ocean[...] = with_wet(everything[:columns]).reshape(ocean.shape)
        levels = everything[columns:]
        mixer = jnp.concatenate(
            [levels, pltpu.roll(levels, NLEV, 1), jnp.zeros((LANES - 2 * NLEV, LANES), jnp.float32)], axis=0
        )
        mix[...] = jnp.concatenate(halves(mixer), axis=1)
        i, j = iota((LANES, 2 * pick_rows), 0), iota((LANES, 2 * pick_rows), 1)
        level = j % pick_rows
        pick = jnp.where((level < own) & (i == level + own * g + NLEV * (j // pick_rows)), 1.0, 0.0)
        last_mix = pick + exact_dot(mixer, pick)
        high, low = halves(last_mix)
        finals[0] = jnp.concatenate([pick.astype(jnp.bfloat16)] * 2 + [jnp.zeros_like(high)], axis=0)
        finals[1] = jnp.concatenate([high, high, low], axis=0)
        set_col_edges(0, ocean)
        for m in sea_first:
            m.start()

    def ocean_prepare():
        for m in sea_first:
            m.wait_recv()
        flat = ocean[...].reshape(columns, LANES)
        plain = flat + ocean_step * (coriolis * swapped(flat) + viscosity * neighbours(0, ocean))
        ocean_next[...] = with_wet(plain).reshape(ocean.shape)
        set_col_edges(1, ocean_next)
        for m in sea_second:
            m.start()
        for m in sea_first:
            m.wait_send()

    def wave_profile():
        depth = dot_on(dw[...], spread, 0, 0)
        rest = jnp.zeros((LANES - 2 * NLEV, bins), jnp.float32)
        high, low = halves(jnp.concatenate([depth * cosine, depth * sine, rest], axis=0))
        profile[...] = jnp.concatenate([high, low], axis=0)

    all_moves = [None] + [wave_moves(s) for s in range(1, WAVE_SECTIONS)]

    def next_written(s):
        def written(interior):
            moves = all_moves[s]
            if interior:

                @pl.when(late)
                def _():
                    for m in moves[2:4]:
                        m.start()

            else:
                for m in moves[4:]:
                    m.start()
                for m in moves[:2]:
                    m.start()

                @pl.when(jnp.logical_not(late))
                def _():
                    for m in moves[2:4]:
                        m.start()

        return written

    their = tile_x * (1 - y)
    back = [
        Move(
            field.at[WAVE_SECTIONS % 2, their + row],
            spec_out.at[row, mine, :],
            sent_at(21 + k),
            got_at(21 + k),
            at(0, pair),
            True,
            True,
        )
        for k, row in enumerate((y, 1 - y))
    ]

    def last_written(interior):
        if interior:
            back[0].start()

    with jax.named_scope("pair"):
        for m, onward in zip(to_pair, passed_on):
            m.wait_recv()
            onward.start()
    with jax.named_scope("load_rest"):
        for load in loads[8:]:
            load.wait()
    with jax.named_scope("inter"):
        interaction(0)
    with jax.named_scope("wait_send"):
        for m in to_pair + share_moves + straight + edges_first:
            m.wait_send()
    finish(
        0,
        edges_arrived,
        layers_arrived,
        lambda side: jnp.concatenate([halo_first[side, 0], halo_first[side, 1]], axis=0),
        next_written(1),
    )

    def section(s, meanwhile):
        moves = all_moves[s]
        with jax.named_scope("inter"):
            interaction(s)


        with jax.named_scope("wait_send"):
            for m in all_moves[s - 1] if s > 1 else passed_on + across:
                m.wait_send()
        for work in meanwhile:
            work()

        def edges_in():
            for m in moves[4:]:
                m.wait_recv()

        def layers_in(first):
            for m in moves[0:2] if first else moves[2:4]:
                m.wait_recv()

        written = next_written(s + 1) if s + 1 < WAVE_SECTIONS else last_written
        finish(s, edges_in, layers_in, lambda side: halo_y[s, side], written)

    for s in range(1, WAVE_SECTIONS):
        section(s, {1: (ocean_gather, wave_profile), 2: (ocean_prepare,)}.get(s, ()))

    last = field.at[WAVE_SECTIONS % 2]
    drift = split_dot(last[...].reshape(rows * half, bins), profile[...], 1)
    drift_q[...] = drift.reshape(drift_q.shape)
    lane_s = iota((half, LANES), 1)

    def turned(a, shift):
        shift %= LANES
        return pltpu.roll(a, shift, 1) if shift else a

    by_row = [drift[r * half : (r + 1) * half] for r in range(rows)]
    low_s = iota((8, LANES), 0)
    for yy in range(2):
        for part in range(2):
            packed = jnp.zeros((half, LANES), jnp.float32)
            for k in range(tile_x + 1):
                piece = turned(by_row[(tile_x - 1) * yy + k], NLEV * (k - part))
                packed = jnp.where((lane_s >= NLEV * k) & (lane_s < NLEV * (k + 1)), piece, packed)
            drift_p[yy, part] = packed
        packed = jnp.zeros((8, LANES), jnp.float32)
        for r in range(tile_x):
            values = by_row[tile_x * yy + r]
            piece = jnp.where(flip == 0, values[:8], pltpu.roll(values[half - 8 :], 1, 0))
            packed = jnp.where(low_s == r, pltpu.roll(piece, r, 0) if r else piece, packed)
        drift_s[yy] = packed
    drift_moves = [
        Move(
            drift_p.at[yy],
            drift_n.at[g, :, mine, :],
            sent_at(5 + k),
            got_at(got),
            device,
            True,
            True,
        )
        for k, (got, yy, device) in enumerate(((35, 1 - y, at(1, pair)), (23, 1 - y, at(0, pair)), (36, y, at(1))))
    ]
    to_side = 1 - 2 * flip
    for dg in (1, 0):
        for side, (row, device, cond) in enumerate(
            ((0, near(dg, -1, 1, 0), above), (rows - 1, near(dg, 1, 0, 0), below))
        ):
            drift_moves.append(
                Move(
                    drift_q.at[row],
                    drift_z.at[g, mine, :],
                    sent_at((8, 9, 10, 23)[2 * dg + side]),
                    got_at((24, 37)[dg] + y),
                    device,
                    cond,
                    False,
                )
            )
        for yy in range(2):
            drift_moves.append(
                Move(
                    drift_s.at[yy],
                    drift_c.at[g, 1 - flip],
                    sent_at((24, 0, 25, 26)[2 * dg + yy]),
                    got_at((1, 39)[dg] + 1 - flip),
                    near(dg, 0, yy, -to_side),
                    outer,
                    False,
                )
            )
    for m in drift_moves:
        m.start()
    back[1].start()
    spec_out[:, mine, :] = last[my_rows]
    drift_n[g, :, mine, :] = drift_p[y]
    with jax.named_scope("sea_second"):
        for m in sea_second:
            m.wait_recv()
    plain = jnp.concatenate(
        [row_halo[1, 0]] + [ocean_next[r] for r in range(tile_x)] + [row_halo[1, 1], col_halo[1, 0], col_halo[1, 1]], axis=0
    )
    plain_mixed = mixed(plain)
    with jax.named_scope("drift_wait"):
        for m in drift_moves[:3]:
            m.wait_recv()
        for dg in range(2):
            for yy in range(2):
                strip_cols = pl.ds(pl.multiple_of(half * ((yy + gy + 1) % 2), 8), half)
                arrived(drift_z.at[(g + dg) % 2, strip_cols, :], got_at((24, 37)[dg] + yy), reaches)
            for side, cond in enumerate((left_tile, right_tile)):
                arrived(drift_c.at[(g + dg) % 2, side], got_at((1, 39)[dg] + side), cond)
    lane_r = iota((tile_y, LANES), 1)
    both_u, both_v = drift_n[0, 0] + drift_n[1, 0], drift_n[0, 1] + drift_n[1, 1]
    near_rows = [
        jnp.where(
            lane_r < NLEV,
            turned(both_u, -NLEV * k),
            jnp.where(lane_r < 2 * NLEV, turned(both_v, NLEV * (1 - k)), 0.0),
        )
        for k in range(tile_x + 1)
    ]
    beyond = drift_z[0] + drift_z[1]
    drift_rows = jnp.concatenate(
        [jnp.where(y == 0, a, b) for a, b in zip([beyond] + near_rows, near_rows + [beyond])], axis=0
    )
    drifts = [drift_rows, drift_c[0, 0] + drift_c[1, 0], drift_c[0, 1] + drift_c[1, 1]]
    pulled = ocean_step * coriolis * swapped(jnp.concatenate(drifts, axis=0))
    after_one = plain[:, 2 * NLEV : 2 * NLEV + 1] * (plain_mixed + mixed(pulled))
    sea = (tile_x + 2) * tile_y
    row_halo[0, 0] = after_one[:tile_y]
    flat = after_one[tile_y : sea - tile_y]
    ocean[...] = flat.reshape(ocean.shape)
    row_halo[0, 1] = after_one[sea - tile_y : sea]
    col_halo[0, 0] = after_one[sea : sea + 8]
    col_halo[0, 1] = after_one[sea + 8 :]
    drift_all = drift_rows[tile_y : sea - tile_y]

    def give(out_u, out_v, which, values, wet):
        for r in range(tile_x):
            high, low = halves(values[r * tile_y : (r + 1) * tile_y])
            result = dot_on(finals[which], jnp.concatenate([high, low, high], axis=1), 0, 1, None)
            if wet:
                result = result * wet_mask[r : r + 1, :].astype(jnp.float32)
            out_u[:, r, :] = result[:own]
            out_v[:, r, :] = result[pick_rows : pick_rows + own]

    second = flat + ocean_step * (coriolis * swapped(flat + drift_all) + viscosity * neighbours(0, ocean))
    give(u_out, v_out, 1, second, True)
    give(du_out, dv_out, 0, drift_all, False)
    with jax.named_scope("back"):
        for m in back:
            m.wait_recv()
    for m in back + all_moves[-1] + drift_moves + sea_second:
        m.wait_send()


def store_kernel(*refs):
    count = (len(refs) - 1) // 2
    copies = [pltpu.make_async_copy(refs[i], refs[count + i], refs[-1].at[i]) for i in range(count)]
    for copy in copies:
        copy.start()
    for copy in copies:
        copy.wait()


def solution(mesh):
    sizes = (mesh.shape["gx"], mesh.shape["gy"])
    theta = 2.0 * np.pi * np.arange(ND) / ND
    table = np.zeros((8, ND * NFL), np.float32)
    table[0] = np.repeat(np.cos(theta), NFL)
    table[1] = np.repeat(np.sin(theta), NFL)

    def body(spectrum, wet_mask, ocean_source, ocean_u, ocean_v, current_weights, drift_weights, inter_left, inter_right, inter_out, mixing):
        tile_x, tile_y, bins = spectrum.shape
        half, rows = tile_y // 2, 2 * tile_x
        own = ocean_u.shape[2]
        columns = tile_x * tile_y
        f32 = jnp.float32
        vmem = pl.BlockSpec(memory_space=pltpu.VMEM)
        sea = (tile_x, tile_y, LANES)
        sections = WAVE_SECTIONS
        wave = (rows, half, bins)

        def V(*shape):
            return pltpu.VMEM(shape, f32)

        def D(*shape):
            return pltpu.SemaphoreType.DMA(shape)

        outs = (jax.ShapeDtypeStruct(spectrum.shape, f32),) + (
            jax.ShapeDtypeStruct((own, tile_x, tile_y), f32),
        ) * 4
        anywhere = pl.BlockSpec(memory_space=pl.ANY)
        results = pl.pallas_call(
            functools.partial(kernel, sizes),
            out_shape=tuple(pltpu.VMEM(a.shape, a.dtype) for a in outs),
            in_specs=[anywhere] * 12,
            out_specs=(vmem,) * 5,
            scratch_shapes=[
                V(tile_x, tile_y, bins),
                pltpu.VMEM(wet_mask.shape, wet_mask.dtype),
                pltpu.VMEM(ocean_source.shape, ocean_source.dtype),
                V(own, tile_x, tile_y),
                V(own, tile_x, tile_y),
                V(*table.shape),
                V(*current_weights.shape[::-1]),
                V(*drift_weights.shape[::-1]),
                pltpu.VMEM(inter_left.shape, inter_left.dtype),
                pltpu.VMEM(inter_right.shape, inter_right.dtype),
                pltpu.VMEM(inter_out.shape[::-1], inter_out.dtype),
                V(*mixing.shape[::-1]),
                D(12),
                V(columns + NLEV, LANES),
                V(LANES, LANES),
                pltpu.VMEM((2 * LANES, bins), jnp.bfloat16),
                V(tile_x, tile_y, bins),
                V(columns + NLEV, LANES),
                V(2, tile_y, LANES),
                V(2, 2, half + 8, LANES),
                V(2, 2, 8, LANES),
                V(rows, half, LANES),
                V(4, 2 * tile_x, bins),
                V(2, 2, 2 * tile_x, bins),
                V(2, *wave),
                V(sections, 2, 8, bins),
                V(sections, 2, 2, half, bins),
                V(sections, 2, 8, bins),
                V(sections, 2, 2, 4, bins),
                V(sections, 2, 2, 4, bins),
                V(*wave),
                V(*wave),
                V(*wave),
                V(*wave),
                V(*wave),
                V(8, bins),
                V(8, bins),
                V(rows, half + 16, bins),
                V(*wave),
                pltpu.VMEM((LANES, 2 * LANES), jnp.bfloat16),
                pltpu.VMEM((2, 3 * LANES, -(-own // 8) * 16), jnp.bfloat16),
                V(*sea),
                V(*sea),
                V(2, 2, tile_y, LANES),
                V(2, 2, 8, LANES),
                V(2, 2, 8, LANES),
                V(rows, half, LANES),
                V(2, 2, half, LANES),
                V(2, 8, LANES),
                V(2, 2, tile_y, LANES),
                V(2, tile_y, LANES),
                V(2, 2, 8, LANES),
                D(SENDS - 8),
                D(RECEIVES),
            ],
            compiler_params=pltpu.CompilerParams(collective_id=0, has_side_effects=True),
        )(
            spectrum,
            wet_mask,
            ocean_source,
            jnp.transpose(ocean_u, (2, 0, 1)),
            jnp.transpose(ocean_v, (2, 0, 1)),
            jnp.asarray(table),
            current_weights.T,
            drift_weights.T,
            inter_left,
            inter_right,
            inter_out.T,
            mixing.T,
        )
        results = pl.pallas_call(
            store_kernel,
            out_shape=outs,
            in_specs=[anywhere] * 5,
            out_specs=(anywhere,) * 5,
            scratch_shapes=[D(5)],
        )(*(pltpu.with_memory_space_constraint(a, pltpu.VMEM) for a in results))
        return (results[0],) + tuple(jnp.transpose(a, (1, 2, 0)) for a in results[1:])

    tile = P("gx", "gy", "grp")
    in_specs = (
        tile,
        P("gx", "gy"),
        P("gx", "gy"),
        tile,
        tile,
        P(),
        P(),
        P("grp", None),
        P("grp", None),
        P(None, "grp"),
        P(None, "grp"),
    )
    return jax.shard_map(body, mesh=mesh, in_specs=in_specs, out_specs=(tile,) * 5, check_vma=False)
```

```python
import functools

import jax
import jax.numpy as jnp
import numpy as np
from jax import lax
from jax.experimental import pallas as pl
from jax.experimental.pallas import tpu as pltpu
from jax.sharding import PartitionSpec as P

NF = 32
ND = 36
NLEV = 40
WAVE_SECTIONS = 3
NFL = 16
LANES = 128
SENDS, RECEIVES = 25, 41
MESH = pl.DeviceIdType.MESH

highest = lax.Precision.HIGHEST
inter_step = 0.1
ocean_step = 0.4
coriolis = 0.5
viscosity = 0.1


def exact_dot(a, b):
    return jnp.dot(a, b, precision=highest, preferred_element_type=jnp.float32)


def dot_on(a, b, dim_a, dim_b, precision=highest):
    return lax.dot_general(
        a, b, (((dim_a,), (dim_b,)), ((), ())), precision=precision, preferred_element_type=jnp.float32
    )


def halves(a):
    high = a.astype(jnp.bfloat16)
    return high, (a - high.astype(jnp.float32)).astype(jnp.bfloat16)


def split_dot(a, both, dim):
    high, low = halves(a)
    result = dot_on(high, both, 1, dim, None) + dot_on(low, both, 1, dim, None)
    half = result.shape[1] // 2
    return result[:, :half] + result[:, half:]


def sweep(centre, back_one, back_two, next_one, next_two, velocity, rest):
    up = velocity >= 0.0
    one = jnp.where(up, back_one, next_one)
    two = jnp.where(up, back_two, next_two)
    step = centre - one
    return centre - jnp.abs(velocity) * (step + rest * (step - (one - two)))


def rest_of(velocity):
    return 0.5 - 0.5 * jnp.abs(velocity)


def iota(shape, dim):
    return lax.broadcasted_iota(jnp.int32, shape, dim)


class Move:
    def __init__(self, src, dst, send, recv, device, sends, receives):
        self.copy = pltpu.make_async_remote_copy(
            src_ref=src, dst_ref=dst, send_sem=send, recv_sem=recv, device_id=device, device_id_type=MESH
        )
        self.sends, self.receives = sends, receives

    def when(self, cond, act):
        if cond is True:
            act()
        elif cond is not False:
            pl.when(cond)(act)

    def start(self):
        self.when(self.sends, self.copy.start)

    def wait_send(self):
        self.when(self.sends, self.copy.wait_send)

    def wait_recv(self):
        self.when(self.receives, self.copy.wait_recv)


def kernel(
    sizes,
    spectrum_hbm,
    wet_mask_hbm,
    ocean_source_hbm,
    ocean_u_hbm,
    ocean_v_hbm,
    angles_hbm,
    cw_hbm,
    dw_hbm,
    left_hbm,
    right_hbm,
    out_hbm,
    mixing_hbm,
    spec_out,
    u_out,
    v_out,
    du_out,
    dv_out,
    spectrum,
    wet_mask,
    ocean_source,
    ocean_u,
    ocean_v,
    angles,
    cw,
    dw,
    left,
    right,
    out_map,
    mixing,
    load_sem,
    pack,
    currents,
    profile,
    masked,
    packs,
    shares,
    share_in,
    seam_in,
    flow,
    edge_first,
    halo_first,
    field,
    edge,
    halo_x,
    halo_y,
    corner,
    halo_c,
    speed_x,
    speed_y,
    rest_x,
    rest_y,
    turn,
    speed_l,
    speed_r,
    wide,
    source,
    mix,
    finals,
    ocean,
    ocean_next,
    row_halo,
    col_edge,
    col_halo,
    drift_q,
    drift_p,
    drift_s,
    drift_n,
    drift_z,
    drift_c,
    send_sem,
    recv_sem,
):
    nx, ny = sizes

    def sent_at(k):
        if k < 8:
            return load_sem.at[k]
        return send_sem.at[k - 8] if k < SENDS else load_sem.at[8 + k - SENDS]

    def got_at(k):
        return recv_sem.at[k]

    loads = [
        pltpu.make_async_copy(src, dst, load_sem.at[k])
        for k, (src, dst) in enumerate(
            (
                (spectrum_hbm, spectrum),
                (wet_mask_hbm, wet_mask),
                (ocean_source_hbm, ocean_source),
                (ocean_u_hbm, ocean_u),
                (ocean_v_hbm, ocean_v),
                (cw_hbm, cw),
                (mixing_hbm, mixing),
                (angles_hbm, angles),
                (dw_hbm, dw),
                (left_hbm, left),
                (right_hbm, right),
                (out_hbm, out_map),
            )
        )
    ]
    for load in loads[:2]:
        load.start()
    tile_x, tile_y, bins = spectrum.shape
    half = tile_y // 2
    own = u_out.shape[0]
    rows = 2 * tile_x
    g, gx, gy = lax.axis_index("grp"), lax.axis_index("gx"), lax.axis_index("gy")
    z, y = gx // 2, gx % 2
    flip = (y + gy + 1) % 2
    q = 2 * gy + flip
    late = gy % 2 == 1
    nz, nq = nx // 2, 2 * ny

    def at(dg=0, x=gx, c=gy):
        return {"grp": (g + dg) % 2, "gx": x, "gy": c}

    pair = 2 * z + 1 - y

    def q_at(dz, dq):
        qq = q + dq
        return at(0, 2 * (z + dz) + (qq + qq // 2 + 1) % 2, qq // 2)

    def inside(value, step, limit):
        return value + step >= 0 if step < 0 else value + step < limit

    def both(dz, dq):
        cond = inside(q, dq, nq)
        return cond if dz == 0 else cond & inside(z, dz, nz)

    def near(dg, dz, yy, dc):
        return {"grp": (g + dg) % 2, "gx": 2 * (z + dz) + yy, "gy": gy + dc}

    barrier = pltpu.get_barrier_semaphore()
    total = 0
    for dz in (-1, 0, 1):
        for dc in (-1, 0, 1):
            friends = [at(1), at(0, pair), at(1, pair)]
            if dz or dc:
                groups = (0,) if dz and dc else (0, 1)
                friends = [near(dg, dz, yy, dc) for dg in groups for yy in (0, 1)]
            cond = inside(z, dz, nz) & inside(gy, dc, ny)

            @pl.when(cond)
            def _():
                for device in friends:
                    pl.semaphore_signal(barrier, inc=1, device_id=device, device_id_type=MESH)

            total = total + jnp.where(cond, len(friends), 0)

    for load in loads[2:]:
        load.start()
    columns = tile_x * tile_y

    def as_columns(table):
        ones = jnp.ones((1, LANES), jnp.float32)
        values = table[...].astype(jnp.float32)
        exact = None if columns <= 256 else highest
        return jnp.concatenate([dot_on(values[r : r + 1], ones, 0, 0, exact) for r in range(tile_x)], axis=0)

    loads[1].wait()
    wet_wide = as_columns(wet_mask)
    wet_n = wet_wide[:, 0:1]

    away = pl.ds(pl.multiple_of(half * (1 - flip), 8), half)
    mine = pl.ds(pl.multiple_of(half * flip, 8), half)
    my_rows = pl.ds(tile_x * y, tile_x)

    reaches = jnp.where(y == 0, z > 0, z < nz - 1)

    @pl.when(jnp.logical_not(reaches))
    def _():
        drift_z[...] = jnp.zeros_like(drift_z)

    @pl.when(z == 0)
    def _():
        halo_x[:, 0] = jnp.zeros_like(halo_x[:, 0])

    @pl.when(z == nz - 1)
    def _():
        halo_x[:, 1] = jnp.zeros_like(halo_x[:, 1])

    for side, dq in ((0, -1), (1, 1)):

        @pl.when(jnp.logical_not(inside(q, dq, nq)))
        def _():
            halo_y[:, side] = jnp.zeros_like(halo_y[:, side])
            halo_c[:, side] = jnp.zeros_like(halo_c[:, side])
            halo_first[side] = jnp.zeros_like(halo_first[side])
            seam_in[...] = jnp.zeros_like(seam_in)

        for slot, dz in ((0, -1), (1, 1)):

            @pl.when(inside(q, dq, nq) & jnp.logical_not(inside(z, dz, nz)))
            def _():
                halo_c[:, side, slot] = jnp.zeros_like(halo_c[:, side, slot])

    for side, d in ((0, -1), (1, 1)):

        @pl.when(jnp.logical_not(inside(gx, d, nx)))
        def _():
            row_halo[:, side] = jnp.zeros_like(row_halo[:, side])

        @pl.when(jnp.logical_not(inside(gy, d, ny)))
        def _():
            col_halo[:, side] = jnp.zeros_like(col_halo[:, side])
            drift_c[:, side] = jnp.zeros_like(drift_c[:, side])

    loads[0].wait()
    masked[...] = (spectrum[...].reshape(columns, bins) * wet_n).reshape(tile_x, tile_y, bins)

    for k, first in enumerate((0, half - 2, half, tile_y - 2)):
        for r in range(tile_x):
            edge_first[k, 2 * r : 2 * r + 2, :] = masked[r, first : first + 2, :]

    for load in loads[2:8]:
        load.wait()
    place_i, place_j = iota((own, LANES), 0), iota((own, LANES), 1)
    place_u = jnp.where(place_j == place_i + own * g, 1.0, 0.0)
    place_v = jnp.where(place_j == place_i + own * g + NLEV, 1.0, 0.0)

    def placed(pieces):
        values = jnp.concatenate([part.astype(jnp.float32) for a, _ in pieces for part in halves(a)], axis=0)
        places = jnp.concatenate([p for _, p in pieces for _ in range(2)], axis=0)
        return dot_on(values.astype(jnp.bfloat16), places.astype(jnp.bfloat16), 0, 0, None)

    for r in range(tile_x):
        pack[r * tile_y : (r + 1) * tile_y] = placed([(ocean_u[:, r, :], place_u), (ocean_v[:, r, :], place_v)])
    pack[columns:] = placed([(mixing[...], place_u)])
    chosen_at = as_columns(ocean_source)[:, 0:1]
    chosen = jnp.where(iota((columns, columns), 1).astype(jnp.float32) == chosen_at, 1.0, 0.0)
    currents[...] = jnp.zeros_like(currents)
    for b in range(NF // NFL):
        at_u = 2 * NFL * b
        currents[at_u : at_u + NFL, 0:NLEV] = cw[b * NFL : (b + 1) * NFL]
        currents[at_u + NFL : at_u + 2 * NFL] = pltpu.roll(currents[at_u : at_u + NFL], NLEV, 1)
    own_share = split_dot(pack[:columns], jnp.concatenate(halves(currents[...]), axis=0), 1)
    felt_parts = dot_on(chosen.astype(jnp.bfloat16), jnp.concatenate(halves(own_share), axis=1), 1, 0, None)
    felt = felt_parts[:, :LANES] + felt_parts[:, LANES:]
    lane_t = iota((tile_y, LANES), 1)
    row_lanes = 2 * NFL
    for b in range(NF // NFL):
        share = jnp.zeros((tile_y, LANES), jnp.float32)
        for r in range(tile_x):
            own_row = felt[r * tile_y : (r + 1) * tile_y]
            shift = (r - b) * row_lanes % LANES
            own_row = pltpu.roll(own_row, shift, 1) if shift else own_row
            share = jnp.where((lane_t >= r * row_lanes) & (lane_t < (r + 1) * row_lanes), own_row, share)
            wet_lane = lane_t == jnp.where(g == b, tile_x * row_lanes + r, LANES)
            share = jnp.where(wet_lane, wet_wide[r * tile_y : (r + 1) * tile_y], share)
        shares[b] = share
    field[0, my_rows] = masked[:, mine, :]
    with jax.named_scope("barrier"):
        pl.semaphore_wait(barrier, total)

    to_pair = [
        Move(
            masked.at[row, away, :],
            field.at[0, tile_x * y + row],
            sent_at(k),
            got_at(k),
            at(0, pair),
            True,
            True,
        )
        for k, row in ((1, y), (2, 1 - y))
    ]
    dz_first = 2 * y - 1
    reaches_back = jnp.where(y == 0, z < nz - 1, z > 0)

    def layer(k, source_ref, row, owner, device, cond):
        return Move(
            source_ref,
            halo_x.at[0, 1 - owner, row],
            sent_at(k),
            got_at(6 + 2 * (1 - owner) + row),
            device,
            cond,
            False,
        )

    straight = [
        layer(k, masked.at[row, mine, :], row, y, near(0, dz_first, y, 0), reaches) for k, row in ((10, y), (11, 1 - y))
    ]
    across = [
        layer(k, masked.at[row, away, :], row, y, near(0, dz_first, 1 - y, 0), reaches & jnp.logical_not(late))
        for k, row in ((12, y), (13, 1 - y))
    ]
    passed_on = [
        layer(k, field.at[0, tile_x * (1 - y) + row], row, 1 - y, near(0, -dz_first, y, 0), reaches_back & late)
        for k, row in ((12, 1 - y), (13, y))
    ]
    def strip_at(dz, strip):
        return near(0, dz, (strip + strip // 2 + 1) % 2, strip // 2 - gy)

    left_tile, right_tile = gy > 0, gy < ny - 1
    edges_first = [
        Move(
            edge_first.at[1 + flip],
            halo_first.at[flip, y],
            sent_at(14),
            got_at(12),
            at(0, pair),
            True,
            True,
        )
    ]
    after = 1 - y
    for k, (cond, strip, side) in enumerate(
        ((left_tile, 2 * gy - 1, 1), (True, 2 * gy + 1, 0), (True, 2 * gy, 1), (right_tile, 2 * gy + 2, 0))
    ):
        if cond is not True:
            edges_first.append(
                Move(
                    edge_first.at[k],
                    halo_first.at[side, y],
                    sent_at(15 + side),
                    got_at(10 + y),
                    strip_at(0, strip),
                    cond,
                    False,
                )
            )
        edges_first.append(
            Move(
                edge_first.at[k],
                halo_c.at[0, side, after],
                sent_at(17 + k),
                got_at((13 if cond is True else 15) + after),
                strip_at(dz_first, strip),
                reaches if cond is True else reaches & cond,
                False,
            )
        )
    halo_first[1 - flip, y] = edge_first[2 - flip]

    def wave_moves(s):
        moves = []
        sends_from, got_from = ((1, 21), (11, 6))[(s - 1) % 2]
        for near in (True, False):
            for side, dz in ((0, -1), (1, 1)):
                layer = 0 if near == (dz < 0) else 1
                moves.append(
                    Move(
                        field.at[s % 2, layer if dz < 0 else rows - 2 + layer],
                        halo_x.at[s, 1 - side, layer],
                        sent_at(sends_from + len(moves)),
                        got_at(got_from + len(moves)),
                        at(0, gx + 2 * dz),
                        inside(z, dz, nz),
                        inside(z, -dz, nz),
                    )
                )
        k = 4
        for side, dq in ((0, -1), (1, 1)):
            for dz in (-1, 0, 1):
                moves.append(
                    Move(
                        edge.at[s, side] if dz == 0 else corner.at[s, side, (1 + dz) // 2],
                        halo_y.at[s, 1 - side] if dz == 0 else halo_c.at[s, 1 - side, (1 - dz) // 2],
                        sent_at(sends_from + k),
                        got_at(got_from + k),
                        q_at(dz, dq),
                        both(dz, dq),
                        both(-dz, -dq),
                    )
                )
                k += 1
        return moves

    wider = half + 8

    def wide_strip(f):
        return pl.ds(pl.multiple_of((tile_y - wider) * f, 8), wider)

    share_moves = [
        Move(
            shares.at[(g + dg) % 2, wide_strip(f), :],
            share_in.at[g, y],
            sent_at(3 + k),
            got_at(3 + k),
            device,
            True,
            True,
        )
        for k, (dg, f, device) in enumerate(
            ((1, 1 - flip, at(1, pair)), (1, flip, at(1)), (0, 1 - flip, at(0, pair)))
        )
    ]
    for dg in (1, 0):
        for side, (cond, strip, block) in enumerate(
            ((left_tile, 2 * gy - 1, pl.ds(0, 8)), (right_tile, 2 * gy + 2, pl.ds(tile_y - 8, 8)))
        ):
            share_moves.append(
                Move(
                    shares.at[(g + dg) % 2, block, :],
                    seam_in.at[g, y],
                    sent_at(6 + 2 * dg + side),
                    got_at(17 + 2 * dg + y),
                    {**strip_at(0, strip), "grp": (g + dg) % 2},
                    cond,
                    False,
                )
            )
    for m in share_moves:
        m.start()

    @pl.when(jnp.logical_not(late))
    def _():
        for m in to_pair + straight + edges_first:
            m.start()

    share_in[g, y] = shares[g, wide_strip(flip), :]
    to_grp = Move(pack, packs, sent_at(0), got_at(0), at(1), True, True)
    to_grp.start()

    def arrived(ref, sem, cond=True):
        Move(ref, ref, sem, sem, at(0, pair), False, cond).wait_recv()

    outer = jnp.where(flip == 0, left_tile, right_tile)
    above, below = z > 0, z < nz - 1

    def edges_arrived():
        edges_first[0].wait_recv()
        for yy in range(2):
            arrived(halo_first.at[flip, yy], got_at(10 + yy), outer)
        for i, cond in enumerate((above, below)):
            arrived(halo_c.at[0, 1 - flip, i], got_at(13 + i), cond)
            arrived(halo_c.at[0, flip, i], got_at(15 + i), cond & outer)

    def layers_arrived(first):
        for side, cond, layer in ((0, above, 1 if first else 0), (1, below, 0 if first else 1)):
            arrived(halo_x.at[0, side, layer], got_at(6 + 2 * side + layer), cond)

    def sea_moves(k, array):
        moves = []
        sends_from, got_from = ((21, 31), (1, 16))[k]
        for side, d in ((0, -1), (1, 1)):
            moves.append(
                Move(
                    array.at[0 if d < 0 else tile_x - 1],
                    row_halo.at[k, 1 - side],
                    sent_at(sends_from + side),
                    got_at(got_from + side),
                    at(0, gx + d),
                    inside(gx, d, nx),
                    inside(gx, -d, nx),
                )
            )
            moves.append(
                Move(
                    col_edge.at[k, side],
                    col_halo.at[k, 1 - side],
                    sent_at(sends_from + 2 + side),
                    got_at(got_from + 2 + side),
                    at(0, gx, gy + d),
                    inside(gy, d, ny),
                    inside(gy, -d, ny),
                )
            )
        return moves

    def set_col_edges(k, array):
        for side, column in ((0, 0), (1, tile_y - 1)):
            for r in range(tile_x):
                col_edge[k, side, r : r + 1, :] = array[r, column : column + 1, :]

    lane = iota((1, bins), 1)
    frequency = (g * NFL + (lane & (NFL - 1))).astype(jnp.float32)
    group_speed = 0.2 + 0.4 * (NF - 1 - frequency) / (NF - 1)
    turning = 0.5 * (frequency + 1.0) / NF
    cosine, sine = angles[0:1, :], angles[1:2, :]
    spread_f = g * NFL + (iota((NF, bins), 1) & (NFL - 1))
    spread = jnp.where(iota((NF, bins), 0) == spread_f, 1.0, 0.0)

    def repeated(values, start):
        place = iota(values.shape, 1)
        values = pltpu.roll(values, LANES - start, 1) if start else values
        width = NFL
        while width < LANES:
            values = jnp.where(place < width, values, pltpu.roll(values, width, 1))
            width *= 2
        return jnp.concatenate([values] * (-(-bins // LANES)), axis=1)[:, :bins]

    def set_edges(s, r, values):
        for side, first in ((0, 0), (1, half - 2)):
            pair_of = values[first : first + 2]
            edge[s, side, 2 * r : 2 * r + 2, :] = pair_of
            corner[s, side, r // 2, 2 * (r % 2) : 2 * (r % 2) + 2, :] = pair_of

    def interaction(s, part=slice(None)):
        now = field[s % 2, part].reshape(-1, bins).astype(jnp.bfloat16)
        product = jnp.dot(now, left[...], preferred_element_type=jnp.float32) * jnp.dot(
            now, right[...], preferred_element_type=jnp.float32
        )
        result = dot_on(product.astype(jnp.bfloat16), out_map[...], 1, 1, None)
        source[part] = (inter_step * result).reshape(-1, half, bins)

    def finish(s, edges_in, layers_in, edge_of, written):
        with jax.named_scope("wait_edges"):
            edges_in()
        for side, speed, start in ((0, speed_l, 6), (1, speed_r, half + 8)):
            here = edge_of(side)
            before, after = (jnp.concatenate([halo_c[s, side, i]] * 2, axis=0) for i in range(2))
            low = iota((8, bins), 0)

            def joined(a, b, n):
                return jnp.where(low < n, pltpu.roll(a, n, 0), pltpu.roll(b, n, 0))

            packed = sweep(
                here,
                joined(before, here, 2),
                joined(before, here, 4),
                joined(here, after, 6),
                joined(here, after, 4),
                speed[...],
                rest_of(speed[...]),
            )
            for r in range(rows):
                wide[r, start : start + 2, :] = packed[2 * r : 2 * r + 2]

        def line(r):
            if r < 0:
                return halo_x[s, 0, r + 2]
            if r >= rows:
                return halo_x[s, 1, r - rows]
            return field[s % 2, r]

        for r in [*range(1, rows - 1), 0, rows - 1]:
            if r < 2:
                with jax.named_scope("wait_layers"):
                    layers_in(r == 1)
            wide[r, 8 : 8 + half, :] = sweep(
                line(r), line(r - 1), line(r - 2), line(r + 1), line(r + 2), speed_x[r], rest_x[r]
            )
            b = sweep(
                wide[r, 8 : 8 + half, :],
                wide[r, 7 : 7 + half, :],
                wide[r, 6 : 6 + half, :],
                wide[r, 9 : 9 + half, :],
                wide[r, 10 : 10 + half, :],
                speed_y[r],
                rest_y[r],
            )
            t = turn[r]
            behind = jnp.concatenate([b[:, bins - NFL :], b[:, : bins - NFL]], axis=1)
            ahead = jnp.concatenate([b[:, NFL:], b[:, :NFL]], axis=1)
            c = b - jnp.abs(t) * (b - jnp.where(t >= 0.0, behind, ahead))
            wet_at = tile_x * row_lanes + r % tile_x
            values = flow[r, :, wet_at : wet_at + 1] * (c + source[r])
            field[(s + 1) % 2, r] = values
            if s + 1 < WAVE_SECTIONS:
                set_edges(s + 1, r, values)
            if r in (rows - 2, rows - 1):
                written(r == rows - 2)

    with jax.named_scope("load_rest"):
        for load in loads[8:]:
            load.wait()
    interaction(0, my_rows)

    @pl.when(late)
    def _():
        for m in to_pair + straight + edges_first:
            m.start()

    with jax.named_scope("flow_wait"):
        for m in share_moves[:3]:
            m.wait_recv()
        for dg in range(2):
            for yy in range(2):
                arrived(seam_in.at[(g + dg) % 2, yy], got_at(17 + 2 * dg + yy), outer)
    for m in across:
        m.start()
    side_f = [[], []]
    low = iota((8, LANES), 0)
    for yy in range(2):
        felt_here = share_in[0, yy, pl.ds(pl.multiple_of(8 * flip, 8), half), :] + share_in[
            1, yy, pl.ds(pl.multiple_of(8 * flip, 8), half), :
        ]
        inner = pl.ds(pl.multiple_of(half * (1 - flip), 8), 8)
        inner_f = share_in[0, yy, inner, :] + share_in[1, yy, inner, :]
        seam_f = seam_in[0, yy] + seam_in[1, yy]
        for r in range(tile_x):
            row = tile_x * yy + r
            flow[row] = felt_here
            fx, fy = (repeated(felt_here, r * row_lanes + k * NFL) for k in (0, 1))
            speed_x[row] = group_speed * cosine + fx
            speed_y[row] = group_speed * sine + fy
            rest_x[row] = rest_of(speed_x[row])
            rest_y[row] = rest_of(speed_y[row])
            turn[row] = turning * (sine * fx - cosine * fy)
        side_f[0].append(jnp.where(flip == 0, seam_f, inner_f))
        side_f[1].append(jnp.where(flip == 0, inner_f, seam_f))
    for side, speed in ((0, speed_l), (1, speed_r)):
        packed_f = jnp.zeros((8, LANES), jnp.float32)
        for yy in range(2):
            for r in range(tile_x):
                at_row = 2 * (tile_x * yy + r)
                piece = side_f[side][yy]
                shift = (at_row - (6 if side == 0 else 0)) % 8
                piece = pltpu.roll(piece, shift, 0) if shift else piece
                piece = pltpu.roll(piece, LANES - r * row_lanes, 1) if r else piece
                packed_f = jnp.where((low >= at_row) & (low < at_row + 2), piece, packed_f)
        speed[...] = group_speed * cosine + repeated(packed_f, 0)
    column_n = iota((tile_y, LANES), 0)

    def neighbours(k, array):
        result = []
        for r in range(tile_x):
            a = array[r]
            below = array[r - 1] if r > 0 else row_halo[k, 0]
            above = array[r + 1] if r < tile_x - 1 else row_halo[k, 1]
            lower = jnp.where(column_n == 0, col_halo[k, 0, r : r + 1, :], pltpu.roll(a, 1, 0))
            upper = jnp.where(column_n == tile_y - 1, col_halo[k, 1, r : r + 1, :], pltpu.roll(a, tile_y - 1, 0))
            result.append(above + below + upper + lower - 4.0 * a)
        return jnp.concatenate(result, axis=0)

    def swapped(a):
        lane_n = iota(a.shape, 1)
        from_v = pltpu.roll(a, LANES - NLEV, 1)
        from_u = pltpu.roll(a, NLEV, 1)
        return jnp.where(lane_n < NLEV, from_v, jnp.where(lane_n < 2 * NLEV, -from_u, 0.0))

    def mixed(first):
        return first + split_dot(first, mix[...], 0)

    pick_rows = -(-own // 8) * 8

    def with_wet(a):
        return jnp.where(iota(a.shape, 1) == 2 * NLEV, wet_wide, a)

    sea_first = sea_moves(0, ocean)
    sea_second = sea_moves(1, ocean_next)

    def ocean_gather():
        to_grp.wait_send()
        to_grp.wait_recv()
        everything = pack[...] + packs[...]
        ocean[...] = with_wet(everything[:columns]).reshape(ocean.shape)
        levels = everything[columns:]
        mixer = jnp.concatenate(
            [levels, pltpu.roll(levels, NLEV, 1), jnp.zeros((LANES - 2 * NLEV, LANES), jnp.float32)], axis=0
        )
        mix[...] = jnp.concatenate(halves(mixer), axis=1)
        i, j = iota((LANES, 2 * pick_rows), 0), iota((LANES, 2 * pick_rows), 1)
        level = j % pick_rows
        pick = jnp.where((level < own) & (i == level + own * g + NLEV * (j // pick_rows)), 1.0, 0.0)
        last_mix = pick + exact_dot(mixer, pick)
        high, low = halves(last_mix)
        finals[0] = jnp.concatenate([pick.astype(jnp.bfloat16)] * 2 + [jnp.zeros_like(high)], axis=0)
        finals[1] = jnp.concatenate([high, high, low], axis=0)
        set_col_edges(0, ocean)
        for m in sea_first:
            m.start()

    def ocean_prepare():
        for m in sea_first:
            m.wait_recv()
        flat = ocean[...].reshape(columns, LANES)
        plain = flat + ocean_step * (coriolis * swapped(flat) + viscosity * neighbours(0, ocean))
        ocean_next[...] = with_wet(plain).reshape(ocean.shape)
        set_col_edges(1, ocean_next)
        for m in sea_second:
            m.start()
        for m in sea_first:
            m.wait_send()

    def wave_profile():
        depth = dot_on(dw[...], spread, 0, 0)
        rest = jnp.zeros((LANES - 2 * NLEV, bins), jnp.float32)
        high, low = halves(jnp.concatenate([depth * cosine, depth * sine, rest], axis=0))
        profile[...] = jnp.concatenate([high, low], axis=0)

    all_moves = [None] + [wave_moves(s) for s in range(1, WAVE_SECTIONS)]

    def next_written(s):
        def written(interior):
            moves = all_moves[s]
            if interior:

                @pl.when(late)
                def _():
                    for m in moves[2:4]:
                        m.start()

            else:
                for m in moves[4:]:
                    m.start()
                for m in moves[:2]:
                    m.start()

                @pl.when(jnp.logical_not(late))
                def _():
                    for m in moves[2:4]:
                        m.start()

        return written

    their = tile_x * (1 - y)
    back = [
        Move(
            field.at[WAVE_SECTIONS % 2, their + row],
            spec_out.at[row, mine, :],
            sent_at(21 + k),
            got_at(21 + k),
            at(0, pair),
            True,
            True,
        )
        for k, row in enumerate((y, 1 - y))
    ]

    def last_written(interior):
        if interior:
            back[0].start()

    with jax.named_scope("pair"):
        for m, onward in zip(to_pair, passed_on):
            m.wait_recv()
            onward.start()
    with jax.named_scope("inter"):
        interaction(0, pl.ds(tile_x * (1 - y), tile_x))
    with jax.named_scope("wait_send"):
        for m in to_pair + share_moves + straight + edges_first:
            m.wait_send()
    finish(
        0,
        edges_arrived,
        layers_arrived,
        lambda side: jnp.concatenate([halo_first[side, 0], halo_first[side, 1]], axis=0),
        next_written(1),
    )

    def section(s, meanwhile):
        moves = all_moves[s]
        with jax.named_scope("inter"):
            interaction(s)


        with jax.named_scope("wait_send"):
            for m in all_moves[s - 1] if s > 1 else passed_on + across:
                m.wait_send()
        for work in meanwhile:
            work()

        def edges_in():
            for m in moves[4:]:
                m.wait_recv()

        def layers_in(first):
            for m in moves[0:2] if first else moves[2:4]:
                m.wait_recv()

        written = next_written(s + 1) if s + 1 < WAVE_SECTIONS else last_written
        finish(s, edges_in, layers_in, lambda side: halo_y[s, side], written)

    for s in range(1, WAVE_SECTIONS):
        section(s, {1: (ocean_gather, wave_profile), 2: (ocean_prepare,)}.get(s, ()))

    last = field.at[WAVE_SECTIONS % 2]
    drift = split_dot(last[...].reshape(rows * half, bins), profile[...], 1)
    drift_q[...] = drift.reshape(drift_q.shape)
    lane_s = iota((half, LANES), 1)

    def turned(a, shift):
        shift %= LANES
        return pltpu.roll(a, shift, 1) if shift else a

    by_row = [drift[r * half : (r + 1) * half] for r in range(rows)]
    low_s = iota((8, LANES), 0)
    for yy in range(2):
        for part in range(2):
            packed = jnp.zeros((half, LANES), jnp.float32)
            for k in range(tile_x + 1):
                piece = turned(by_row[(tile_x - 1) * yy + k], NLEV * (k - part))
                packed = jnp.where((lane_s >= NLEV * k) & (lane_s < NLEV * (k + 1)), piece, packed)
            drift_p[yy, part] = packed
        packed = jnp.zeros((8, LANES), jnp.float32)
        for r in range(tile_x):
            values = by_row[tile_x * yy + r]
            piece = jnp.where(flip == 0, values[:8], pltpu.roll(values[half - 8 :], 1, 0))
            packed = jnp.where(low_s == r, pltpu.roll(piece, r, 0) if r else piece, packed)
        drift_s[yy] = packed
    drift_moves = [
        Move(
            drift_p.at[yy],
            drift_n.at[g, :, mine, :],
            sent_at(5 + k),
            got_at(got),
            device,
            True,
            True,
        )
        for k, (got, yy, device) in enumerate(((35, 1 - y, at(1, pair)), (23, 1 - y, at(0, pair)), (36, y, at(1))))
    ]
    to_side = 1 - 2 * flip
    for dg in (1, 0):
        for side, (row, device, cond) in enumerate(
            ((0, near(dg, -1, 1, 0), above), (rows - 1, near(dg, 1, 0, 0), below))
        ):
            drift_moves.append(
                Move(
                    drift_q.at[row],
                    drift_z.at[g, mine, :],
                    sent_at((8, 9, 10, 23)[2 * dg + side]),
                    got_at((24, 37)[dg] + y),
                    device,
                    cond,
                    False,
                )
            )
        for yy in range(2):
            drift_moves.append(
                Move(
                    drift_s.at[yy],
                    drift_c.at[g, 1 - flip],
                    sent_at((24, 0, 25, 26)[2 * dg + yy]),
                    got_at((1, 39)[dg] + 1 - flip),
                    near(dg, 0, yy, -to_side),
                    outer,
                    False,
                )
            )
    for m in drift_moves:
        m.start()
    back[1].start()
    spec_out[:, mine, :] = last[my_rows]
    drift_n[g, :, mine, :] = drift_p[y]
    with jax.named_scope("sea_second"):
        for m in sea_second:
            m.wait_recv()
    plain = jnp.concatenate(
        [row_halo[1, 0]] + [ocean_next[r] for r in range(tile_x)] + [row_halo[1, 1], col_halo[1, 0], col_halo[1, 1]], axis=0
    )
    plain_mixed = mixed(plain)
    with jax.named_scope("drift_wait"):
        for m in drift_moves[:3]:
            m.wait_recv()
        for dg in range(2):
            for yy in range(2):
                strip_cols = pl.ds(pl.multiple_of(half * ((yy + gy + 1) % 2), 8), half)
                arrived(drift_z.at[(g + dg) % 2, strip_cols, :], got_at((24, 37)[dg] + yy), reaches)
            for side, cond in enumerate((left_tile, right_tile)):
                arrived(drift_c.at[(g + dg) % 2, side], got_at((1, 39)[dg] + side), cond)
    lane_r = iota((tile_y, LANES), 1)
    both_u, both_v = drift_n[0, 0] + drift_n[1, 0], drift_n[0, 1] + drift_n[1, 1]
    near_rows = [
        jnp.where(
            lane_r < NLEV,
            turned(both_u, -NLEV * k),
            jnp.where(lane_r < 2 * NLEV, turned(both_v, NLEV * (1 - k)), 0.0),
        )
        for k in range(tile_x + 1)
    ]
    beyond = drift_z[0] + drift_z[1]
    drift_rows = jnp.concatenate(
        [jnp.where(y == 0, a, b) for a, b in zip([beyond] + near_rows, near_rows + [beyond])], axis=0
    )
    drifts = [drift_rows, drift_c[0, 0] + drift_c[1, 0], drift_c[0, 1] + drift_c[1, 1]]
    pulled = ocean_step * coriolis * swapped(jnp.concatenate(drifts, axis=0))
    after_one = plain[:, 2 * NLEV : 2 * NLEV + 1] * (plain_mixed + mixed(pulled))
    sea = (tile_x + 2) * tile_y
    row_halo[0, 0] = after_one[:tile_y]
    flat = after_one[tile_y : sea - tile_y]
    ocean[...] = flat.reshape(ocean.shape)
    row_halo[0, 1] = after_one[sea - tile_y : sea]
    col_halo[0, 0] = after_one[sea : sea + 8]
    col_halo[0, 1] = after_one[sea + 8 :]
    drift_all = drift_rows[tile_y : sea - tile_y]

    def give(out_u, out_v, which, values, wet):
        for r in range(tile_x):
            high, low = halves(values[r * tile_y : (r + 1) * tile_y])
            result = dot_on(finals[which], jnp.concatenate([high, low, high], axis=1), 0, 1, None)
            if wet:
                result = result * wet_mask[r : r + 1, :].astype(jnp.float32)
            out_u[:, r, :] = result[:own]
            out_v[:, r, :] = result[pick_rows : pick_rows + own]

    second = flat + ocean_step * (coriolis * swapped(flat + drift_all) + viscosity * neighbours(0, ocean))
    give(u_out, v_out, 1, second, True)
    give(du_out, dv_out, 0, drift_all, False)
    with jax.named_scope("back"):
        for m in back:
            m.wait_recv()
    for m in back + all_moves[-1] + drift_moves + sea_second:
        m.wait_send()


def store_kernel(*refs):
    count = (len(refs) - 1) // 2
    copies = [pltpu.make_async_copy(refs[i], refs[count + i], refs[-1].at[i]) for i in range(count)]
    for copy in copies:
        copy.start()
    for copy in copies:
        copy.wait()


def solution(mesh):
    sizes = (mesh.shape["gx"], mesh.shape["gy"])
    theta = 2.0 * np.pi * np.arange(ND) / ND
    table = np.zeros((8, ND * NFL), np.float32)
    table[0] = np.repeat(np.cos(theta), NFL)
    table[1] = np.repeat(np.sin(theta), NFL)

    def body(spectrum, wet_mask, ocean_source, ocean_u, ocean_v, current_weights, drift_weights, inter_left, inter_right, inter_out, mixing):
        tile_x, tile_y, bins = spectrum.shape
        half, rows = tile_y // 2, 2 * tile_x
        own = ocean_u.shape[2]
        columns = tile_x * tile_y
        f32 = jnp.float32
        vmem = pl.BlockSpec(memory_space=pltpu.VMEM)
        sea = (tile_x, tile_y, LANES)
        sections = WAVE_SECTIONS
        wave = (rows, half, bins)

        def V(*shape):
            return pltpu.VMEM(shape, f32)

        def D(*shape):
            return pltpu.SemaphoreType.DMA(shape)

        outs = (jax.ShapeDtypeStruct(spectrum.shape, f32),) + (
            jax.ShapeDtypeStruct((own, tile_x, tile_y), f32),
        ) * 4
        anywhere = pl.BlockSpec(memory_space=pl.ANY)
        results = pl.pallas_call(
            functools.partial(kernel, sizes),
            out_shape=tuple(pltpu.VMEM(a.shape, a.dtype) for a in outs),
            in_specs=[anywhere] * 12,
            out_specs=(vmem,) * 5,
            scratch_shapes=[
                V(tile_x, tile_y, bins),
                pltpu.VMEM(wet_mask.shape, wet_mask.dtype),
                pltpu.VMEM(ocean_source.shape, ocean_source.dtype),
                V(own, tile_x, tile_y),
                V(own, tile_x, tile_y),
                V(*table.shape),
                V(*current_weights.shape[::-1]),
                V(*drift_weights.shape[::-1]),
                pltpu.VMEM(inter_left.shape, inter_left.dtype),
                pltpu.VMEM(inter_right.shape, inter_right.dtype),
                pltpu.VMEM(inter_out.shape[::-1], inter_out.dtype),
                V(*mixing.shape[::-1]),
                D(12),
                V(columns + NLEV, LANES),
                V(LANES, LANES),
                pltpu.VMEM((2 * LANES, bins), jnp.bfloat16),
                V(tile_x, tile_y, bins),
                V(columns + NLEV, LANES),
                V(2, tile_y, LANES),
                V(2, 2, half + 8, LANES),
                V(2, 2, 8, LANES),
                V(rows, half, LANES),
                V(4, 2 * tile_x, bins),
                V(2, 2, 2 * tile_x, bins),
                V(2, *wave),
                V(sections, 2, 8, bins),
                V(sections, 2, 2, half, bins),
                V(sections, 2, 8, bins),
                V(sections, 2, 2, 4, bins),
                V(sections, 2, 2, 4, bins),
                V(*wave),
                V(*wave),
                V(*wave),
                V(*wave),
                V(*wave),
                V(8, bins),
                V(8, bins),
                V(rows, half + 16, bins),
                V(*wave),
                pltpu.VMEM((LANES, 2 * LANES), jnp.bfloat16),
                pltpu.VMEM((2, 3 * LANES, -(-own // 8) * 16), jnp.bfloat16),
                V(*sea),
                V(*sea),
                V(2, 2, tile_y, LANES),
                V(2, 2, 8, LANES),
                V(2, 2, 8, LANES),
                V(rows, half, LANES),
                V(2, 2, half, LANES),
                V(2, 8, LANES),
                V(2, 2, tile_y, LANES),
                V(2, tile_y, LANES),
                V(2, 2, 8, LANES),
                D(SENDS - 8),
                D(RECEIVES),
            ],
            compiler_params=pltpu.CompilerParams(collective_id=0, has_side_effects=True),
        )(
            spectrum,
            wet_mask,
            ocean_source,
            jnp.transpose(ocean_u, (2, 0, 1)),
            jnp.transpose(ocean_v, (2, 0, 1)),
            jnp.asarray(table),
            current_weights.T,
            drift_weights.T,
            inter_left,
            inter_right,
            inter_out.T,
            mixing.T,
        )
        results = pl.pallas_call(
            store_kernel,
            out_shape=outs,
            in_specs=[anywhere] * 5,
            out_specs=(anywhere,) * 5,
            scratch_shapes=[D(5)],
        )(*(pltpu.with_memory_space_constraint(a, pltpu.VMEM) for a in results))
        return (results[0],) + tuple(jnp.transpose(a, (1, 2, 0)) for a in results[1:])

    tile = P("gx", "gy", "grp")
    in_specs = (
        tile,
        P("gx", "gy"),
        P("gx", "gy"),
        tile,
        tile,
        P(),
        P(),
        P("grp", None),
        P("grp", None),
        P(None, "grp"),
        P(None, "grp"),
    )
    return jax.shard_map(body, mesh=mesh, in_specs=in_specs, out_specs=(tile,) * 5, check_vma=False)
```
